32 devices in a mesh: dp: 16 (over z, y, x), tensor: 2 (over core).
Axes of the slice: x: 2, y: 2, z: 4, core: 2. Of those that a mesh axis runs over, the one named last changes fastest.
Arguments:
- tokens: bfloat16 [8192, 1536], P('dp'), may hold values from -6 to 6
- cotangent: bfloat16 [48, 256, 1536], P('dp'), may hold values from -6 to 6
- lengths: int32 [16, 3], replicated, may hold values from 1 to 256, 512 in all within a row
- dealing: int32 [48], replicated, may hold values from 0 to 47, as said below
- attn_gain: float32 [1536], replicated, may hold values from 0.1 to 1.9
- w_query: bfloat16 [1536, 1536], P(None, 'tensor'), may hold values from -0.15625 to 0.15625
- w_key: bfloat16 [1536, 1536], P(None, 'tensor'), may hold values from -0.15625 to 0.15625
- w_value: bfloat16 [1536, 1536], P(None, 'tensor'), may hold values from -0.15625 to 0.15625
- w_house: bfloat16 [1536, 1536], P(None, 'tensor'), may hold values from -0.15625 to 0.15625
- w_beta: bfloat16 [1536, 12], P(None, 'tensor'), may hold values from -0.15625 to 0.15625
- conv_taps: float32 [4, 1536], P(None, 'tensor'), may hold values from -4 to 4
- w_out: bfloat16 [1536, 1536], P('tensor'), may hold values from -0.625 to 0.625
- ffn_gain: float32 [1536], replicated, may hold values from 0.1 to 1.9
- w_gate: bfloat16 [1536, 4096], P(None, 'tensor'), may hold values from -0.15625 to 0.15625
- w_up: bfloat16 [1536, 4096], P(None, 'tensor'), may hold values from -0.15625 to 0.15625
- w_down: bfloat16 [4096, 1536], P('tensor'), may hold values from -0.09375 to 0.09375
Outputs:
- output: bfloat16 [48, 256, 1536], P('dp')
- input_grad: bfloat16 [8192, 1536], P('dp')
- attn_gain_grad: float32 [1536], P('dp')
- query_grad: float32 [1536, 1536], P('dp', 'tensor')
- key_grad: float32 [1536, 1536], P('dp', 'tensor')
- value_grad: float32 [1536, 1536], P('dp', 'tensor')
- house_grad: float32 [1536, 1536], P('dp', 'tensor')
- beta_grad: float32 [1536, 12], P('dp', 'tensor')
- taps_grad: float32 [4, 1536], P(None, 'tensor')
- out_grad: float32 [1536, 1536], P('tensor', 'dp')
- ffn_gain_grad: float32 [1536], P('dp')
- gate_grad: float32 [1536, 4096], P('dp', 'tensor')
- up_grad: float32 [1536, 4096], P('dp', 'tensor')
- down_grad: float32 [4096, 1536], P('tensor', 'dp')
The draws below stay inside these ranges and needn't reach their ends.
Inputs may be any that keep to these rules, and one draw needn't show every extreme that they name: Each row of lengths sums to exactly 512, and its largest entry is exactly 256. dealing is a permutation of the sequences; dealing[d * 3 + k] is the sequence in slot k of index d of dp. Each index d takes one sequence of group d + 1 if that exists, one of group d - 1 if that exists, and the rest of its own group d.
All inputs are finite; a program needn't handle non-finite values.
Results may differ from the reference program's by a relative error of at most 0.012.
The reference program's roundings to bfloat16 on the way count: a program that leaves them out, or rounds other values in their place, can miss the bound.
Values may be sent and summed in bfloat16 or wider, within the bound.
No kernel may reach another device: no remote copies, remote signals or barrier semaphores. Data moves between devices by JAX's collectives and lax.ppermute only.
A program may use at most 320 MiB of HBM per device.

```python
import math
import jax
import jax.numpy as jnp
import numpy as np
from jax import lax

D = 1536
HEADS = 12
FF = 4096
CONV = 4
TOK_DEV = 512
SLOTS = 3
LMAX = 256
GROUPS = 16
SEQS = 48
TOKENS = 8192


def draw_dealing(key, part):
    first_key, second_key = jax.random.split(jax.random.fold_in(key, 7))

    def shuffle(one_key):
        return jax.random.permutation(one_key, SLOTS)
    order_one = jax.vmap(shuffle)(jax.random.split(first_key, GROUPS)).astype(jnp.int32)
    order_two = jax.vmap(shuffle)(jax.random.split(second_key, GROUPS)).astype(jnp.int32)
    groups_idx = jnp.arange(GROUPS, dtype=jnp.int32)
    seq_ids = groups_idx[:, None] * SLOTS + order_one
    partner_one = jnp.bitwise_xor(groups_idx, 1)
    is_odd = groups_idx % 2 == 1
    partner_two = jnp.where(is_odd, groups_idx + 1, groups_idx - 1)
    partner_two = jnp.where((partner_two < 0) | (partner_two >= GROUPS), groups_idx, partner_two)
    swapped = seq_ids.at[:, 0].set(seq_ids[partner_one, 0])
    swapped = swapped.at[:, 1].set(seq_ids[partner_two, 1])
    dealt = jnp.take_along_axis(swapped, order_two, axis=1)
    return dealt.reshape(-1).astype(jnp.int32)


def raised(array, stream_key, source, target, blocks, factor):
    owner, partner = [(jnp.arange(array.shape[position]) // (array.shape[position] // blocks)).reshape([-1 if axis == position else 1 for axis in range(array.ndim)]) for position in (source, target)]
    chosen = jax.random.permutation(stream_key, blocks)[partner]
    strong = (owner == chosen) | (owner == (partner + blocks // 2) % blocks)
    return jnp.where(strong, factor * array, array)


def steps_of(key, dims, shards, least, high):
    def one(position, parts):
        draws = jax.random.uniform(jax.random.fold_in(jax.random.fold_in(key, 6), position), (parts,), jnp.float32, least / len(shards), high / len(shards))
        return jnp.repeat(jnp.exp(draws), dims[position] // parts).reshape((-1,) + (1,) * (len(dims) - position - 1))

    gain = one(*shards[0])
    for cut in shards[1:]:
        gain = gain * one(*cut)
    return gain


def split_up(amount, total, limit, skew):
    portions = [(1 << 20) // math.isqrt(standing ** skew) + 1 for standing in range(2, amount + 1)]
    rest, given = total - limit - (amount - 1), [1] * (amount - 1)
    while rest > 0:
        movable = [i for i in range(amount - 1) if given[i] < limit]
        mass, left = sum([portions[i] for i in movable]), rest
        for i in movable:
            addition = min(limit - given[i], max(1, left * portions[i] // mass), rest)
            given[i] = given[i] + addition
            rest = rest - addition
    return np.array([limit] + given)


def uneven_parts(key, amount, total, most, slope):
    if amount == 2:
        one = jax.random.randint(key, (), max(1, total - most), min(most, total - 1) + 1)
        return jnp.stack([one, total - one])
    sizes = jnp.asarray(split_up(amount, total, most, slope), jnp.int32)
    couples = (amount - 1) // 2
    donor, receiver = sizes[1:1 + 2 * couples:2], sizes[2:2 + 2 * couples:2]
    room = jnp.minimum(donor - 1, most - receiver)
    moved = jax.random.randint(jax.random.fold_in(key, 1), (couples,), 0, 1 << 20) % (room + 1)
    sizes = sizes.at[1:1 + 2 * couples:2].set(donor - moved).at[2:2 + 2 * couples:2].set(receiver + moved)
    return sizes[jax.random.permutation(jax.random.fold_in(key, 2), amount)]


def noise(key, dims, deviation, limit, cuts=(), kind=jnp.bfloat16):
    drawn = deviation * jax.random.normal(key, dims, jnp.float32)
    if cuts:
        drawn = drawn * steps_of(key, dims, cuts, -0.22, 0.18)
    return jnp.clip(drawn, -limit, limit).astype(kind)


def noise_with(own_key, extent, spread, reach, pieces, heavy, kind=jnp.bfloat16):
    values = spread * jax.random.normal(own_key, extent, jnp.float32)
    if pieces:
        values = values * steps_of(own_key, extent, pieces, -0.22, 0.18)
    return jnp.clip(raised(values, jax.random.fold_in(own_key, 3), *heavy), -reach, reach).astype(kind)


def setup_inputs(seed: int = 0) -> dict:
    key_of = jax.random.split(jax.random.key(seed), 17)
    tokens = noise_with(key_of[0], (TOKENS, D), 1.0, 6.0, ((0, 16),), (0, 1, 16, 2.0))
    cotangent = noise_with(key_of[1], (SEQS, LMAX, D), 1.0, 6.0, ((0, 16),), (0, 2, 16, 2.0))
    lengths = jax.vmap(lambda own: uneven_parts(own, SLOTS, TOK_DEV, LMAX, 1))(jax.random.split(key_of[2], GROUPS)).reshape((GROUPS, SLOTS)).astype(jnp.int32)
    dealing = draw_dealing(jax.random.fold_in(key_of[16], 71), 0)
    attn_gain = jnp.clip(1.0 + 0.18 * jax.random.normal(key_of[4], (D,), jnp.float32), 0.1, 1.9)
    w_query = noise(key_of[5], (D, D), D ** -0.5, 0.15625, ((1, 2),))
    w_key = noise(key_of[6], (D, D), D ** -0.5, 0.15625, ((1, 2),))
    w_value = noise(key_of[7], (D, D), D ** -0.5, 0.15625, ((1, 2),))
    w_house = noise(key_of[8], (D, D), D ** -0.5, 0.15625, ((1, 2),))
    w_beta = noise(key_of[9], (D, HEADS), D ** -0.5, 0.15625, ((1, 2),))
    conv_taps = noise(key_of[10], (CONV, D), 1.0, 4.0, ((1, 2),), jnp.float32)
    w_out = noise(key_of[11], (D, D), (D // 16) ** -0.5, 0.625, ((0, 2),))
    ffn_gain = jnp.clip(1.0 + 0.18 * jax.random.normal(key_of[12], (D,), jnp.float32), 0.1, 1.9)
    w_gate = noise(key_of[13], (D, FF), D ** -0.5, 0.15625, ((1, 2),))
    w_up = noise(key_of[14], (D, FF), D ** -0.5, 0.15625, ((1, 2),))
    w_down = noise(key_of[15], (FF, D), FF ** -0.5, 0.09375, ((0, 2),))
    return {"tokens": tokens, "cotangent": cotangent, "lengths": lengths, "dealing": dealing, "attn_gain": attn_gain, "w_query": w_query, "w_key": w_key, "w_value": w_value, "w_house": w_house, "w_beta": w_beta, "conv_taps": conv_taps, "w_out": w_out, "ffn_gain": ffn_gain, "w_gate": w_gate, "w_up": w_up, "w_down": w_down}


EPSILON = 1e-06
HIGHEST = lax.Precision.HIGHEST

@jax.custom_vjp
def low(v):
    return lax.optimization_barrier(v.astype(jnp.bfloat16)).astype(jnp.float32)

@jax.custom_vjp
def low_back(v):
    return v

def low_keep(v):
    return (low(v), None)

def low_pass(kept, grad):
    return (grad,)

def back_keep(v):
    return (v, None)

def back_low(kept, grad):
    return (low(grad),)
low.defvjp(low_keep, low_pass)
low_back.defvjp(back_keep, back_low)

def matmul(first_op, second_op):
    return jnp.dot(first_op, second_op, precision=HIGHEST)

def rms_norm(source, gain_vec):
    return source * lax.rsqrt(lax.optimization_barrier(jnp.mean(source * source, axis=-1, keepdims=True)) + EPSILON) * gain_vec

def path_mixer(query_all, key_all, value_all, house_all, beta_logit, taps, segment):
    length = query_all.shape[0]
    head_count = beta_logit.shape[1]
    same_seq = segment[:, None] == segment[None, :]
    conv_out = taps[0] * house_all
    for shift_by in range(1, taps.shape[0]):
        shifted = jnp.pad(house_all, ((shift_by, 0), (0, 0)))[:length]
        keep_mask = jnp.pad(segment, (shift_by, 0), constant_values=-1)[:length] == segment
        conv_out = conv_out + taps[shift_by] * jnp.where(keep_mask[:, None], shifted, 0.0)

    def heads_first(matrix):
        return matrix.reshape(length, head_count, -1).transpose(1, 0, 2)
    query_heads = heads_first(query_all)
    key_heads = heads_first(key_all)
    value_heads = heads_first(value_all)
    conv_heads = heads_first(conv_out)
    scaling = query_heads.shape[-1] ** (-0.5)
    house_dir = low(conv_heads * lax.rsqrt(lax.optimization_barrier(jnp.sum(conv_heads * conv_heads, axis=-1, keepdims=True)) + EPSILON))
    beta_gate = 2.0 * jax.nn.sigmoid(beta_logit.T)
    row_index = jnp.arange(length)[:, None]
    col_index = jnp.arange(length)[None, :]
    lower_incl = col_index <= row_index
    strict = col_index < row_index
    gram_matrix = jnp.einsum('hsd,hrd->hsr', house_dir, house_dir, precision=HIGHEST)
    coupling = jnp.where(strict & same_seq, gram_matrix * beta_gate[:, None, :], 0.0)
    query_house = jnp.where(lower_incl, jnp.einsum('hid,hsd->his', query_heads, house_dir, precision=HIGHEST), 0.0)
    house_key = jnp.where(strict, jnp.einsum('hrd,hjd->hrj', house_dir, key_heads, precision=HIGHEST), 0.0)
    identity = jnp.eye(length, dtype=jnp.float32)
    solved = lax.linalg.triangular_solve(identity + coupling, house_key, left_side=True, lower=True)
    scores = jnp.einsum('hid,hjd->hij', query_heads, key_heads, precision=HIGHEST)
    scores = scores - jnp.einsum('his,hsj->hij', query_house * beta_gate[:, None, :], solved, precision=HIGHEST)
    scores = jnp.where(lower_incl & same_seq, scores * scaling, -1e+30)
    row_max = lax.optimization_barrier(jnp.max(scores, axis=-1, keepdims=True))
    raw_weights = jnp.exp(scores - row_max)
    weights = low(raw_weights / lax.optimization_barrier(jnp.sum(raw_weights, axis=-1, keepdims=True)))
    mixed = jnp.einsum('hij,hjd->hid', weights, value_heads, precision=HIGHEST)
    return mixed.transpose(1, 0, 2).reshape(length, -1)

def block_forward(row_data, segment, params):
    attn_gain, w_query, w_key, w_value, w_house, w_beta, conv_taps, w_out, ffn_gain, w_gate, w_up, w_down = params
    normed = low(rms_norm(row_data, attn_gain))
    query_all = low(low_back(matmul(normed, w_query)))
    key_all = low(low_back(matmul(normed, w_key)))
    value_all = low(low_back(matmul(normed, w_value)))
    house_all = low_back(matmul(normed, w_house))
    beta_logit = low_back(matmul(normed, w_beta))
    mixer_out = path_mixer(query_all, key_all, value_all, house_all, beta_logit, conv_taps, segment)
    hidden = row_data + low_back(matmul(low(mixer_out), w_out))
    normed2 = low(rms_norm(hidden, ffn_gain))
    gate_all = low_back(matmul(normed2, w_gate))
    up_all = low_back(matmul(normed2, w_up))
    inner_act = low(jax.nn.silu(gate_all) * up_all)
    return hidden + low_back(matmul(inner_act, w_down))

def reference(tokens, cotangent, lengths, dealing, attn_gain, w_query, w_key, w_value, w_house, w_beta, conv_taps, w_out, ffn_gain, w_gate, w_up, w_down):
    params = tuple((item.astype(jnp.float32) for item in (attn_gain, w_query, w_key, w_value, w_house, w_beta, conv_taps, w_out, ffn_gain, w_gate, w_up, w_down)))
    group_count = lengths.shape[0]
    tok_rows = tokens.shape[0] // group_count
    width = tokens.shape[1]
    seq_ends = jnp.cumsum(lengths, axis=1, dtype=jnp.int32)
    places = jnp.arange(tok_rows, dtype=jnp.int32)
    segment = lax.optimization_barrier(jnp.sum((places[None, :, None] >= seq_ends[:, None, :]).astype(jnp.int32), axis=2, dtype=jnp.int32))
    group_base = jnp.repeat(jnp.arange(group_count, dtype=jnp.int32) * tok_rows, lengths.shape[1])
    starts = (seq_ends - lengths).reshape(-1) + group_base
    seq_first = starts[dealing]
    seq_size = lengths.reshape(-1)[dealing]
    offset = jnp.arange(LMAX, dtype=jnp.int32)
    row_index = jnp.clip(seq_first[:, None] + offset[None, :], 0, tokens.shape[0] - 1).astype(jnp.int32)
    live_mask = offset[None, :] < seq_size[:, None]
    row_data = tokens.astype(jnp.float32).reshape(group_count, tok_rows, width)
    checked = jax.checkpoint(block_forward)

    def forward(row_data, params):

        def scan_step(scan_carry, group_item):
            return (scan_carry, checked(group_item[0], group_item[1], params))
        _, group_out = lax.scan(scan_step, jnp.int32(0), (row_data, segment))
        flat_rows = group_out.reshape(-1, width)
        return jnp.where(live_mask[:, :, None], flat_rows[row_index], 0.0)
    result, pull = jax.vjp(forward, row_data, params)
    d_rows, d_params = pull(cotangent.astype(jnp.float32))
    return (result.astype(jnp.bfloat16), d_rows.reshape(-1, width).astype(jnp.bfloat16), d_params[0], d_params[1], d_params[2], d_params[3], d_params[4], d_params[5], d_params[6], d_params[7], d_params[8], d_params[9], d_params[10], d_params[11])
```

```python
import functools
import jax
import jax.numpy as jnp
from jax import lax
from jax.experimental import pallas as pl
from jax.experimental.pallas import tpu as pltpu
from jax.sharding import PartitionSpec as P

EPSILON = 1e-06
BF = jnp.bfloat16
F32 = jnp.float32


def dot_nn(a, b):
    return lax.dot_general(a, b, (((1,), (0,)), ((), ())), preferred_element_type=F32)


def dot_nt(a, b):
    return lax.dot_general(a, b, (((1,), (1,)), ((), ())), preferred_element_type=F32)


def dot_tn(a, b):
    return lax.dot_general(a, b, (((0,), (0,)), ((), ())), preferred_element_type=F32)


def halves(x):
    high = x.astype(BF)
    return high, (x - high.astype(F32)).astype(BF)


def dot_split(a, b):
    a_high, a_low = halves(a)
    b_high, b_low = halves(b)
    return dot_nn(a_high, b_high) + (dot_nn(a_high, b_low) + dot_nn(a_low, b_high))


def unit_lower_inverse(strict, base):
    size = strict.shape[0]
    lanes = 128
    tiles = size // lanes
    per_tile = lanes // base
    lane = lax.broadcasted_iota(jnp.int32, (base, lanes), 1)
    row = lax.broadcasted_iota(jnp.int32, (base, lanes), 0)
    owner = lane // base
    within = lane % base
    compact = []
    for tile in range(tiles):
        piece = jnp.zeros((base, lanes), F32)
        for block in range(per_tile):
            top = tile * lanes + block * base
            piece = jnp.where(
                owner == block, strict[top : top + base, tile * lanes : (tile + 1) * lanes], piece
            )
        compact.append(piece)
    solved = [jnp.where(row == within, 1.0, 0.0).astype(F32) for _ in range(tiles)]
    for step in range(base - 1):
        index = owner * base + step
        for tile in range(tiles):
            weight = jnp.take_along_axis(compact[tile], index, axis=1)
            solved[tile] = solved[tile] - weight * solved[tile][step : step + 1, :]
    rows = []
    for tile in range(tiles):
        for block in range(per_tile):
            piece = jnp.where(owner == block, solved[tile], 0.0)
            parts = [jnp.zeros((base, lanes), F32)] * tiles
            parts[tile] = piece
            rows.append(jnp.concatenate(parts, axis=1))
    inverse = jnp.concatenate(rows, axis=0)
    grown = base * 2
    row_big = lax.broadcasted_iota(jnp.int32, (size, size), 0)
    col_big = lax.broadcasted_iota(jnp.int32, (size, size), 1)
    while grown < size:
        joined = (row_big // grown == col_big // grown) & (
            row_big // (grown // 2) != col_big // (grown // 2)
        )
        cross = jnp.where(joined, strict, 0.0)
        inverse = inverse - dot_split(dot_split(inverse, cross), inverse)
        grown *= 2
    half = size // 2
    first, second = inverse[:half, :half], inverse[half:, half:]
    corner = -dot_split(dot_split(second, strict[half:, :half]), first)
    top = jnp.concatenate([first, jnp.zeros((half, half), F32)], axis=1)
    bottom = jnp.concatenate([corner, second], axis=1)
    return jnp.concatenate([top, bottom], axis=0)


def shifted_rows(x, amount, place):
    return jnp.where(place >= amount, pltpu.roll(x, amount, 0), 0.0)


def direction(house, taps, place):
    conv = taps[0:1, :] * house
    for shift in range(1, taps.shape[0]):
        conv = conv + taps[shift : shift + 1, :] * shifted_rows(house, shift, place)
    inverse = lax.rsqrt(jnp.sum(conv * conv, axis=1, keepdims=True) + EPSILON)
    return conv, inverse


PAIRS = ((0, 0), (1, 0), (1, 1))


def scores_of(query, key, house_dir, begin, half, a, b):
    rows, cols = slice(a * half, (a + 1) * half), slice(b * half, (b + 1) * half)
    left = jnp.concatenate([query[rows], house_dir[rows]], axis=0)
    right = jnp.concatenate([key[cols], house_dir[cols]], axis=0)
    every = dot_nt(left, right)
    col = lax.broadcasted_iota(jnp.int32, (half, half), 1) + b * half
    row = lax.broadcasted_iota(jnp.int32, (half, half), 0) + a * half
    inside = col >= begin[rows]
    upto = inside & (col <= row)
    before = inside & (col < row)
    return (
        every[:half, :half],
        jnp.where(upto, every[:half, half:], 0.0),
        jnp.where(before, every[half:, :half], 0.0),
        jnp.where(before, every[half:, half:], 0.0),
        upto,
        before,
    )


def forward_head(query, key, value, house, logit, taps, begin, place):
    half = query.shape[0] // 2
    scaling = query.shape[1] ** (-0.5)
    conv, inverse = direction(house, taps, place)
    house_dir = (conv * inverse).astype(BF)
    beta = 2.0 * jax.nn.sigmoid(logit)
    raw, cross, know, gram, upto = {}, {}, {}, {}, {}
    for a, b in PAIRS:
        raw[a, b], x, know[a, b], g, upto[a, b], _ = scores_of(
            query, key, house_dir, begin, half, a, b
        )
        beta_cols = beta[:, b * half : (b + 1) * half]
        cross[a, b] = (x * beta_cols).astype(BF)
        gram[a, b] = g * beta_cols
    eye = (
        lax.broadcasted_iota(jnp.int32, (half, half), 0)
        == lax.broadcasted_iota(jnp.int32, (half, half), 1)
    )
    tail = {}
    for a in (0, 1):
        tail[a] = jnp.where(eye, 0.0, unit_lower_inverse(gram[a, a], 32)).astype(BF)
    z00 = know[0, 0] + dot_nn(tail[0], know[0, 0].astype(BF))
    z00b = z00.astype(BF)
    z11 = know[1, 1] + dot_nn(tail[1], know[1, 1].astype(BF))
    z11b = z11.astype(BF)
    rest = know[1, 0] - dot_nn(gram[1, 0].astype(BF), z00b)
    z10 = rest + dot_nn(tail[1], rest.astype(BF))
    z10b = z10.astype(BF)
    s00 = raw[0, 0] - dot_nn(cross[0, 0], z00b)
    s10 = raw[1, 0] - dot_nn(cross[1, 0], z00b) - dot_nn(cross[1, 1], z10b)
    s11 = raw[1, 1] - dot_nn(cross[1, 1], z11b)
    s00 = jnp.where(upto[0, 0], s00 * scaling, -1e30)
    s10 = jnp.where(upto[1, 0], s10 * scaling, -1e30)
    s11 = jnp.where(upto[1, 1], s11 * scaling, -1e30)
    top0 = jnp.max(s00, axis=1, keepdims=True)
    top1 = jnp.maximum(
        jnp.max(s10, axis=1, keepdims=True), jnp.max(s11, axis=1, keepdims=True)
    )
    e00, e10, e11 = jnp.exp(s00 - top0), jnp.exp(s10 - top1), jnp.exp(s11 - top1)
    sum0 = jnp.sum(e00, axis=1, keepdims=True)
    sum1 = jnp.sum(e10, axis=1, keepdims=True) + jnp.sum(e11, axis=1, keepdims=True)
    inv0, inv1 = 1.0 / sum0, 1.0 / sum1
    p00, p10, p11 = (
        (e00 * inv0).astype(BF),
        (e10 * inv1).astype(BF),
        (e11 * inv1).astype(BF),
    )
    mixed0 = dot_nn(p00, value[:half])
    mixed1 = dot_nn(p10, value[:half]) + dot_nn(p11, value[half:])
    mixed = jnp.concatenate([mixed0, mixed1], axis=0).astype(BF)
    return mixed, (p00, p10, p11, z00b, z10b, z11b, tail[0], tail[1])


def forward_kernel(heads, begin_ref, logit_ref, taps_ref, house_ref, q_ref, k_ref, v_ref, mixed_ref, kept_ref):
    step = pl.program_id(0)
    begin = begin_ref[...]
    rows = begin.shape[0]
    place = lax.broadcasted_iota(jnp.int32, (rows, 1), 0) - begin
    for head in range(heads):
        cols = slice(head * 128, (head + 1) * 128)
        logit = logit_ref[pl.ds(step * heads + head, 1), :]
        mixed, kept = forward_head(
            q_ref[:, cols], k_ref[:, cols], v_ref[:, cols], house_ref[:, cols], logit,
            taps_ref[:, cols], begin, place,
        )
        mixed_ref[:, cols] = mixed
        for slot, item in enumerate(kept):
            kept_ref[head, slot] = item


def mixer_forward(begin, logit, taps, house, query, key, value, heads=2):
    rows, width = query.shape
    count = width // 128
    half = rows // 2
    wide = pl.BlockSpec((rows, heads * 128), lambda i: (0, i))
    return pl.pallas_call(
        functools.partial(forward_kernel, heads),
        grid=(count // heads,),
        in_specs=[
            pl.BlockSpec((rows, 1), lambda i: (0, 0)),
            pl.BlockSpec(logit.shape, lambda i: (0, 0)),
            pl.BlockSpec((taps.shape[0], heads * 128), lambda i: (0, i)),
            wide, wide, wide, wide,
        ],
        out_specs=[wide, pl.BlockSpec((heads, 8, half, half), lambda i: (i, 0, 0, 0))],
        out_shape=[
            jax.ShapeDtypeStruct((rows, width), BF),
            jax.ShapeDtypeStruct((count, 8, half, half), BF),
        ],
        compiler_params=pltpu.CompilerParams(vmem_limit_bytes=56 << 20),
        cost_estimate=pl.CostEstimate(flops=60_000_000_000, bytes_accessed=16_000_000, transcendentals=2_000_000),
        name="mixer_forward",
    )(begin, logit, taps, house, query, key, value)


def backward_head(query, key, value, house, logit, taps, begin, place, d_mixed, kept):
    p00, p10, p11, z00, z10, z11, tail0, tail1 = kept
    rows = query.shape[0]
    half = rows // 2
    scaling = query.shape[1] ** (-0.5)
    conv, inverse = direction(house, taps, place)
    direct = conv * inverse
    house_dir = direct.astype(BF)
    beta = 2.0 * jax.nn.sigmoid(logit)
    cross, cross_b, gram, gram_raw, upto, before, beta_cols = {}, {}, {}, {}, {}, {}, {}
    for a, b in PAIRS:
        _, cross[a, b], _, gram_raw[a, b], upto[a, b], before[a, b] = scores_of(
            query, key, house_dir, begin, half, a, b
        )
        beta_cols[b] = beta[:, b * half : (b + 1) * half]
        cross_b[a, b] = (cross[a, b] * beta_cols[b]).astype(BF)
    gram10 = (gram_raw[1, 0] * beta_cols[0]).astype(BF)
    d0, d1 = d_mixed[:half], d_mixed[half:]
    v0, v1 = value[:half], value[half:]
    dp00, dp10, dp11 = dot_nt(d0, v0), dot_nt(d1, v0), dot_nt(d1, v1)
    dv0 = dot_tn(p00, d0) + dot_tn(p10, d1)
    dv1 = dot_tn(p11, d1)
    f00, f10, f11 = p00.astype(F32), p10.astype(F32), p11.astype(F32)
    mean0 = jnp.sum(f00 * dp00, axis=1, keepdims=True)
    mean1 = jnp.sum(f10 * dp10, axis=1, keepdims=True) + jnp.sum(f11 * dp11, axis=1, keepdims=True)
    ds = {
        (0, 0): (f00 * (dp00 - mean0) * scaling).astype(BF),
        (1, 0): (f10 * (dp10 - mean1) * scaling).astype(BF),
        (1, 1): (f11 * (dp11 - mean1) * scaling).astype(BF),
    }
    dx = {
        (0, 0): dot_nt(ds[0, 0], z00),
        (1, 0): dot_nt(ds[1, 0], z00),
        (1, 1): dot_nt(ds[1, 1], z11) + dot_nt(ds[1, 0], z10),
    }
    dz00 = dot_tn(cross_b[0, 0], ds[0, 0]) + dot_tn(cross_b[1, 0], ds[1, 0])
    dz10 = dot_tn(cross_b[1, 1], ds[1, 0])
    dz11 = dot_tn(cross_b[1, 1], ds[1, 1])
    e11 = dz11 + dot_tn(tail1, dz11.astype(BF))
    e10 = dz10 + dot_tn(tail1, dz10.astype(BF))
    rest = dz00 - dot_tn(gram10, e10.astype(BF))
    e00 = rest + dot_tn(tail0, rest.astype(BF))
    e00b, e10b, e11b = e00.astype(BF), e10.astype(BF), e11.astype(BF)
    dn = {
        (0, 0): dot_nt(e00b, z00),
        (1, 0): dot_nt(e10b, z00),
        (1, 1): dot_nt(e10b, z10) + dot_nt(e11b, z11),
    }
    dy = {(0, 0): e00, (1, 0): e10, (1, 1): e11}
    d_beta = [jnp.zeros((1, half), F32), jnp.zeros((1, half), F32)]
    d_q = [0.0, 0.0]
    d_w = [0.0, 0.0]
    d_k = [0.0, 0.0]
    for a, b in PAIRS:
        part_x = jnp.where(upto[a, b], -dx[a, b], 0.0)
        part_n = jnp.where(before[a, b], dn[a, b], 0.0)
        part_y = jnp.where(before[a, b], -dy[a, b], 0.0)
        d_beta[b] = d_beta[b] + jnp.sum(
            part_x * cross[a, b] + part_n * gram_raw[a, b], axis=0, keepdims=True
        )
        upper = jnp.concatenate([ds[a, b], (part_x * beta_cols[b]).astype(BF)], axis=1)
        lower = jnp.concatenate([part_y.astype(BF), (part_n * beta_cols[b]).astype(BF)], axis=1)
        big = jnp.concatenate([upper, lower], axis=0)
        rows_a, cols_b = slice(a * half, (a + 1) * half), slice(b * half, (b + 1) * half)
        right = jnp.concatenate([key[cols_b], house_dir[cols_b]], axis=0)
        left = jnp.concatenate([query[rows_a], house_dir[rows_a]], axis=0)
        by_row = dot_nn(big, right)
        by_col = dot_tn(big, left)
        d_q[a] = d_q[a] + by_row[:half]
        d_w[a] = d_w[a] + by_row[half:]
        d_k[b] = d_k[b] + by_col[:half]
        d_w[b] = d_w[b] + by_col[half:]
    d_dir = jnp.concatenate(d_w, axis=0)
    d_conv = inverse * d_dir - direct * (
        inverse * jnp.sum(direct * d_dir, axis=1, keepdims=True)
    )
    d_house = taps[0:1, :] * d_conv
    d_taps = [jnp.sum(d_conv * house, axis=0, keepdims=True)]
    for shift in range(1, taps.shape[0]):
        live = jnp.where(place >= shift, d_conv, 0.0)
        d_house = d_house + taps[shift : shift + 1, :] * pltpu.roll(live, rows - shift, 0)
        d_taps.append(jnp.sum(live * pltpu.roll(house, shift, 0), axis=0, keepdims=True))
    d_logit = jnp.concatenate(d_beta, axis=1) * beta * (1.0 - 0.5 * beta)
    return (
        jnp.concatenate(d_q, axis=0).astype(BF),
        jnp.concatenate(d_k, axis=0).astype(BF),
        jnp.concatenate([dv0, dv1], axis=0).astype(BF),
        d_house.astype(BF),
        d_logit,
        d_taps,
    )


def backward_kernel(
    heads, begin_ref, logit_ref, taps_ref, house_ref, q_ref, k_ref, v_ref, dm_ref, kept_ref,
    dq_ref, dk_ref, dv_ref, dh_ref, dl_ref, dt_ref,
):
    step = pl.program_id(0)
    begin = begin_ref[...]
    rows = begin.shape[0]
    place = lax.broadcasted_iota(jnp.int32, (rows, 1), 0) - begin
    for head in range(heads):
        cols = slice(head * 128, (head + 1) * 128)
        logit = logit_ref[pl.ds(step * heads + head, 1), :]
        kept = tuple(kept_ref[head, slot] for slot in range(8))
        d_q, d_k, d_v, d_h, d_l, d_t = backward_head(
            q_ref[:, cols], k_ref[:, cols], v_ref[:, cols], house_ref[:, cols], logit,
            taps_ref[:, cols], begin, place, dm_ref[:, cols], kept,
        )
        dq_ref[:, cols] = d_q
        dk_ref[:, cols] = d_k
        dv_ref[:, cols] = d_v
        dh_ref[:, cols] = d_h
        dl_ref[pl.ds(step * heads + head, 1), :] = d_l
        for tap, item in enumerate(d_t):
            dt_ref[tap : tap + 1, cols] = item


def mixer_backward(begin, logit, taps, house, query, key, value, d_mixed, kept, heads=2):
    rows, width = query.shape
    count = width // 128
    half = rows // 2
    wide = pl.BlockSpec((rows, heads * 128), lambda i: (0, i))
    narrow = pl.BlockSpec((taps.shape[0], heads * 128), lambda i: (0, i))
    whole = pl.BlockSpec(logit.shape, lambda i: (0, 0))
    big = jax.ShapeDtypeStruct((rows, width), BF)
    return pl.pallas_call(
        functools.partial(backward_kernel, heads),
        grid=(count // heads,),
        in_specs=[
            pl.BlockSpec((rows, 1), lambda i: (0, 0)),
            whole, narrow, wide, wide, wide, wide, wide,
            pl.BlockSpec((heads, 8, half, half), lambda i: (i, 0, 0, 0)),
        ],
        out_specs=[wide, wide, wide, wide, whole, narrow],
        out_shape=[big, big, big, big, jax.ShapeDtypeStruct(logit.shape, F32), jax.ShapeDtypeStruct(taps.shape, F32)],
        compiler_params=pltpu.CompilerParams(vmem_limit_bytes=56 << 20),
        cost_estimate=pl.CostEstimate(flops=60_000_000_000, bytes_accessed=20_000_000, transcendentals=2_000_000),
        name="mixer_backward",
    )(begin, logit, taps, house, query, key, value, d_mixed, kept)


def wgrad_kernel(order_ref, left_ref, right_ref, out_ref, packed):
    count = out_ref.shape[0] // left_ref.shape[1]
    block = left_ref.shape[1]

    @pl.when(pl.program_id(0) == 0)
    def _():
        for i in range(count):
            packed[i * block : (i + 1) * block, :] = left_ref[order_ref[i]]

    out_ref[...] = dot_nn(packed[...], right_ref[...]).astype(out_ref.dtype)


def wgrad(order, left, right, dtype, tile=512):
    count = order.shape[0]
    block, tokens = left.shape[1:]
    columns = right.shape[1]
    tile = next(t for t in (tile, 384, 256, 128) if columns % t == 0)
    return pl.pallas_call(
        wgrad_kernel,
        grid_spec=pltpu.PrefetchScalarGridSpec(
            num_scalar_prefetch=1,
            grid=(columns // tile,),
            in_specs=[
                pl.BlockSpec(left.shape, lambda j, order: (0, 0, 0)),
                pl.BlockSpec((tokens, tile), lambda j, order: (0, j)),
            ],
            out_specs=pl.BlockSpec((count * block, tile), lambda j, order: (0, j)),
            scratch_shapes=[pltpu.VMEM((count * block, tokens), BF)],
        ),
        out_shape=jax.ShapeDtypeStruct((count * block, columns), dtype),
        compiler_params=pltpu.CompilerParams(vmem_limit_bytes=32 << 20),
        cost_estimate=pl.CostEstimate(
            flops=2 * count * block * tokens * columns,
            bytes_accessed=2 * (left.size + right.size + count * block * columns),
            transcendentals=0,
        ),
        name="wgrad",
    )(order, left, right)


def swap(x, axis, bit):
    size = lax.axis_size(axis)
    return lax.ppermute(x, axis, [(i, i ^ (1 << bit)) for i in range(size)])


def shard_order(me, size, bits):
    position = size - 1 - jnp.arange(size, dtype=jnp.int32)
    flips = jnp.zeros((size,), jnp.int32)
    for rank, bit in enumerate(bits):
        flips = flips + (((position >> (len(bits) - 1 - rank)) & 1) << bit)
    return me ^ flips


def scatter_sum(leave, stay, bits):
    terms = [stay, swap(leave, "dp", bits[0])]
    for bit in bits[1:]:
        half = terms[0].shape[0] // 2
        out = sum(t[:half].astype(F32) for t in terms).astype(BF)
        terms = [t[half:] for t in terms] + [swap(out, "dp", bit)]
    return sum(t.astype(F32) for t in terms)


def tensor_sum(x):
    if lax.axis_size("tensor") == 2:
        return x.astype(F32) + swap(x, "tensor", 0).astype(F32)
    return lax.psum(x, "tensor").astype(F32)


def contract_cols(a, b):
    return dot_nt(a, b)


def norm_back(d_normed, source, inverse, gain_vec):
    scaled = d_normed * gain_vec
    return inverse * scaled - source * (inverse * inverse * inverse) * jnp.mean(
        scaled * source, axis=1, keepdims=True
    )


def chosen(index, count):
    return (index[:, None] == jnp.arange(count, dtype=jnp.int32)[None, :]).astype(BF)


def on_device(
    tokens,
    cotangent,
    lengths,
    dealing,
    attn_gain,
    w_query,
    w_key,
    w_value,
    w_house,
    w_beta,
    conv_taps,
    w_out,
    ffn_gain,
    w_gate,
    w_up,
    w_down,
):
    rows, width = tokens.shape
    slots, span = cotangent.shape[:2]
    size = lax.axis_size("dp")
    me = lax.axis_index("dp")
    block = width // size
    up = [(i, i + 1) for i in range(size - 1)]
    down = [(i + 1, i) for i in range(size - 1)]

    own = lax.dynamic_index_in_dim(lengths, me, 0, keepdims=False)
    earlier = jnp.arange(slots)[None, :] < jnp.arange(slots)[:, None]
    starts = jnp.sum(jnp.where(earlier, own[None, :], 0), axis=1)
    row = jnp.arange(rows, dtype=jnp.int32)
    segment = jnp.sum((starts[None, :] <= row[:, None]).astype(jnp.int32), axis=1) - 1
    begin = jnp.max(jnp.where(starts[None, :] <= row[:, None], starts[None, :], 0), axis=1)
    ids = me * slots + jnp.arange(slots, dtype=jnp.int32)
    place = jnp.sum(
        jnp.where(
            dealing[None, :] == ids[:, None],
            jnp.arange(dealing.shape[0], dtype=jnp.int32)[None, :],
            0,
        ),
        axis=1,
    )
    holder = place // slots - me
    slot_of = place % slots
    held = lax.dynamic_slice_in_dim(dealing, me * slots, slots)
    held_from = held // slots - me
    slot_index = jnp.arange(slots, dtype=jnp.int32)
    slot_up = jnp.sum(jnp.where(held_from == 1, slot_index, 0))
    slot_down = jnp.sum(jnp.where(held_from == -1, slot_index, 0))

    cot_low = lax.ppermute(
        lax.dynamic_index_in_dim(cotangent, slot_up, 0, keepdims=False), "dp", up
    )
    cot_high = lax.ppermute(
        lax.dynamic_index_in_dim(cotangent, slot_down, 0, keepdims=False), "dp", down
    )
    which = jnp.arange(slots, dtype=jnp.int32)[None, :] == segment[:, None]
    row_holder = jnp.sum(jnp.where(which, holder[None, :], 0), axis=1)
    row_slot = jnp.sum(jnp.where(which, slot_of[None, :], 0), axis=1)
    offset = row - begin
    pick_own = chosen(jnp.where(row_holder == 0, row_slot * span + offset, -1), slots * span)
    pick_low = chosen(jnp.where(row_holder == -1, offset, -1), span)
    pick_high = chosen(jnp.where(row_holder == 1, offset, -1), span)
    d_final = (
        dot_nn(pick_own, cotangent.reshape(-1, width))
        + dot_nn(pick_low, cot_low)
        + dot_nn(pick_high, cot_high)
    ).astype(BF)

    row_data = tokens.astype(F32)
    inverse1 = lax.rsqrt(jnp.mean(row_data * row_data, axis=1, keepdims=True) + EPSILON)
    normed1 = (row_data * inverse1 * attn_gain).astype(BF)
    query = dot_nn(normed1, w_query).astype(BF)
    key = dot_nn(normed1, w_key).astype(BF)
    value = dot_nn(normed1, w_value).astype(BF)
    house = dot_nn(normed1, w_house)
    logit = lax.dot_general(
        w_beta, normed1, (((0,), (1,)), ((), ())), preferred_element_type=F32
    )
    begin_col = begin[:, None]
    mixed, kept = mixer_forward(begin_col, logit, conv_taps, house, query, key, value)
    hidden = row_data + tensor_sum(dot_nn(mixed, w_out))
    inverse2 = lax.rsqrt(jnp.mean(hidden * hidden, axis=1, keepdims=True) + EPSILON)
    normed2 = (hidden * inverse2 * ffn_gain).astype(BF)
    gate = dot_nn(normed2, w_gate)
    lift = dot_nn(normed2, w_up)
    gate_sig = jax.nn.sigmoid(gate)
    gate_silu = gate * gate_sig
    inner = (gate_silu * lift).astype(BF)

    d_inner = dot_nt(d_final, w_down)
    d_gate = (d_inner * lift * gate_sig * (1.0 + gate * (1.0 - gate_sig))).astype(BF)
    d_up = (d_inner * gate_silu).astype(BF)
    bits_a = list(range(size.bit_length() - 1))
    bits_b = [1, 0] + bits_a[2:]
    order_a = shard_order(me, size, bits_a)
    order_b = shard_order(me, size, bits_b)
    first = size // 2

    def sharded(left):
        return left.T.reshape(size, block, left.shape[0])

    def scattered(left, right, order, bits):
        leave = wgrad(order[:first], left, right, BF)
        stay = wgrad(order[first:], left, right, BF)
        return scatter_sum(leave, stay, bits)

    d_final_t = sharded(d_final)
    normed2_t = sharded(normed2)
    middle = inner.shape[1] // 2
    g_gate = scattered(normed2_t, d_gate, order_a, bits_a)
    g_up = scattered(normed2_t, d_up, order_b, bits_b)
    g_down_a = scattered(d_final_t, inner[:, :middle], order_a, bits_a)
    g_down_b = scattered(d_final_t, inner[:, middle:], order_b, bits_b)
    d_norm2 = tensor_sum(dot_nt(d_gate, w_gate) + dot_nt(d_up, w_up))
    g_ffn_gain = jnp.sum(d_norm2 * hidden * inverse2, axis=0)
    d_hidden = d_final.astype(F32) + norm_back(d_norm2, hidden, inverse2, ffn_gain)
    d_branch = d_hidden.astype(BF)
    d_mixed = dot_nt(d_branch, w_out).astype(BF)
    d_branch_t = sharded(d_branch)
    middle = mixed.shape[1] // 2
    g_out_a = scattered(d_branch_t, mixed[:, :middle], order_a, bits_a)
    g_out_b = scattered(d_branch_t, mixed[:, middle:], order_b, bits_b)

    d_query, d_key, d_value, d_house, d_logit, g_taps = mixer_backward(
        begin_col, logit, conv_taps, house, query, key, value, d_mixed, kept
    )
    d_logit_b = d_logit.astype(BF)
    normed1_t = sharded(normed1)
    heads = d_logit.shape[0]
    extra = jnp.pad(d_logit_b.T, ((0, 0), (0, 128 - heads)))
    columns = query.shape[1]
    g_qk = scattered(
        normed1_t, jnp.concatenate([d_query, d_key], axis=1), order_a, bits_a
    )
    g_vhb = scattered(
        normed1_t, jnp.concatenate([d_value, d_house, extra], axis=1), order_b, bits_b
    )
    d_norm1_part = (
        dot_nt(d_query, w_query)
        + dot_nt(d_key, w_key)
        + dot_nt(d_value, w_value)
        + dot_nt(d_house, w_house)
        + lax.dot_general(d_logit_b, w_beta, (((0,), (1,)), ((), ())), preferred_element_type=F32)
    )
    d_norm1 = tensor_sum(d_norm1_part)
    g_attn_gain = jnp.sum(d_norm1 * row_data * inverse1, axis=0)
    input_grad = (d_hidden + norm_back(d_norm1, row_data, inverse1, attn_gain)).astype(BF)

    small = jnp.concatenate([g_taps.reshape(-1), g_attn_gain, g_ffn_gain]).reshape(-1, 128)
    for bit in bits_a:
        small = small + swap(small, "dp", bit)
    small = small.reshape(-1)
    taps_total = small[: g_taps.size].reshape(g_taps.shape)
    gains = small[g_taps.size :].reshape(2, width)
    gains = lax.dynamic_slice_in_dim(gains, me * block, block, axis=1)

    down_part = dot_nn(inner, w_down).astype(BF)
    final = (hidden + tensor_sum(down_part)).astype(BF)
    offsets = jnp.arange(span, dtype=jnp.int32)

    def to_neighbour(by):
        start = jnp.sum(jnp.where(holder == by, starts, 0))
        length = jnp.sum(jnp.where(holder == by, own, 0))
        return dot_nn(chosen(jnp.where(offsets < length, start + offsets, -1), rows), final).astype(BF)

    out_low = lax.ppermute(to_neighbour(1), "dp", up)
    out_high = lax.ppermute(to_neighbour(-1), "dp", down)
    mine = held_from == 0
    inside = jnp.where(mine, held % slots, 0)
    slot_start = jnp.where(mine, starts[inside], 0)
    slot_length = jnp.where(mine, own[inside], 0)
    pick = jnp.where(
        offsets[None, :] < slot_length[:, None], slot_start[:, None] + offsets[None, :], -1
    ).reshape(-1)
    kept_rows = dot_nn(chosen(pick, rows), final).astype(BF).reshape(slots, span, width)
    output = jnp.where(
        (held_from == -1)[:, None, None],
        out_low[None],
        jnp.where((held_from == 1)[:, None, None], out_high[None], kept_rows),
    )
    return (
        output,
        input_grad,
        gains[0],
        g_qk[:, :columns],
        g_qk[:, columns:],
        g_vhb[:, :columns],
        g_vhb[:, columns : 2 * columns],
        g_vhb[:, 2 * columns : 2 * columns + heads],
        taps_total,
        jnp.concatenate([g_out_a, g_out_b], axis=1).T,
        gains[1],
        g_gate,
        g_up,
        jnp.concatenate([g_down_a, g_down_b], axis=1).T,
    )


def solution(mesh):
    in_specs = (
        P("dp", None),
        P("dp", None, None),
        P(),
        P(),
        P(),
        P(None, "tensor"),
        P(None, "tensor"),
        P(None, "tensor"),
        P(None, "tensor"),
        P(None, "tensor"),
        P(None, "tensor"),
        P("tensor", None),
        P(),
        P(None, "tensor"),
        P(None, "tensor"),
        P("tensor", None),
    )
    out_specs = (
        P("dp", None, None),
        P("dp", None),
        P("dp"),
        P("dp", "tensor"),
        P("dp", "tensor"),
        P("dp", "tensor"),
        P("dp", "tensor"),
        P("dp", "tensor"),
        P(None, "tensor"),
        P("tensor", "dp"),
        P("dp"),
        P("dp", "tensor"),
        P("dp", "tensor"),
        P("tensor", "dp"),
    )
    return jax.shard_map(
        on_device, mesh=mesh, in_specs=in_specs, out_specs=out_specs, check_vma=False
    )
```

```python
import functools
import jax
import jax.numpy as jnp
from jax import lax
from jax.experimental import pallas as pl
from jax.experimental.pallas import tpu as pltpu
from jax.sharding import PartitionSpec as P

EPSILON = 1e-06
BF = jnp.bfloat16
F32 = jnp.float32

VMEM = 60 << 20
COST = pl.CostEstimate(flops=0, bytes_accessed=0, transcendentals=0)


def dot_nn(a, b):
    return lax.dot_general(a, b, (((1,), (0,)), ((), ())), preferred_element_type=F32)


def dot_nt(a, b):
    return lax.dot_general(a, b, (((1,), (1,)), ((), ())), preferred_element_type=F32)


def dot_tn(a, b):
    return lax.dot_general(a, b, (((0,), (0,)), ((), ())), preferred_element_type=F32)


def halves(x):
    high = x.astype(BF)
    return high, (x - high.astype(F32)).astype(BF)


def dot_split(a, b):
    a_high, a_low = halves(a)
    b_high, b_low = halves(b)
    return dot_nn(a_high, b_high) + (dot_nn(a_high, b_low) + dot_nn(a_low, b_high))


def unit_lower_inverse(strict, base):
    size = strict.shape[0]
    lanes = 128
    tiles = size // lanes
    per_tile = lanes // base
    lane = lax.broadcasted_iota(jnp.int32, (base, lanes), 1)
    row = lax.broadcasted_iota(jnp.int32, (base, lanes), 0)
    owner = lane // base
    within = lane % base
    compact = []
    for tile in range(tiles):
        piece = jnp.zeros((base, lanes), F32)
        for block in range(per_tile):
            top = tile * lanes + block * base
            piece = jnp.where(
                owner == block, strict[top : top + base, tile * lanes : (tile + 1) * lanes], piece
            )
        compact.append(piece)
    solved = [jnp.where(row == within, 1.0, 0.0).astype(F32) for _ in range(tiles)]
    for step in range(base - 1):
        index = owner * base + step
        for tile in range(tiles):
            weight = jnp.take_along_axis(compact[tile], index, axis=1)
            solved[tile] = solved[tile] - weight * solved[tile][step : step + 1, :]
    rows = []
    for tile in range(tiles):
        for block in range(per_tile):
            piece = jnp.where(owner == block, solved[tile], 0.0)
            parts = [jnp.zeros((base, lanes), F32)] * tiles
            parts[tile] = piece
            rows.append(jnp.concatenate(parts, axis=1))
    inverse = jnp.concatenate(rows, axis=0)
    grown = base * 2
    row_big = lax.broadcasted_iota(jnp.int32, (size, size), 0)
    col_big = lax.broadcasted_iota(jnp.int32, (size, size), 1)
    while grown < size:
        joined = (row_big // grown == col_big // grown) & (
            row_big // (grown // 2) != col_big // (grown // 2)
        )
        cross = jnp.where(joined, strict, 0.0)
        inverse = inverse - dot_split(dot_split(inverse, cross), inverse)
        grown *= 2
    half = size // 2
    first, second = inverse[:half, :half], inverse[half:, half:]
    corner = -dot_split(dot_split(second, strict[half:, :half]), first)
    top = jnp.concatenate([first, jnp.zeros((half, half), F32)], axis=1)
    bottom = jnp.concatenate([corner, second], axis=1)
    return jnp.concatenate([top, bottom], axis=0)


def shifted_rows(x, amount, place):
    return jnp.where(place >= amount, pltpu.roll(x, amount, 0), 0.0)


def direction(house, taps, place):
    conv = taps[0:1, :] * house
    for shift in range(1, taps.shape[0]):
        conv = conv + taps[shift : shift + 1, :] * shifted_rows(house, shift, place)
    inverse = lax.rsqrt(jnp.sum(conv * conv, axis=1, keepdims=True) + EPSILON)
    return conv, inverse


PAIRS = ((0, 0), (1, 0), (1, 1))


def scores_of(query, key, house_dir, begin, half, a, b):
    rows, cols = slice(a * half, (a + 1) * half), slice(b * half, (b + 1) * half)
    left = jnp.concatenate([query[rows], house_dir[rows]], axis=0)
    right = jnp.concatenate([key[cols], house_dir[cols]], axis=0)
    every = dot_nt(left, right)
    col = lax.broadcasted_iota(jnp.int32, (half, half), 1) + b * half
    row = lax.broadcasted_iota(jnp.int32, (half, half), 0) + a * half
    inside = col >= begin[rows]
    upto = inside & (col <= row)
    before = inside & (col < row)
    return (
        every[:half, :half],
        jnp.where(upto, every[:half, half:], 0.0),
        jnp.where(before, every[half:, :half], 0.0),
        jnp.where(before, every[half:, half:], 0.0),
        upto,
        before,
    )


def forward_head(query, key, value, house, logit, taps, begin, place):
    half = query.shape[0] // 2
    scaling = query.shape[1] ** (-0.5)
    conv, inverse = direction(house, taps, place)
    house_dir = (conv * inverse).astype(BF)
    beta = 2.0 * jax.nn.sigmoid(logit)
    raw, cross, know, gram, upto = {}, {}, {}, {}, {}
    for a, b in PAIRS:
        raw[a, b], x, know[a, b], g, upto[a, b], _ = scores_of(
            query, key, house_dir, begin, half, a, b
        )
        beta_cols = beta[:, b * half : (b + 1) * half]
        cross[a, b] = (x * beta_cols).astype(BF)
        gram[a, b] = g * beta_cols
    eye = (
        lax.broadcasted_iota(jnp.int32, (half, half), 0)
        == lax.broadcasted_iota(jnp.int32, (half, half), 1)
    )
    tail = {}
    for a in (0, 1):
        tail[a] = jnp.where(eye, 0.0, unit_lower_inverse(gram[a, a], 32)).astype(BF)
    z00 = know[0, 0] + dot_nn(tail[0], know[0, 0].astype(BF))
    z00b = z00.astype(BF)
    z11 = know[1, 1] + dot_nn(tail[1], know[1, 1].astype(BF))
    z11b = z11.astype(BF)
    rest = know[1, 0] - dot_nn(gram[1, 0].astype(BF), z00b)
    z10 = rest + dot_nn(tail[1], rest.astype(BF))
    z10b = z10.astype(BF)
    s00 = raw[0, 0] - dot_nn(cross[0, 0], z00b)
    s10 = raw[1, 0] - dot_nn(cross[1, 0], z00b) - dot_nn(cross[1, 1], z10b)
    s11 = raw[1, 1] - dot_nn(cross[1, 1], z11b)
    s00 = jnp.where(upto[0, 0], s00 * scaling, -1e30)
    s10 = jnp.where(upto[1, 0], s10 * scaling, -1e30)
    s11 = jnp.where(upto[1, 1], s11 * scaling, -1e30)
    top0 = jnp.max(s00, axis=1, keepdims=True)
    top1 = jnp.maximum(
        jnp.max(s10, axis=1, keepdims=True), jnp.max(s11, axis=1, keepdims=True)
    )
    e00, e10, e11 = jnp.exp(s00 - top0), jnp.exp(s10 - top1), jnp.exp(s11 - top1)
    sum0 = jnp.sum(e00, axis=1, keepdims=True)
    sum1 = jnp.sum(e10, axis=1, keepdims=True) + jnp.sum(e11, axis=1, keepdims=True)
    inv0, inv1 = 1.0 / sum0, 1.0 / sum1
    p00, p10, p11 = (
        (e00 * inv0).astype(BF),
        (e10 * inv1).astype(BF),
        (e11 * inv1).astype(BF),
    )
    mixed0 = dot_nn(p00, value[:half])
    mixed1 = dot_nn(p10, value[:half]) + dot_nn(p11, value[half:])
    mixed = jnp.concatenate([mixed0, mixed1], axis=0).astype(BF)
    return mixed, (p00, p10, p11, z00b, z10b, z11b, tail[0], tail[1])


def forward_kernel(heads, slots, lengths_ref, me_ref, logit_ref, taps_ref, house_ref, q_ref, k_ref, v_ref, mixed_ref, kept_ref):
    step = pl.program_id(0)
    rows = q_ref.shape[0]
    row = lax.broadcasted_iota(jnp.int32, (rows, 1), 0)
    begin = begins(starts_of(lengths_ref, me_ref[0], slots), row)
    place = row - begin
    for head in range(heads):
        cols = slice(head * 128, (head + 1) * 128)
        logit = logit_ref[pl.ds(step * heads + head, 1), :]
        mixed, kept = forward_head(
            q_ref[:, cols], k_ref[:, cols], v_ref[:, cols], house_ref[:, cols], logit,
            taps_ref[:, cols], begin, place,
        )
        mixed_ref[:, cols] = mixed
        for slot, item in enumerate(kept):
            kept_ref[head, slot] = item


def mixer_forward(lengths, me, logit, taps, house, query, key, value, heads=2):
    rows, width = query.shape
    count = width // 128
    half = rows // 2
    wide = pl.BlockSpec((rows, heads * 128), lambda i: (0, i))
    return pl.pallas_call(
        functools.partial(forward_kernel, heads, lengths.shape[1]),
        grid=(count // heads,),
        in_specs=[
            pl.BlockSpec(memory_space=pltpu.SMEM),
            pl.BlockSpec(memory_space=pltpu.SMEM),
            pl.BlockSpec(logit.shape, lambda i: (0, 0)),
            pl.BlockSpec((taps.shape[0], heads * 128), lambda i: (0, i)),
            wide, wide, wide, wide,
        ],
        out_specs=[wide, pl.BlockSpec((heads, 8, half, half), lambda i: (i, 0, 0, 0))],
        out_shape=[
            jax.ShapeDtypeStruct((rows, width), BF),
            jax.ShapeDtypeStruct((count, 8, half, half), BF),
        ],
        compiler_params=pltpu.CompilerParams(vmem_limit_bytes=VMEM),
        cost_estimate=COST,
        name="mixer_forward",
    )(lengths, me, logit, taps, house, query, key, value)


def backward_head(query, key, value, house, logit, taps, begin, place, d_mixed, kept):
    p00, p10, p11, z00, z10, z11, tail0, tail1 = kept
    rows = query.shape[0]
    half = rows // 2
    scaling = query.shape[1] ** (-0.5)
    conv, inverse = direction(house, taps, place)
    direct = conv * inverse
    house_dir = direct.astype(BF)
    beta = 2.0 * jax.nn.sigmoid(logit)
    cross, cross_b, gram, gram_raw, upto, before, beta_cols = {}, {}, {}, {}, {}, {}, {}
    for a, b in PAIRS:
        _, cross[a, b], _, gram_raw[a, b], upto[a, b], before[a, b] = scores_of(
            query, key, house_dir, begin, half, a, b
        )
        beta_cols[b] = beta[:, b * half : (b + 1) * half]
        cross_b[a, b] = (cross[a, b] * beta_cols[b]).astype(BF)
    gram10 = (gram_raw[1, 0] * beta_cols[0]).astype(BF)
    d0, d1 = d_mixed[:half], d_mixed[half:]
    v0, v1 = value[:half], value[half:]
    dp00, dp10, dp11 = dot_nt(d0, v0), dot_nt(d1, v0), dot_nt(d1, v1)
    dv0 = dot_tn(p00, d0) + dot_tn(p10, d1)
    dv1 = dot_tn(p11, d1)
    f00, f10, f11 = p00.astype(F32), p10.astype(F32), p11.astype(F32)
    mean0 = jnp.sum(f00 * dp00, axis=1, keepdims=True)
    mean1 = jnp.sum(f10 * dp10, axis=1, keepdims=True) + jnp.sum(f11 * dp11, axis=1, keepdims=True)
    ds = {
        (0, 0): (f00 * (dp00 - mean0) * scaling).astype(BF),
        (1, 0): (f10 * (dp10 - mean1) * scaling).astype(BF),
        (1, 1): (f11 * (dp11 - mean1) * scaling).astype(BF),
    }
    dx = {
        (0, 0): dot_nt(ds[0, 0], z00),
        (1, 0): dot_nt(ds[1, 0], z00),
        (1, 1): dot_nt(ds[1, 1], z11) + dot_nt(ds[1, 0], z10),
    }
    dz00 = dot_tn(cross_b[0, 0], ds[0, 0]) + dot_tn(cross_b[1, 0], ds[1, 0])
    dz10 = dot_tn(cross_b[1, 1], ds[1, 0])
    dz11 = dot_tn(cross_b[1, 1], ds[1, 1])
    e11 = dz11 + dot_tn(tail1, dz11.astype(BF))
    e10 = dz10 + dot_tn(tail1, dz10.astype(BF))
    rest = dz00 - dot_tn(gram10, e10.astype(BF))
    e00 = rest + dot_tn(tail0, rest.astype(BF))
    e00b, e10b, e11b = e00.astype(BF), e10.astype(BF), e11.astype(BF)
    dn = {
        (0, 0): dot_nt(e00b, z00),
        (1, 0): dot_nt(e10b, z00),
        (1, 1): dot_nt(e10b, z10) + dot_nt(e11b, z11),
    }
    dy = {(0, 0): e00, (1, 0): e10, (1, 1): e11}
    d_beta = [jnp.zeros((1, half), F32), jnp.zeros((1, half), F32)]
    d_q = [0.0, 0.0]
    d_w = [0.0, 0.0]
    d_k = [0.0, 0.0]
    for a, b in PAIRS:
        part_x = jnp.where(upto[a, b], -dx[a, b], 0.0)
        part_n = jnp.where(before[a, b], dn[a, b], 0.0)
        part_y = jnp.where(before[a, b], -dy[a, b], 0.0)
        d_beta[b] = d_beta[b] + jnp.sum(
            part_x * cross[a, b] + part_n * gram_raw[a, b], axis=0, keepdims=True
        )
        upper = jnp.concatenate([ds[a, b], (part_x * beta_cols[b]).astype(BF)], axis=1)
        lower = jnp.concatenate([part_y.astype(BF), (part_n * beta_cols[b]).astype(BF)], axis=1)
        big = jnp.concatenate([upper, lower], axis=0)
        rows_a, cols_b = slice(a * half, (a + 1) * half), slice(b * half, (b + 1) * half)
        right = jnp.concatenate([key[cols_b], house_dir[cols_b]], axis=0)
        left = jnp.concatenate([query[rows_a], house_dir[rows_a]], axis=0)
        by_row = dot_nn(big, right)
        by_col = dot_tn(big, left)
        d_q[a] = d_q[a] + by_row[:half]
        d_w[a] = d_w[a] + by_row[half:]
        d_k[b] = d_k[b] + by_col[:half]
        d_w[b] = d_w[b] + by_col[half:]
    d_dir = jnp.concatenate(d_w, axis=0)
    d_conv = inverse * d_dir - direct * (
        inverse * jnp.sum(direct * d_dir, axis=1, keepdims=True)
    )
    d_house = taps[0:1, :] * d_conv
    d_taps = [jnp.sum(d_conv * house, axis=0, keepdims=True)]
    for shift in range(1, taps.shape[0]):
        live = jnp.where(place >= shift, d_conv, 0.0)
        d_house = d_house + taps[shift : shift + 1, :] * pltpu.roll(live, rows - shift, 0)
        d_taps.append(jnp.sum(live * pltpu.roll(house, shift, 0), axis=0, keepdims=True))
    d_logit = jnp.concatenate(d_beta, axis=1) * beta * (1.0 - 0.5 * beta)
    return (
        jnp.concatenate(d_q, axis=0).astype(BF),
        jnp.concatenate(d_k, axis=0).astype(BF),
        jnp.concatenate([dv0, dv1], axis=0).astype(BF),
        d_house.astype(BF),
        d_logit,
        d_taps,
    )


def backward_kernel(
    heads, slots, lengths_ref, me_ref, logit_ref, taps_ref, house_ref, q_ref, k_ref, v_ref, dm_ref, kept_ref,
    four_ref, dl_ref, dt_ref,
):
    step = pl.program_id(0)
    rows = q_ref.shape[0]
    row = lax.broadcasted_iota(jnp.int32, (rows, 1), 0)
    begin = begins(starts_of(lengths_ref, me_ref[0], slots), row)
    place = row - begin
    for head in range(heads):
        cols = slice(head * 128, (head + 1) * 128)
        logit = logit_ref[pl.ds(step * heads + head, 1), :]
        kept = tuple(kept_ref[head, slot] for slot in range(8))
        d_q, d_k, d_v, d_h, d_l, d_t = backward_head(
            q_ref[:, cols], k_ref[:, cols], v_ref[:, cols], house_ref[:, cols], logit,
            taps_ref[:, cols], begin, place, dm_ref[:, cols], kept,
        )
        for slot, item in enumerate((d_q, d_k, d_v, d_h)):
            four_ref[slot, :, cols] = item
        dl_ref[pl.ds(step * heads + head, 1), :] = d_l
        for tap, item in enumerate(d_t):
            dt_ref[tap : tap + 1, cols] = item


def mixer_backward(lengths, me, logit, taps, house, query, key, value, d_mixed, kept, heads=2):
    rows, width = query.shape
    count = width // 128
    half = rows // 2
    wide = pl.BlockSpec((rows, heads * 128), lambda i: (0, i))
    narrow = pl.BlockSpec((taps.shape[0], heads * 128), lambda i: (0, i))
    whole = pl.BlockSpec(logit.shape, lambda i: (0, 0))
    return pl.pallas_call(
        functools.partial(backward_kernel, heads, lengths.shape[1]),
        grid=(count // heads,),
        in_specs=[
            pl.BlockSpec(memory_space=pltpu.SMEM),
            pl.BlockSpec(memory_space=pltpu.SMEM),
            whole, narrow, wide, wide, wide, wide, wide,
            pl.BlockSpec((heads, 8, half, half), lambda i: (i, 0, 0, 0)),
        ],
        out_specs=[pl.BlockSpec((4, rows, heads * 128), lambda i: (0, 0, i)), whole, narrow],
        out_shape=[
            jax.ShapeDtypeStruct((4, rows, width), BF),
            jax.ShapeDtypeStruct(logit.shape, F32),
            jax.ShapeDtypeStruct(taps.shape, F32),
        ],
        compiler_params=pltpu.CompilerParams(vmem_limit_bytes=VMEM),
        cost_estimate=COST,
        name="mixer_backward",
    )(lengths, me, logit, taps, house, query, key, value, d_mixed, kept)


def starts_of(lengths_ref, me, slots):
    starts, sum_so_far = [], 0
    for j in range(slots):
        starts.append(sum_so_far)
        sum_so_far = sum_so_far + lengths_ref[me, j]
    return starts


def begins(starts, row):
    begin = jnp.zeros_like(row)
    for start in starts[1:]:
        begin = jnp.where(row >= start, start, begin)
    return begin


def group_of(sequence, slots):
    return lax.div(sequence, jnp.int32(slots))


def slot_taken(dealing_ref, me, slots, group):
    found = jnp.int32(0)
    for k in range(slots):
        found = jnp.where(group_of(dealing_ref[me * slots + k], slots) == group, k, found)
    return found


def holder_of(dealing_ref, me, slots, count, sequence):
    far, slot = jnp.int32(0), jnp.int32(0)
    for by in (-1, 0, 1):
        for k in range(slots):
            position = (me + by) * slots + k
            inside = (position >= 0) & (position < count)
            hit = inside & (dealing_ref[jnp.clip(position, 0, count - 1)] == sequence)
            far = jnp.where(hit, by, far)
            slot = jnp.where(hit, k, slot)
    return far, slot


def part_kernel(dealing_ref, me_ref, up_in, down_in, up_out, down_out):
    up_out[...] = up_in[0]
    down_out[...] = down_in[0]


def slots_to_send(dealing, me, cotangent):
    slots, span, width = cotangent.shape
    tile = 512
    out = pl.BlockSpec((span, tile), lambda j, dealing, me: (0, j))

    def source(by):
        return pl.BlockSpec(
            (1, span, tile),
            lambda j, dealing, me: (slot_taken(dealing, me[0], slots, me[0] + by), 0, j),
        )

    shape = jax.ShapeDtypeStruct((span, width), BF)
    return pl.pallas_call(
        part_kernel,
        grid_spec=pltpu.PrefetchScalarGridSpec(
            num_scalar_prefetch=2,
            grid=(width // tile,),
            in_specs=[source(1), source(-1)],
            out_specs=[out, out],
        ),
        out_shape=[shape, shape],
        compiler_params=pltpu.CompilerParams(vmem_limit_bytes=VMEM),
        cost_estimate=COST,
        name="slots_to_send",
    )(dealing, me, cotangent, cotangent)


def arrive_kernel(slots, count, lengths_ref, dealing_ref, me_ref, own_ref, low_ref, high_ref, out_ref, turned_ref, picks):
    span = low_ref.shape[0]

    @pl.when(pl.program_id(0) == 0)
    def _():
        me = me_ref[0]
        starts = starts_of(lengths_ref, me, slots)
        row = lax.broadcasted_iota(jnp.int32, (picks.shape[0], 1), 0)
        index = jnp.zeros_like(row)
        for j in range(slots):
            far, slot = holder_of(dealing_ref, me, slots, count, me * slots + j)
            base = jnp.where(far == 0, slot * span, jnp.where(far < 0, slots * span, (slots + 1) * span))
            index = jnp.where(row >= starts[j], base + row - starts[j], index)
        column = lax.broadcasted_iota(jnp.int32, picks.shape, 1)
        picks[...] = jnp.where(column == index, 1.0, 0.0).astype(BF)

    out = (
        dot_nn(picks[:, : slots * span], own_ref[...])
        + dot_nn(picks[:, slots * span : (slots + 1) * span], low_ref[...])
        + dot_nn(picks[:, (slots + 1) * span :], high_ref[...])
    ).astype(BF)
    out_ref[...] = out
    turned_ref[...] = out.T


def cotangent_arrived(lengths, dealing, me, own, low, high, rows):
    span, width = low.shape
    slots = own.shape[0] // span
    tile = 512
    column = lambda n: pl.BlockSpec((n, tile), lambda j, *s: (0, j))
    return pl.pallas_call(
        functools.partial(arrive_kernel, slots, dealing.shape[0]),
        grid_spec=pltpu.PrefetchScalarGridSpec(
            num_scalar_prefetch=3,
            grid=(width // tile,),
            in_specs=[column(own.shape[0]), column(span), column(span)],
            out_specs=[column(rows), pl.BlockSpec((tile, rows), lambda j, *s: (j, 0))],
            scratch_shapes=[pltpu.VMEM((rows, (slots + 2) * span), BF)],
        ),
        out_shape=[
            jax.ShapeDtypeStruct((rows, width), BF),
            jax.ShapeDtypeStruct((width, rows), BF),
        ],
        compiler_params=pltpu.CompilerParams(vmem_limit_bytes=VMEM),
        cost_estimate=COST,
        name="cotangent_arrived",
    )(lengths, dealing, me, own, low, high)


def deal_kernel(slots, count, span, lengths_ref, dealing_ref, me_ref, hidden_ref, part_ref, other_ref, own_ref, up_ref, down_ref, picks):
    @pl.when(pl.program_id(0) == 0)
    def _():
        me = me_ref[0]
        starts = starts_of(lengths_ref, me, slots)

        def zone(chosen):
            start, length = jnp.int32(0), jnp.int32(0)
            for j in range(slots):
                start = jnp.where(chosen[j], starts[j], start)
                length = jnp.where(chosen[j], lengths_ref[me, j], length)
            return start, length

        held = [dealing_ref[me * slots + k] for k in range(slots)]
        far = [holder_of(dealing_ref, me, slots, count, me * slots + j)[0] for j in range(slots)]
        zones = [zone([held[k] == me * slots + j for j in range(slots)]) for k in range(slots)]
        zones.append(zone([far[j] == 1 for j in range(slots)]))
        zones.append(zone([far[j] == -1 for j in range(slots)]))
        row = lax.broadcasted_iota(jnp.int32, (picks.shape[0], 1), 0)
        index = jnp.full_like(row, -1)
        for k, (start, length) in enumerate(zones):
            offset = row - k * span
            index = jnp.where((offset >= 0) & (offset < length), start + offset, index)
        column = lax.broadcasted_iota(jnp.int32, picks.shape, 1)
        picks[...] = jnp.where(column == index, 1.0, 0.0).astype(BF)

    final = hidden_ref[...] + (part_ref[...].astype(F32) + other_ref[...].astype(F32))
    out = dot_nn(picks[...], final.astype(BF)).astype(BF)
    own_ref[...] = out[: slots * span]
    up_ref[...] = out[slots * span : (slots + 1) * span]
    down_ref[...] = out[(slots + 1) * span :]


def rows_dealt(lengths, dealing, me, hidden, part, other, slots, span):
    rows, width = hidden.shape
    tile = 512
    column = lambda n: pl.BlockSpec((n, tile), lambda j, *s: (0, j))
    return pl.pallas_call(
        functools.partial(deal_kernel, slots, dealing.shape[0], span),
        grid_spec=pltpu.PrefetchScalarGridSpec(
            num_scalar_prefetch=3,
            grid=(width // tile,),
            in_specs=[column(rows)] * 3,
            out_specs=[column(slots * span), column(span), column(span)],
            scratch_shapes=[pltpu.VMEM(((slots + 2) * span, rows), BF)],
        ),
        out_shape=[
            jax.ShapeDtypeStruct((slots * span, width), BF),
            jax.ShapeDtypeStruct((span, width), BF),
            jax.ShapeDtypeStruct((span, width), BF),
        ],
        compiler_params=pltpu.CompilerParams(vmem_limit_bytes=VMEM),
        cost_estimate=COST,
        name="rows_dealt",
    )(lengths, dealing, me, hidden, part, other)


def norm_kernel(tokens_ref, gain_ref, normed_ref, turned_ref):
    data = tokens_ref[...].astype(F32)
    inverse = lax.rsqrt(jnp.mean(data * data, axis=1, keepdims=True) + EPSILON)
    normed = (data * inverse * gain_ref[...]).astype(BF)
    normed_ref[...] = normed
    turned_ref[...] = normed.T


def first_norm(tokens, gain, tile=128):
    rows, width = tokens.shape
    flat = pl.BlockSpec((tile, width), lambda i: (i, 0))
    return pl.pallas_call(
        norm_kernel,
        grid=(rows // tile,),
        in_specs=[flat, pl.BlockSpec((1, width), lambda i: (0, 0))],
        out_specs=[flat, pl.BlockSpec((width, tile), lambda i: (0, i))],
        out_shape=[
            jax.ShapeDtypeStruct((rows, width), BF),
            jax.ShapeDtypeStruct((width, rows), BF),
        ],
        compiler_params=pltpu.CompilerParams(vmem_limit_bytes=VMEM),
        cost_estimate=COST,
        name="first_norm",
    )(tokens, gain[None, :])


def hidden_kernel(tokens_ref, part_ref, other_ref, gain_ref, hidden_ref, normed_ref, turned_ref):
    hidden = tokens_ref[...].astype(F32) + (part_ref[...].astype(F32) + other_ref[...].astype(F32))
    inverse = lax.rsqrt(jnp.mean(hidden * hidden, axis=1, keepdims=True) + EPSILON)
    normed = (hidden * inverse * gain_ref[...]).astype(BF)
    hidden_ref[...] = hidden
    normed_ref[...] = normed
    turned_ref[...] = normed.T


def hidden_and_norm(tokens, part, other, gain, tile=128):
    rows, width = tokens.shape
    flat = pl.BlockSpec((tile, width), lambda i: (i, 0))
    return pl.pallas_call(
        hidden_kernel,
        grid=(rows // tile,),
        in_specs=[flat, flat, flat, pl.BlockSpec((1, width), lambda i: (0, 0))],
        out_specs=[flat, flat, pl.BlockSpec((width, tile), lambda i: (0, i))],
        out_shape=[
            jax.ShapeDtypeStruct((rows, width), F32),
            jax.ShapeDtypeStruct((rows, width), BF),
            jax.ShapeDtypeStruct((width, rows), BF),
        ],
        compiler_params=pltpu.CompilerParams(vmem_limit_bytes=VMEM),
        cost_estimate=COST,
        name="hidden_and_norm",
    )(tokens, part, other, gain[None, :])


def norm_back(d_normed, source, gain):
    inverse = lax.rsqrt(jnp.mean(source * source, axis=1, keepdims=True) + EPSILON)
    scaled = d_normed * gain
    back = inverse * scaled - source * (inverse * inverse * inverse) * jnp.mean(
        scaled * source, axis=1, keepdims=True
    )
    return back, jnp.sum(d_normed * source * inverse, axis=0, keepdims=True)


def accumulate(ref, value):
    @pl.when(pl.program_id(0) == 0)
    def _():
        ref[...] = value

    @pl.when(pl.program_id(0) > 0)
    def _():
        ref[...] += value


def branch_kernel(
    part_ref, other_ref, hidden_ref, d_final_ref, gain_ref, out_ref,
    d_hidden_ref, turned_ref, d_mixed_ref, d_gain_ref,
):
    back, d_gain = norm_back(part_ref[...].astype(F32) + other_ref[...].astype(F32), hidden_ref[...], gain_ref[...])
    accumulate(d_gain_ref, d_gain)
    d_hidden = d_final_ref[...].astype(F32) + back
    d_hidden_ref[...] = d_hidden
    d_branch = d_hidden.astype(BF)
    turned_ref[...] = d_branch.T
    d_mixed_ref[...] = dot_nt(d_branch, out_ref[...]).astype(BF)


def branch_back(part, other, hidden, d_final, gain, w_out, tile=128):
    rows, width = hidden.shape
    channels = w_out.shape[0]
    flat = pl.BlockSpec((tile, width), lambda i: (i, 0))
    line = pl.BlockSpec((1, width), lambda i: (0, 0))
    return pl.pallas_call(
        branch_kernel,
        grid=(rows // tile,),
        in_specs=[flat, flat, flat, flat, line, pl.BlockSpec((channels, width), lambda i: (0, 0))],
        out_specs=[
            flat,
            pl.BlockSpec((width, tile), lambda i: (0, i)),
            pl.BlockSpec((tile, channels), lambda i: (i, 0)),
            line,
        ],
        out_shape=[
            jax.ShapeDtypeStruct((rows, width), F32),
            jax.ShapeDtypeStruct((width, rows), BF),
            jax.ShapeDtypeStruct((rows, channels), BF),
            jax.ShapeDtypeStruct((1, width), F32),
        ],
        compiler_params=pltpu.CompilerParams(vmem_limit_bytes=VMEM),
        cost_estimate=COST,
        name="branch_back",
    )(part, other, hidden, d_final, gain[None, :], w_out)


def input_kernel(
    part_ref, other_ref, tokens_ref, d_hidden_ref, gain_ref, taps_ref, ffn_ref, logit_ref, out_ref, small_ref
):
    tokens = tokens_ref[...].astype(F32)
    gain = gain_ref[...]
    taps, heads = taps_ref.shape[0], logit_ref.shape[0]
    back, d_gain = norm_back(part_ref[...].astype(F32) + other_ref[...].astype(F32), tokens, gain)
    out_ref[...] = (d_hidden_ref[...] + back).astype(BF)
    inverse = lax.rsqrt(jnp.mean(tokens * tokens, axis=1, keepdims=True) + EPSILON)
    d_beta = dot_nn(logit_ref[...].astype(BF), (tokens * inverse * gain).astype(BF))

    @pl.when(pl.program_id(0) == 0)
    def _():
        small_ref[...] = jnp.zeros_like(small_ref)
        small_ref[0:taps, 0 : taps_ref.shape[1]] = taps_ref[...]
        small_ref[taps : taps + 1, :] = ffn_ref[...]

    small_ref[taps + 1 : taps + 2, :] += d_gain
    small_ref[taps + 2 : taps + 2 + heads, :] += d_beta


def input_back(part, other, tokens, d_hidden, gain, g_taps, g_ffn_gain, d_logit, tile=128):
    rows, width = tokens.shape
    flat = pl.BlockSpec((tile, width), lambda i: (i, 0))
    line = pl.BlockSpec((1, width), lambda i: (0, 0))
    height = -(-(g_taps.shape[0] + 2 + d_logit.shape[0]) // 8) * 8
    return pl.pallas_call(
        input_kernel,
        grid=(rows // tile,),
        in_specs=[flat, flat, flat, flat, line]
        + [
            pl.BlockSpec(g_taps.shape, lambda i: (0, 0)),
            line,
            pl.BlockSpec((d_logit.shape[0], tile), lambda i: (0, i)),
        ],
        out_specs=[flat, pl.BlockSpec((height, width), lambda i: (0, 0))],
        out_shape=[
            jax.ShapeDtypeStruct((rows, width), BF),
            jax.ShapeDtypeStruct((height, width), F32),
        ],
        compiler_params=pltpu.CompilerParams(vmem_limit_bytes=VMEM),
        cost_estimate=COST,
        name="input_back",
    )(part, other, tokens, d_hidden, gain[None, :], g_taps, g_ffn_gain, d_logit)


def product_kernel(count, turned, small, *refs):
    lefts, weights, out_ref = refs[:count], refs[count : 2 * count], refs[-1]
    dot = dot_nt if turned else dot_nn
    out = dot(lefts[0][...], weights[0][...])
    for left, weight in zip(lefts[1:], weights[1:]):
        out = out + dot(left[...], weight[...])
    if small:
        out = out + lax.dot_general(
            refs[2 * count][...].astype(BF), refs[2 * count + 1][...], (((0,), (1,)), ((), ())),
            preferred_element_type=F32,
        )
    out_ref[...] = out.astype(out_ref.dtype)


def product(lefts, weights, turned, dtype=F32, small=(), tile=512):
    width = weights[0].shape[0 if turned else 1]
    whole = lambda x: pl.BlockSpec(x.shape, lambda j: (0, 0))
    left_specs, arrays = [], []
    for left in lefts:
        if isinstance(left, tuple):
            array, index = left
            rows = array.shape[1]
            left_specs.append(
                pl.BlockSpec((None,) + array.shape[1:], lambda j, index=index: (index, 0, 0))
            )
            arrays.append(array)
        else:
            rows = left.shape[0]
            left_specs.append(whole(left))
            arrays.append(left)
    if turned:
        parts = [pl.BlockSpec((tile, w.shape[1]), lambda j: (j, 0)) for w in weights]
    else:
        parts = [pl.BlockSpec((w.shape[0], tile), lambda j: (0, j)) for w in weights]
    more = [whole(small[0]), pl.BlockSpec((tile, small[1].shape[1]), lambda j: (j, 0))] if small else []
    return pl.pallas_call(
        functools.partial(product_kernel, len(lefts), turned, bool(small)),
        grid=(width // tile,),
        in_specs=left_specs + parts + more,
        out_specs=pl.BlockSpec((rows, tile), lambda j: (0, j)),
        out_shape=jax.ShapeDtypeStruct((rows, width), dtype),
        compiler_params=pltpu.CompilerParams(vmem_limit_bytes=VMEM),
        cost_estimate=COST,
        name="product",
    )(*arrays, *weights, *small)


def fold_kernel(plan, cuts, *refs):
    count = 1 if cuts is None else sum(cuts)
    ins, outs = refs[:-count], refs[-count:]
    start, first = 0, 0
    for index, (width, terms) in enumerate(plan):
        part = None
        for ref, column in terms:
            term = ins[ref][:, column : column + width].astype(F32)
            part = term if part is None else part + term
        if cuts is None:
            outs[0][:, start : start + width] = part.astype(outs[0].dtype)
            start += width
        else:
            piece = width // cuts[index]
            for i in range(cuts[index]):
                outs[first + i][...] = part[:, i * piece : (i + 1) * piece]
            first += cuts[index]


def fold(streams, height, cuts=None):
    step = height
    while step % 2 == 0 and step > 96 and (step // 2) % 8 == 0:
        step //= 2
    arrays, plan = [], []
    for width, terms in streams:
        places = []
        for array, row, column in terms:
            known = [i for i, (a, r) in enumerate(arrays) if a is array and r == row]
            if not known:
                arrays.append((array, row))
            places.append((known[0] if known else len(arrays) - 1, column))
        plan.append((width, places))
    if cuts is None:
        widths, kind = [sum(width for width, _ in streams)], BF
    else:
        widths = [w // n for (w, _), n in zip(streams, cuts) for _ in range(n)]
        kind = F32
    return pl.pallas_call(
        functools.partial(fold_kernel, plan, cuts),
        grid=(height // step,),
        in_specs=[
            pl.BlockSpec((step, array.shape[1]), lambda i, r=row // step: (r + i, 0))
            for array, row in arrays
        ],
        out_specs=[pl.BlockSpec((step, width), lambda i: (i, 0)) for width in widths],
        out_shape=[jax.ShapeDtypeStruct((height, width), kind) for width in widths],
        compiler_params=pltpu.CompilerParams(vmem_limit_bytes=VMEM),
        cost_estimate=COST,
        name="fold",
    )(*[array for array, _ in arrays])


def added_kernel(a_ref, b_ref, out_ref):
    out_ref[...] = a_ref[...] + b_ref[...]


def added(a, b):
    return pl.pallas_call(
        added_kernel,
        out_shape=jax.ShapeDtypeStruct(a.shape, a.dtype),
        compiler_params=pltpu.CompilerParams(vmem_limit_bytes=VMEM),
        cost_estimate=COST,
        name="added",
    )(a, b)


def wgrad_kernel(plan, order_ref, *refs):
    lefts, rights = refs[: len(refs) - 2 - len(plan)], refs[len(refs) - 2 - len(plan) : -2]
    out_ref, packed = refs[-2:]
    block = lefts[0].shape[1]
    count = packed.shape[1] // block
    step = pl.program_id(0)

    @pl.when(step == 0)
    def _():
        for part, left_ref in enumerate(lefts):
            for i in range(count):
                packed[part, i * block : (i + 1) * block, :] = left_ref[order_ref[i]]

    for (part, first, steps), right_ref in zip(plan, rights):

        @pl.when((step >= first) & (step < first + steps))
        def _(right_ref=right_ref, part=part):
            out_ref[...] = dot_nn(packed[part], right_ref[...]).astype(out_ref.dtype)


def wgrad(order, parts, tile=512):
    count = order.shape[0]
    lefts = [left for left, _ in parts]
    rights = [right for _, several in parts for right in several]
    block, tokens = lefts[0].shape[1:]
    tile = next(t for t in (tile, 384, 256, 128) if all(r.shape[1] % t == 0 for r in rights))
    plan, first = [], 0
    for part, (_, several) in enumerate(parts):
        for right in several:
            plan.append((part, first, right.shape[1] // tile))
            first += right.shape[1] // tile
    return pl.pallas_call(
        functools.partial(wgrad_kernel, plan),
        grid_spec=pltpu.PrefetchScalarGridSpec(
            num_scalar_prefetch=1,
            grid=(first,),
            in_specs=[pl.BlockSpec(left.shape, lambda j, order: (0, 0, 0)) for left in lefts]
            + [
                pl.BlockSpec(
                    (tokens, tile), lambda j, order, s=s, n=n: (0, jnp.clip(j - s, 0, n - 1))
                )
                for _, s, n in plan
            ],
            out_specs=pl.BlockSpec((count * block, tile), lambda j, order: (0, j)),
            scratch_shapes=[pltpu.VMEM((len(lefts), count * block, tokens), BF)],
        ),
        out_shape=jax.ShapeDtypeStruct((count * block, first * tile), BF),
        compiler_params=pltpu.CompilerParams(vmem_limit_bytes=VMEM),
        cost_estimate=COST,
        name="wgrad",
    )(order, *lefts, *rights)


def plane_kernel(order_ref, left_ref, right_ref, out_ref):
    total = dot_nn(left_ref[0], right_ref[0])
    for i in range(1, left_ref.shape[0]):
        total = total + dot_nn(left_ref[i], right_ref[i])
    out_ref[...] = total.astype(out_ref.dtype)


def wgrad_plane(order, left, right, blocks):
    parts, width, tokens = left.shape
    columns = right.shape[2]
    height = width // blocks
    return pl.pallas_call(
        plane_kernel,
        grid_spec=pltpu.PrefetchScalarGridSpec(
            num_scalar_prefetch=1,
            grid=(order.shape[0],),
            in_specs=[
                pl.BlockSpec((parts, height, tokens), lambda j, order: (0, order[j], 0)),
                pl.BlockSpec(right.shape, lambda j, order: (0, 0, 0)),
            ],
            out_specs=pl.BlockSpec((height, columns), lambda j, order: (j, 0)),
        ),
        out_shape=jax.ShapeDtypeStruct((order.shape[0] * height, columns), BF),
        compiler_params=pltpu.CompilerParams(vmem_limit_bytes=VMEM),
        cost_estimate=COST,
        name="wgrad_plane",
    )(order, left, right)


def ffn_kernel(normed_ref, d_final_ref, gate_ref, up_ref, down_ref, inner_ref, d_gate_ref, d_up_ref):
    gate = dot_nn(normed_ref[...], gate_ref[...])
    lift = dot_nn(normed_ref[...], up_ref[...])
    d_inner = dot_nt(d_final_ref[...], down_ref[...])
    sig = jax.nn.sigmoid(gate)
    silu = gate * sig
    inner_ref[...] = (silu * lift).astype(BF)
    d_gate_ref[...] = (d_inner * lift * sig * (1.0 + gate * (1.0 - sig))).astype(BF)
    d_up_ref[...] = (d_inner * silu).astype(BF)


def ffn(normed, d_final, w_gate, w_up, w_down, tile=256):
    rows, width = normed.shape
    hidden = w_gate.shape[1]
    whole = pl.BlockSpec((rows, width), lambda j: (0, 0))
    column = pl.BlockSpec((width, tile), lambda j: (0, j))
    out = pl.BlockSpec((rows, tile), lambda j: (0, j))
    shape = jax.ShapeDtypeStruct((rows, hidden), BF)
    return pl.pallas_call(
        ffn_kernel,
        grid=(hidden // tile,),
        in_specs=[whole, whole, column, column, pl.BlockSpec((tile, width), lambda j: (j, 0))],
        out_specs=[out, out, out],
        out_shape=[shape, shape, shape],
        compiler_params=pltpu.CompilerParams(vmem_limit_bytes=VMEM),
        cost_estimate=COST,
        name="ffn",
    )(normed, d_final, w_gate, w_up, w_down)


def swap(x, axis, bit):
    size = lax.axis_size(axis)
    return lax.ppermute(x, axis, [(i, i ^ (1 << bit)) for i in range(size)])


def flips_of(count, bits):
    flips = []
    for position in reversed(range(count)):
        flips.append(
            sum(((position >> (len(bits) - 1 - rank)) & 1) << bit for rank, bit in enumerate(bits))
        )
    return jnp.array(flips, jnp.int32)


def halve(terms, bits):
    for bit in bits:
        half = terms[0].shape[0] // 2
        out = sum(t[:half].astype(F32) for t in terms).astype(BF)
        terms = [t[half:] for t in terms] + [swap(out, "dp", bit)]
    return terms


def total(terms):
    return sum(t.astype(F32) for t in terms)


def after(value, *others):
    return lax.optimization_barrier((value,) + others)[0]


class Order:
    def __init__(self):
        self.last = ()

    def gate(self, *values):
        if self.last:
            values = lax.optimization_barrier(tuple(values) + self.last)[: len(values)]
        return values if len(values) > 1 else values[0]

    def mark(self, *values):
        self.last = values
        return values if len(values) > 1 else values[0]


def stream(*arrays):
    return arrays[0].shape[1], [(array, 0, 0) for array in arrays]


def joined(streams, got):
    column, out = 0, []
    for width, terms in streams:
        out.append((width, terms + [(got, 0, column)]))
        column += width
    return out


def on_device(
    tokens,
    cotangent,
    lengths,
    dealing,
    attn_gain,
    w_query,
    w_key,
    w_value,
    w_house,
    w_beta,
    conv_taps,
    w_out,
    ffn_gain,
    w_gate,
    w_up,
    w_down,
):
    rows, width = tokens.shape
    slots, span = cotangent.shape[:2]
    size = lax.axis_size("dp")
    me = lax.axis_index("dp").astype(jnp.int32)
    me1 = me.reshape(1)
    block = width // size
    bits = list(range(size.bit_length() - 1))
    plane, line = bits[:2], bits[2:]
    up = [(i, i + 1) for i in range(size - 1)]
    down = [(i + 1, i) for i in range(size - 1)]
    first = size // 2
    groups = [[i + j for j in range(4)] for i in range(0, size, 4)]
    order_line = (me >> 2) ^ flips_of(size // 4, [b - 2 for b in line])
    order_plane = (jnp.arange(4, dtype=jnp.int32)[:, None] + 4 * order_line[None, :]).reshape(-1)
    order_zxy = me ^ flips_of(size, line + plane)
    order_xyz = me ^ flips_of(size, bits)
    order = Order()

    def sharded(turned):
        return turned.reshape(size, block, turned.shape[1])

    cot_up, cot_down = order.mark(*slots_to_send(dealing, me1, cotangent))
    cot_low = lax.ppermute(cot_up, "dp", up)
    cot_high = lax.ppermute(cot_down, "dp", down)

    normed1, normed1_t = order.mark(*first_norm(order.gate(tokens), attn_gain))
    plane_normed = lax.all_gather(normed1_t, "dp", axis_index_groups=groups)
    normed = order.gate(normed1)
    logit = lax.dot_general(
        w_beta, normed, (((0,), (1,)), ((), ())), preferred_element_type=F32
    )
    query = dot_nn(normed, w_query).astype(BF)
    key = dot_nn(normed, w_key).astype(BF)
    value = dot_nn(normed, w_value).astype(BF)
    house = dot_nn(normed, w_house)
    order.mark(query, key, value, house, logit)
    mixed, kept = order.mark(
        *mixer_forward(lengths, me1, logit, conv_taps, house, order.gate(query), key, value)
    )
    cot_low, cot_high = order.mark(*order.gate(cot_low, cot_high))
    attn_part = order.mark(product([order.gate(mixed)], [w_out], False, BF))
    attn_other = swap(attn_part, "tensor", 0)
    cot_low = order.gate(cot_low)
    d_final, d_final_t = order.mark(
        *cotangent_arrived(lengths, dealing, me1, cotangent.reshape(-1, width), cot_low, cot_high, rows)
    )
    hidden, normed2, normed2_t = order.mark(
        *hidden_and_norm(tokens, attn_part, order.gate(attn_other), ffn_gain)
    )
    inner, d_gate, d_up = order.mark(*ffn(order.gate(normed2), d_final, w_gate, w_up, w_down))

    def gated(streams):
        arrays = []
        for _, terms in streams:
            for array, _, _ in terms:
                if not any(array is known for known in arrays):
                    arrays.append(array)
        after = order.gate(*arrays)
        after = list(after) if isinstance(after, tuple) else [after]
        return [
            (w, [(next(n for a, n in zip(arrays, after) if a is array), r, c) for array, r, c in terms])
            for w, terms in streams
        ]

    def leave(streams, height, bit):
        streams = gated(streams)
        got = swap(order.mark(fold(streams, height)[0]), "dp", bit)
        return joined([(w, [(a, r + height, c) for a, r, c in terms]) for w, terms in streams], got)

    def finish(streams, cuts):
        out = fold(gated(streams), block, cuts)
        order.mark(out[0])
        return out

    def wgrad_of(rows_order, *parts):
        left, rights = parts[0]
        parts = [(left, [order.gate(rights[0])] + list(rights[1:]))] + list(parts[1:])
        return order.mark(wgrad(rows_order, parts))

    quarter = width // 4
    columns = query.shape[1]
    heights = [quarter >> (i + 1) for i in range(len(line))]
    d_final_s = sharded(d_final_t)

    ffn_all = wgrad_of(order_plane, (sharded(normed2_t), [d_gate, d_up]))
    ffn_sum = lax.psum_scatter(
        ffn_all, "dp", scatter_dimension=0, tiled=True, axis_index_groups=groups
    )
    down_leave = wgrad_of(order_zxy[:first], (d_final_s, [inner]))
    down_got = swap(down_leave, "dp", line[0])
    d_norm2_part = order.mark(product([order.gate(d_gate), d_up], [w_gate, w_up], True, BF))
    d_norm2_other = swap(d_norm2_part, "tensor", 0)
    down_stay = wgrad_of(order_zxy[first:], (d_final_s, [inner]))
    downs = [stream(down_stay, down_got)]
    d_hidden, d_branch_t, d_mixed, g_ffn_gain = order.mark(
        *branch_back(d_norm2_part, order.gate(d_norm2_other), hidden, d_final, ffn_gain, w_out)
    )
    branch = sharded(d_branch_t)

    out_leave = wgrad_of(order_xyz[:first], (branch, [mixed]))
    out_got = swap(out_leave, "dp", 0)

    d_four, d_logit, g_taps = order.mark(
        *mixer_backward(
            lengths, me1, logit, conv_taps, house, query, key, value, order.gate(d_mixed), kept
        )
    )
    plane_four = lax.all_to_all(d_four, "dp", 0, 0, axis_index_groups=groups)
    out_stay = wgrad_of(order_xyz[first:], (branch, [mixed]))
    height = width // 2
    for bit in line[1:]:
        height //= 2
        downs = leave(downs, height, bit)
    down_part = order.mark(product([order.gate(inner)], [w_down], False, BF))
    down_other = swap(down_part, "tensor", 0)
    outs = leave([stream(out_stay, out_got)], quarter, 1)
    d_norm1_part = order.mark(
        product(
            [(order.gate(d_four), i) for i in range(4)],
            [w_query, w_key, w_value, w_house], True, BF, small=(d_logit, w_beta),
        )
    )
    d_norm1_other = swap(d_norm1_part, "tensor", 0)
    dealt, deal_up, deal_down = order.mark(
        *rows_dealt(lengths, dealing, me1, hidden, *order.gate(down_part, down_other), slots, span)
    )
    input_grad, small = order.mark(
        *input_back(
            d_norm1_part, order.gate(d_norm1_other), tokens, d_hidden, attn_gain, g_taps, g_ffn_gain, d_logit
        )
    )
    lines = size // 4
    attn_leave = order.mark(
        wgrad_plane(order_line[: lines // 2], plane_normed, order.gate(plane_four), lines)
    )
    attn_got = swap(attn_leave, "dp", line[0])
    attn_stay = order.mark(
        wgrad_plane(order_line[lines // 2 :], plane_normed, order.gate(plane_four), lines)
    )
    ffns = leave([stream(ffn_sum)] + outs, heights[0], line[0])
    height //= 2
    downs = leave(downs, height, 0)
    out_low = lax.ppermute(deal_up, "dp", up)
    out_high = lax.ppermute(deal_down, "dp", down)
    attns = [stream(attn_stay, attn_got)]
    attn_height = width // 2
    for bit in line[1:]:
        attn_height //= 2
        attns = leave(attns, attn_height, bit)
    height //= 2
    downs = leave(downs, height, 1)
    for height, bit in zip(heights[1:], line[1:]):
        ffns = leave(ffns, height, bit)
    small_got = None

    def small_step(bit):
        nonlocal small, small_got
        if small_got is not None:
            small = order.mark(added(small, order.gate(small_got)))
        small_got = None if bit is None else swap(small, "dp", bit)

    small_bits = list(bits)
    small_step(small_bits.pop(0))
    attn_sum = order.mark(fold(gated(attns), width // lines)[0])
    plane_rows = lax.all_to_all(
        attn_sum.reshape(4, block, columns), "dp", 0, 0, axis_index_groups=groups
    )
    out_low, out_high = order.mark(*order.gate(out_low, out_high))
    small_step(small_bits.pop(0))
    (g_down,) = finish(downs, [1])
    while small_bits:
        small_step(small_bits.pop(0))
    small_step(None)
    g_gate, g_up, g_out = finish(ffns, [2, 1])
    g_query, g_key, g_value, g_house = order.gate(plane_rows).astype(F32)

    taps = conv_taps.shape[0]
    per_row = lax.dynamic_slice_in_dim(small[taps:], me * block, block, axis=1)
    taps_total = small[:taps, :columns]
    held_from = lax.dynamic_slice_in_dim(dealing, me * slots, slots) // slots - me
    output = jnp.where(
        (held_from == -1)[:, None, None],
        out_low[None],
        jnp.where(
            (held_from == 1)[:, None, None], out_high[None], dealt.reshape(slots, span, width)
        ),
    )
    return (
        output,
        input_grad,
        per_row[1],
        g_query,
        g_key,
        g_value,
        g_house,
        per_row[2 : 2 + d_logit.shape[0]].T,
        taps_total,
        g_out.T,
        per_row[0],
        g_gate,
        g_up,
        g_down.T,
    )


def solution(mesh):
    in_specs = (
        P("dp", None),
        P("dp", None, None),
        P(),
        P(),
        P(),
        P(None, "tensor"),
        P(None, "tensor"),
        P(None, "tensor"),
        P(None, "tensor"),
        P(None, "tensor"),
        P(None, "tensor"),
        P("tensor", None),
        P(),
        P(None, "tensor"),
        P(None, "tensor"),
        P("tensor", None),
    )
    out_specs = (
        P("dp", None, None),
        P("dp", None),
        P("dp"),
        P("dp", "tensor"),
        P("dp", "tensor"),
        P("dp", "tensor"),
        P("dp", "tensor"),
        P("dp", "tensor"),
        P(None, "tensor"),
        P("tensor", "dp"),
        P("dp"),
        P("dp", "tensor"),
        P("dp", "tensor"),
        P("tensor", "dp"),
    )
    return jax.shard_map(
        on_device, mesh=mesh, in_specs=in_specs, out_specs=out_specs, check_vma=False
    )
```

```python
import functools
import jax
import jax.numpy as jnp
from jax import lax
from jax.experimental import pallas as pl
from jax.experimental.pallas import tpu as pltpu
from jax.sharding import PartitionSpec as P

EPSILON = 1e-06
BF = jnp.bfloat16
F32 = jnp.float32

VMEM = 60 << 20
COST = pl.CostEstimate(flops=0, bytes_accessed=0, transcendentals=0)
MORE = pl.CostEstimate(flops=1_000_000_000, bytes_accessed=1_000_000, transcendentals=0)


def dot_nn(a, b):
    return lax.dot_general(a, b, (((1,), (0,)), ((), ())), preferred_element_type=F32)


def dot_nt(a, b):
    return lax.dot_general(a, b, (((1,), (1,)), ((), ())), preferred_element_type=F32)


def dot_tn(a, b):
    return lax.dot_general(a, b, (((0,), (0,)), ((), ())), preferred_element_type=F32)


def halves(x):
    high = x.astype(BF)
    return high, (x - high.astype(F32)).astype(BF)


def split_product(a, b):
    return dot_nn(a[0], b[0]) + (dot_nn(a[0], b[1]) + dot_nn(a[1], b[0]))


def unit_lower_inverses(stricts, base):
    size, lanes = stricts[0].shape[0], 128
    tiles, per_tile = size // lanes, lanes // base
    lane = lax.broadcasted_iota(jnp.int32, (base, lanes), 1)
    row = lax.broadcasted_iota(jnp.int32, (base, lanes), 0)
    owner, within = lane // base, lane % base
    pieces = [
        strict[t * lanes : (t + 1) * lanes, t * lanes : (t + 1) * lanes]
        for strict in stricts
        for t in range(tiles)
    ]
    compact = []
    for piece in pieces:
        packed = jnp.zeros((base, lanes), F32)
        for block in range(per_tile):
            packed = jnp.where(owner == block, piece[block * base : (block + 1) * base], packed)
        compact.append(packed)
    solved = [jnp.where(row == within, 1.0, 0.0).astype(F32)] * len(pieces)
    for step in range(base - 1):
        index = owner * base + step
        solved = [
            s - jnp.take_along_axis(c, index, axis=1) * s[step : step + 1, :]
            for s, c in zip(solved, compact)
        ]
    inverses = [
        jnp.concatenate([jnp.where(owner == b, s, 0.0) for b in range(per_tile)], axis=0)
        for s in solved
    ]
    grown = base * 2
    row = lax.broadcasted_iota(jnp.int32, (lanes, lanes), 0)
    col = lax.broadcasted_iota(jnp.int32, (lanes, lanes), 1)
    while grown <= lanes:
        joined = (row // grown == col // grown) & (row // (grown // 2) != col // (grown // 2))
        parts = [halves(i) for i in inverses]
        crosses = [halves(jnp.where(joined, p, 0.0)) for p in pieces]
        firsts = [halves(split_product(p, c)) for p, c in zip(parts, crosses)]
        inverses = [i - split_product(f, p) for i, f, p in zip(inverses, firsts, parts)]
        grown *= 2
    whole = []
    parts = [halves(i) for i in inverses]
    corners = [halves(strict[lanes:, :lanes]) for strict in stricts]
    firsts = [halves(split_product(parts[2 * n + 1], c)) for n, c in enumerate(corners)]
    for n, first in enumerate(firsts):
        corner = -split_product(first, parts[2 * n])
        top = jnp.concatenate([inverses[2 * n], jnp.zeros((lanes, lanes), F32)], axis=1)
        whole.append(
            jnp.concatenate([top, jnp.concatenate([corner, inverses[2 * n + 1]], axis=1)], axis=0)
        )
    return whole


def shifted_rows(x, amount, place):
    return jnp.where(place >= amount, pltpu.roll(x, amount, 0), 0.0)


def direction(house, taps, place):
    conv = taps[0:1, :] * house
    for shift in range(1, taps.shape[0]):
        conv = conv + taps[shift : shift + 1, :] * shifted_rows(house, shift, place)
    inverse = lax.rsqrt(jnp.sum(conv * conv, axis=1, keepdims=True) + EPSILON)
    return conv, inverse


PAIRS = ((0, 0), (1, 0), (1, 1))


def masks_of(begin, half, a, b):
    inside = lax.broadcasted_iota(jnp.int32, (half, half), 1) + b * half >= begin[
        a * half : (a + 1) * half
    ]
    if a != b:
        return inside, inside
    col = lax.broadcasted_iota(jnp.int32, (half, half), 1)
    row = lax.broadcasted_iota(jnp.int32, (half, half), 0)
    return inside & (col <= row), inside & (col < row)


def scores_of(query, key, house_dir, begin, half, a, b):
    rows, cols = slice(a * half, (a + 1) * half), slice(b * half, (b + 1) * half)
    left = jnp.concatenate([query[rows], house_dir[rows]], axis=0)
    right = jnp.concatenate([key[cols], house_dir[cols]], axis=0)
    every = dot_nt(left, right)
    col = lax.broadcasted_iota(jnp.int32, (half, half), 1) + b * half
    row = lax.broadcasted_iota(jnp.int32, (half, half), 0) + a * half
    inside = col >= begin[rows]
    upto = inside & (col <= row)
    before = inside & (col < row)
    return (
        every[:half, :half],
        jnp.where(upto, every[:half, half:], 0.0),
        jnp.where(before, every[half:, :half], 0.0),
        jnp.where(before, every[half:, half:], 0.0),
        upto,
        before,
    )


def forward_heads(items, begin, place):
    half = items[0][0].shape[0] // 2
    scaling = items[0][0].shape[1] ** (-0.5)
    both = (slice(0, half), slice(half, 2 * half))
    upto, before = {}, {}
    for a, b in PAIRS:
        upto[a, b], before[a, b] = masks_of(begin, half, a, b)
    heads = []
    for query, key, value, house, logit, taps in items:
        conv, inverse = direction(house, taps, place)
        house_dir = (conv * inverse).astype(BF)
        beta = 2.0 * jax.nn.sigmoid(logit)
        cross, know, gram = {}, {}, {}
        for a, b in PAIRS:
            left = jnp.concatenate([query[both[a]], house_dir[both[a]]], axis=0)
            every = dot_nt(left, house_dir[both[b]])
            beta_cols = beta[:, both[b]]
            cross[a, b] = jnp.where(upto[a, b], every[:half] * -beta_cols, 0.0).astype(BF)
            gram[a, b] = jnp.where(before[a, b], every[half:] * beta_cols, 0.0)
            know[a, b] = jnp.where(
                before[a, b], dot_nt(house_dir[both[a]], key[both[b]]), 0.0
            )
        heads.append((cross, know, gram, query, key.T, value))
    inverses = unit_lower_inverses([h[2][a, a] for h in heads for a in (0, 1)], 16)
    eye = (
        lax.broadcasted_iota(jnp.int32, (half, half), 0)
        == lax.broadcasted_iota(jnp.int32, (half, half), 1)
    )
    tails = [jnp.where(eye, 0.0, i).astype(BF) for i in inverses]
    results = []
    for n, (cross, know, gram, query, key_t, value) in enumerate(heads):
        tail0, tail1 = tails[2 * n : 2 * n + 2]
        z00 = (know[0, 0] + dot_nn(tail0, know[0, 0].astype(BF))).astype(BF)
        z11 = (know[1, 1] + dot_nn(tail1, know[1, 1].astype(BF))).astype(BF)
        rest = know[1, 0] - dot_nn(gram[1, 0].astype(BF), z00)
        z10 = (rest + dot_nn(tail1, rest.astype(BF))).astype(BF)

        def score(pair, lefts, rights):
            out = dot_nn(jnp.concatenate(lefts, axis=1), jnp.concatenate(rights, axis=0))
            return jnp.where(upto[pair], out * scaling, -1e30)

        q0, q1 = query[both[0]], query[both[1]]
        s00 = score((0, 0), [q0, cross[0, 0]], [key_t[:, both[0]], z00])
        s10 = score((1, 0), [q1, cross[1, 0], cross[1, 1]], [key_t[:, both[0]], z00, z10])
        s11 = score((1, 1), [q1, cross[1, 1]], [key_t[:, both[1]], z11])
        top0 = jnp.max(s00, axis=1, keepdims=True)
        top1 = jnp.maximum(
            jnp.max(s10, axis=1, keepdims=True), jnp.max(s11, axis=1, keepdims=True)
        )
        e00, e10, e11 = jnp.exp(s00 - top0), jnp.exp(s10 - top1), jnp.exp(s11 - top1)
        inv0 = 1.0 / jnp.sum(e00, axis=1, keepdims=True)
        inv1 = 1.0 / (jnp.sum(e10, axis=1, keepdims=True) + jnp.sum(e11, axis=1, keepdims=True))
        p00, p10, p11 = (e00 * inv0).astype(BF), (e10 * inv1).astype(BF), (e11 * inv1).astype(BF)
        mixed0 = dot_nn(p00, value[both[0]])
        mixed1 = dot_nn(jnp.concatenate([p10, p11], axis=1), value)
        mixed = jnp.concatenate([mixed0, mixed1], axis=0).astype(BF)
        results.append((mixed, (p00, p10, p11, z00, z10, z11, tail0, tail1)))
    return results


def forward_kernel(heads, slots, lengths_ref, me_ref, logit_ref, taps_ref, house_ref, q_ref, k_ref, v_ref, mixed_ref, kept_ref):
    step = pl.program_id(0)
    rows = q_ref.shape[0]
    row = lax.broadcasted_iota(jnp.int32, (rows, 1), 0)
    begin = begins(starts_of(lengths_ref, me_ref[0], slots), row)
    place = row - begin
    columns = [slice(head * 128, (head + 1) * 128) for head in range(heads)]
    items = [
        (
            q_ref[:, cols], k_ref[:, cols], v_ref[:, cols], house_ref[:, cols],
            logit_ref[pl.ds(step * heads + head, 1), :], taps_ref[:, cols],
        )
        for head, cols in enumerate(columns)
    ]
    for head, (mixed, kept) in enumerate(forward_heads(items, begin, place)):
        mixed_ref[:, columns[head]] = mixed
        for slot, item in enumerate(kept):
            kept_ref[head, slot] = item


def mixer_forward(lengths, me, logit, taps, house, query, key, value, heads=2):
    rows, width = query.shape
    count = width // 128
    half = rows // 2
    wide = pl.BlockSpec((rows, heads * 128), lambda i: (0, i))
    return pl.pallas_call(
        functools.partial(forward_kernel, heads, lengths.shape[1]),
        grid=(count // heads,),
        in_specs=[
            pl.BlockSpec(memory_space=pltpu.SMEM),
            pl.BlockSpec(memory_space=pltpu.SMEM),
            pl.BlockSpec(logit.shape, lambda i: (0, 0)),
            pl.BlockSpec((taps.shape[0], heads * 128), lambda i: (0, i)),
            wide, wide, wide, wide,
        ],
        out_specs=[wide, pl.BlockSpec((heads, 8, half, half), lambda i: (i, 0, 0, 0))],
        out_shape=[
            jax.ShapeDtypeStruct((rows, width), BF),
            jax.ShapeDtypeStruct((count, 8, half, half), BF),
        ],
        compiler_params=pltpu.CompilerParams(vmem_limit_bytes=VMEM),
        cost_estimate=COST,
        name="mixer_forward",
    )(lengths, me, logit, taps, house, query, key, value)


def backward_head(query, key, value, house, logit, taps, begin, place, d_mixed, kept):
    p00, p10, p11, z00, z10, z11, tail0, tail1 = kept
    rows = query.shape[0]
    half = rows // 2
    scaling = query.shape[1] ** (-0.5)
    conv, inverse = direction(house, taps, place)
    direct = conv * inverse
    house_dir = direct.astype(BF)
    beta = 2.0 * jax.nn.sigmoid(logit)
    cross, cross_b, gram, gram_raw, upto, before, beta_cols = {}, {}, {}, {}, {}, {}, {}
    for a, b in PAIRS:
        _, cross[a, b], _, gram_raw[a, b], upto[a, b], before[a, b] = scores_of(
            query, key, house_dir, begin, half, a, b
        )
        beta_cols[b] = beta[:, b * half : (b + 1) * half]
        cross_b[a, b] = (cross[a, b] * beta_cols[b]).astype(BF)
    gram10 = (gram_raw[1, 0] * beta_cols[0]).astype(BF)
    d0, d1 = d_mixed[:half], d_mixed[half:]
    v0, v1 = value[:half], value[half:]
    dp00, dp10, dp11 = dot_nt(d0, v0), dot_nt(d1, v0), dot_nt(d1, v1)
    dv0 = dot_tn(p00, d0) + dot_tn(p10, d1)
    dv1 = dot_tn(p11, d1)
    f00, f10, f11 = p00.astype(F32), p10.astype(F32), p11.astype(F32)
    mean0 = jnp.sum(f00 * dp00, axis=1, keepdims=True)
    mean1 = jnp.sum(f10 * dp10, axis=1, keepdims=True) + jnp.sum(f11 * dp11, axis=1, keepdims=True)
    ds = {
        (0, 0): (f00 * (dp00 - mean0) * scaling).astype(BF),
        (1, 0): (f10 * (dp10 - mean1) * scaling).astype(BF),
        (1, 1): (f11 * (dp11 - mean1) * scaling).astype(BF),
    }
    dx = {
        (0, 0): dot_nt(ds[0, 0], z00),
        (1, 0): dot_nt(ds[1, 0], z00),
        (1, 1): dot_nt(ds[1, 1], z11) + dot_nt(ds[1, 0], z10),
    }
    dz00 = dot_tn(cross_b[0, 0], ds[0, 0]) + dot_tn(cross_b[1, 0], ds[1, 0])
    dz10 = dot_tn(cross_b[1, 1], ds[1, 0])
    dz11 = dot_tn(cross_b[1, 1], ds[1, 1])
    e11 = dz11 + dot_tn(tail1, dz11.astype(BF))
    e10 = dz10 + dot_tn(tail1, dz10.astype(BF))
    rest = dz00 - dot_tn(gram10, e10.astype(BF))
    e00 = rest + dot_tn(tail0, rest.astype(BF))
    e00b, e10b, e11b = e00.astype(BF), e10.astype(BF), e11.astype(BF)
    dn = {
        (0, 0): dot_nt(e00b, z00),
        (1, 0): dot_nt(e10b, z00),
        (1, 1): dot_nt(e10b, z10) + dot_nt(e11b, z11),
    }
    dy = {(0, 0): e00, (1, 0): e10, (1, 1): e11}
    d_beta = [jnp.zeros((1, half), F32), jnp.zeros((1, half), F32)]
    d_q = [0.0, 0.0]
    d_w = [0.0, 0.0]
    d_k = [0.0, 0.0]
    for a, b in PAIRS:
        part_x = jnp.where(upto[a, b], -dx[a, b], 0.0)
        part_n = jnp.where(before[a, b], dn[a, b], 0.0)
        part_y = jnp.where(before[a, b], -dy[a, b], 0.0)
        d_beta[b] = d_beta[b] + jnp.sum(
            part_x * cross[a, b] + part_n * gram_raw[a, b], axis=0, keepdims=True
        )
        upper = jnp.concatenate([ds[a, b], (part_x * beta_cols[b]).astype(BF)], axis=1)
        lower = jnp.concatenate([part_y.astype(BF), (part_n * beta_cols[b]).astype(BF)], axis=1)
        big = jnp.concatenate([upper, lower], axis=0)
        rows_a, cols_b = slice(a * half, (a + 1) * half), slice(b * half, (b + 1) * half)
        right = jnp.concatenate([key[cols_b], house_dir[cols_b]], axis=0)
        left = jnp.concatenate([query[rows_a], house_dir[rows_a]], axis=0)
        by_row = dot_nn(big, right)
        by_col = dot_tn(big, left)
        d_q[a] = d_q[a] + by_row[:half]
        d_w[a] = d_w[a] + by_row[half:]
        d_k[b] = d_k[b] + by_col[:half]
        d_w[b] = d_w[b] + by_col[half:]
    d_dir = jnp.concatenate(d_w, axis=0)
    d_conv = inverse * d_dir - direct * (
        inverse * jnp.sum(direct * d_dir, axis=1, keepdims=True)
    )
    d_house = taps[0:1, :] * d_conv
    d_taps = [jnp.sum(d_conv * house, axis=0, keepdims=True)]
    for shift in range(1, taps.shape[0]):
        live = jnp.where(place >= shift, d_conv, 0.0)
        d_house = d_house + taps[shift : shift + 1, :] * pltpu.roll(live, rows - shift, 0)
        d_taps.append(jnp.sum(live * pltpu.roll(house, shift, 0), axis=0, keepdims=True))
    d_logit = jnp.concatenate(d_beta, axis=1) * beta * (1.0 - 0.5 * beta)
    return (
        jnp.concatenate(d_q, axis=0).astype(BF),
        jnp.concatenate(d_k, axis=0).astype(BF),
        jnp.concatenate([dv0, dv1], axis=0).astype(BF),
        d_house.astype(BF),
        d_logit,
        d_taps,
    )


def backward_kernel(
    heads, slots, lengths_ref, me_ref, logit_ref, taps_ref, house_ref, q_ref, k_ref, v_ref, dm_ref, kept_ref,
    four_ref, dl_ref, dt_ref,
):
    step = pl.program_id(0)
    rows = q_ref.shape[0]
    row = lax.broadcasted_iota(jnp.int32, (rows, 1), 0)
    begin = begins(starts_of(lengths_ref, me_ref[0], slots), row)
    place = row - begin
    for head in range(heads):
        cols = slice(head * 128, (head + 1) * 128)
        logit = logit_ref[pl.ds(step * heads + head, 1), :]
        kept = tuple(kept_ref[head, slot] for slot in range(8))
        d_q, d_k, d_v, d_h, d_l, d_t = backward_head(
            q_ref[:, cols], k_ref[:, cols], v_ref[:, cols], house_ref[:, cols], logit,
            taps_ref[:, cols], begin, place, dm_ref[:, cols], kept,
        )
        for slot, item in enumerate((d_q, d_k, d_v, d_h)):
            four_ref[slot, :, cols] = item
        dl_ref[pl.ds(step * heads + head, 1), :] = d_l
        for tap, item in enumerate(d_t):
            dt_ref[tap : tap + 1, cols] = item


def mixer_backward(lengths, me, logit, taps, house, query, key, value, d_mixed, kept, heads=2):
    rows, width = query.shape
    count = width // 128
    half = rows // 2
    wide = pl.BlockSpec((rows, heads * 128), lambda i: (0, i))
    narrow = pl.BlockSpec((taps.shape[0], heads * 128), lambda i: (0, i))
    whole = pl.BlockSpec(logit.shape, lambda i: (0, 0))
    return pl.pallas_call(
        functools.partial(backward_kernel, heads, lengths.shape[1]),
        grid=(count // heads,),
        in_specs=[
            pl.BlockSpec(memory_space=pltpu.SMEM),
            pl.BlockSpec(memory_space=pltpu.SMEM),
            whole, narrow, wide, wide, wide, wide, wide,
            pl.BlockSpec((heads, 8, half, half), lambda i: (i, 0, 0, 0)),
        ],
        out_specs=[pl.BlockSpec((4, rows, heads * 128), lambda i: (0, 0, i)), whole, narrow],
        out_shape=[
            jax.ShapeDtypeStruct((4, rows, width), BF),
            jax.ShapeDtypeStruct(logit.shape, F32),
            jax.ShapeDtypeStruct(taps.shape, F32),
        ],
        compiler_params=pltpu.CompilerParams(vmem_limit_bytes=VMEM),
        cost_estimate=COST,
        name="mixer_backward",
    )(lengths, me, logit, taps, house, query, key, value, d_mixed, kept)


def starts_of(lengths_ref, me, slots):
    starts, sum_so_far = [], 0
    for j in range(slots):
        starts.append(sum_so_far)
        sum_so_far = sum_so_far + lengths_ref[me, j]
    return starts


def begins(starts, row):
    begin = jnp.zeros_like(row)
    for start in starts[1:]:
        begin = jnp.where(row >= start, start, begin)
    return begin


def group_of(sequence, slots):
    return lax.div(sequence, jnp.int32(slots))


def slot_taken(dealing_ref, me, slots, group):
    found = jnp.int32(0)
    for k in range(slots):
        found = jnp.where(group_of(dealing_ref[me * slots + k], slots) == group, k, found)
    return found


def holder_of(dealing_ref, me, slots, count, sequence):
    far, slot = jnp.int32(0), jnp.int32(0)
    for by in (-1, 0, 1):
        for k in range(slots):
            position = (me + by) * slots + k
            inside = (position >= 0) & (position < count)
            hit = inside & (dealing_ref[jnp.clip(position, 0, count - 1)] == sequence)
            far = jnp.where(hit, by, far)
            slot = jnp.where(hit, k, slot)
    return far, slot


def part_kernel(dealing_ref, me_ref, up_in, down_in, up_out, down_out):
    span = up_in.shape[1]
    for source, out in ((up_in, up_out), (down_in, down_out)):
        out[:span] = source[0]
        out[span:] = jnp.zeros((out.shape[0] - span, out.shape[1]), BF)


def slots_to_send(dealing, me, cotangent):
    slots, span, width = cotangent.shape
    tile = 512
    out = pl.BlockSpec((span + 8, tile), lambda j, dealing, me: (0, j))

    def source(by):
        return pl.BlockSpec(
            (1, span, tile),
            lambda j, dealing, me: (slot_taken(dealing, me[0], slots, me[0] + by), 0, j),
        )

    shape = jax.ShapeDtypeStruct((span + 8, width), BF)
    return pl.pallas_call(
        part_kernel,
        grid_spec=pltpu.PrefetchScalarGridSpec(
            num_scalar_prefetch=2,
            grid=(width // tile,),
            in_specs=[source(1), source(-1)],
            out_specs=[out, out],
        ),
        out_shape=[shape, shape],
        compiler_params=pltpu.CompilerParams(vmem_limit_bytes=VMEM),
        cost_estimate=COST,
        name="slots_to_send",
    )(dealing, me, cotangent, cotangent)


def arrive_kernel(slots, count, span, lengths_ref, dealing_ref, me_ref, own_ref, low_ref, high_ref, out_ref, picks):
    @pl.when(pl.program_id(0) == 0)
    def _():
        me = me_ref[0]
        starts = starts_of(lengths_ref, me, slots)
        row = lax.broadcasted_iota(jnp.int32, (picks.shape[0], 1), 0)
        index = jnp.zeros_like(row)
        for j in range(slots):
            far, slot = holder_of(dealing_ref, me, slots, count, me * slots + j)
            base = jnp.where(far == 0, slot * span, jnp.where(far < 0, slots * span, (slots + 1) * span))
            index = jnp.where(row >= starts[j], base + row - starts[j], index)
        column = lax.broadcasted_iota(jnp.int32, picks.shape, 1)
        picks[...] = jnp.where(column == index, 1.0, 0.0).astype(BF)

    out_ref[...] = (
        dot_nn(picks[:, : slots * span], own_ref[...])
        + dot_nn(picks[:, slots * span : (slots + 1) * span], low_ref[:span])
        + dot_nn(picks[:, (slots + 1) * span :], high_ref[:span])
    ).astype(BF)


def cotangent_arrived(lengths, dealing, me, own, low, high, rows):
    slots, span, width = own.shape
    own = own.reshape(slots * span, width)
    tile = 512
    column = lambda n: pl.BlockSpec((n, tile), lambda j, *s: (0, j))
    return pl.pallas_call(
        functools.partial(arrive_kernel, slots, dealing.shape[0], span),
        grid_spec=pltpu.PrefetchScalarGridSpec(
            num_scalar_prefetch=3,
            grid=(width // tile,),
            in_specs=[column(own.shape[0]), column(low.shape[0]), column(high.shape[0])],
            out_specs=column(rows),
            scratch_shapes=[pltpu.VMEM((rows, (slots + 2) * span), BF)],
        ),
        out_shape=jax.ShapeDtypeStruct((rows, width), BF),
        compiler_params=pltpu.CompilerParams(vmem_limit_bytes=VMEM),
        cost_estimate=COST,
        name="cotangent_arrived",
    )(lengths, dealing, me, own, low, high)


def deal_kernel(
    slots, count, span, lengths_ref, dealing_ref, me_ref, hidden_ref, upper_ref, lower_ref, other_upper_ref, other_lower_ref,
    own_ref, up_ref, down_ref, picks,
):
    @pl.when(pl.program_id(0) == 0)
    def _():
        me = me_ref[0]
        starts = starts_of(lengths_ref, me, slots)

        def zone(chosen):
            start, length = jnp.int32(0), jnp.int32(0)
            for j in range(slots):
                start = jnp.where(chosen[j], starts[j], start)
                length = jnp.where(chosen[j], lengths_ref[me, j], length)
            return start, length

        held = [dealing_ref[me * slots + k] for k in range(slots)]
        far = [holder_of(dealing_ref, me, slots, count, me * slots + j)[0] for j in range(slots)]
        zones = [zone([held[k] == me * slots + j for j in range(slots)]) for k in range(slots)]
        zones.append(zone([far[j] == 1 for j in range(slots)]))
        zones.append(zone([far[j] == -1 for j in range(slots)]))
        row = lax.broadcasted_iota(jnp.int32, (picks.shape[0], 1), 0)
        index = jnp.full_like(row, -1)
        for k, (start, length) in enumerate(zones):
            offset = row - k * span
            index = jnp.where((offset >= 0) & (offset < length), start + offset, index)
        column = lax.broadcasted_iota(jnp.int32, picks.shape, 1)
        picks[...] = jnp.where(column == index, 1.0, 0.0).astype(BF)

    share = jnp.concatenate([upper_ref[...], lower_ref[...]], axis=0).astype(F32)
    other = jnp.concatenate([other_upper_ref[...], other_lower_ref[...]], axis=0).astype(F32)
    final = hidden_ref[...] + (share + other)
    out = dot_nn(picks[...], final.astype(BF)).astype(BF)
    own_ref[...] = out[: slots * span]
    up_ref[...] = out[slots * span : (slots + 1) * span]
    down_ref[...] = out[(slots + 1) * span :]


def rows_dealt(lengths, dealing, me, hidden, shares, slots, span):
    rows, width = hidden.shape
    tile = 512
    column = lambda n: pl.BlockSpec((n, tile), lambda j, *s: (0, j))
    return pl.pallas_call(
        functools.partial(deal_kernel, slots, dealing.shape[0], span),
        grid_spec=pltpu.PrefetchScalarGridSpec(
            num_scalar_prefetch=3,
            grid=(width // tile,),
            in_specs=[column(rows)] + [column(rows // 2)] * 4,
            out_specs=[column(slots * span), column(span), column(span)],
            scratch_shapes=[pltpu.VMEM(((slots + 2) * span, rows), BF)],
        ),
        out_shape=[
            jax.ShapeDtypeStruct((slots * span, width), BF),
            jax.ShapeDtypeStruct((span, width), BF),
            jax.ShapeDtypeStruct((span, width), BF),
        ],
        compiler_params=pltpu.CompilerParams(vmem_limit_bytes=VMEM),
        cost_estimate=COST,
        name="rows_dealt",
    )(lengths, dealing, me, hidden, *shares)


def norm_kernel(tokens_ref, gain_ref, normed_ref, turned_ref):
    data = tokens_ref[...].astype(F32)
    inverse = lax.rsqrt(jnp.mean(data * data, axis=1, keepdims=True) + EPSILON)
    normed = (data * inverse * gain_ref[...]).astype(BF)
    normed_ref[...] = normed
    turned_ref[...] = normed.T


def first_norm(tokens, gain, tile=128):
    rows, width = tokens.shape
    flat = pl.BlockSpec((tile, width), lambda i: (i, 0))
    return pl.pallas_call(
        norm_kernel,
        grid=(rows // tile,),
        in_specs=[flat, pl.BlockSpec((1, width), lambda i: (0, 0))],
        out_specs=[flat, pl.BlockSpec((width, tile), lambda i: (0, i))],
        out_shape=[
            jax.ShapeDtypeStruct((rows, width), BF),
            jax.ShapeDtypeStruct((width, rows), BF),
        ],
        compiler_params=pltpu.CompilerParams(vmem_limit_bytes=VMEM),
        cost_estimate=COST,
        name="first_norm",
    )(tokens, gain[None, :])


def shares_of(halves_of, step_count):
    upper, lower, other_upper, other_lower = halves_of
    above = pl.program_id(0) < step_count // 2
    one = jnp.where(above, upper[...], lower[...]).astype(F32)
    return one + jnp.where(above, other_upper[...], other_lower[...]).astype(F32)


def half_specs(rows, tile, width):
    half = rows // 2 // tile
    above = pl.BlockSpec((tile, width), lambda i: (jnp.minimum(i, half - 1), 0))
    below = pl.BlockSpec((tile, width), lambda i: (jnp.maximum(i - half, 0), 0))
    return [above, below, above, below]


def hidden_kernel(steps, tokens_ref, *refs):
    shares, (gain_ref, hidden_ref, normed_ref) = refs[:4], refs[4:]
    hidden_body(tokens_ref, shares_of(shares, steps), gain_ref, hidden_ref, normed_ref)


def hidden_body(tokens_ref, share, gain_ref, hidden_ref, normed_ref):
    hidden = tokens_ref[...].astype(F32) + share
    inverse = lax.rsqrt(jnp.mean(hidden * hidden, axis=1, keepdims=True) + EPSILON)
    normed = (hidden * inverse * gain_ref[...]).astype(BF)
    hidden_ref[...] = hidden
    normed_ref[...] = normed


def hidden_and_norm(tokens, shares, gain, tile=128):
    rows, width = tokens.shape
    flat = pl.BlockSpec((tile, width), lambda i: (i, 0))
    return pl.pallas_call(
        functools.partial(hidden_kernel, rows // tile),
        grid=(rows // tile,),
        in_specs=[flat] + half_specs(rows, tile, width) + [pl.BlockSpec((1, width), lambda i: (0, 0))],
        out_specs=[flat, flat],
        out_shape=[
            jax.ShapeDtypeStruct((rows, width), F32),
            jax.ShapeDtypeStruct((rows, width), BF),
        ],
        compiler_params=pltpu.CompilerParams(vmem_limit_bytes=VMEM),
        cost_estimate=COST,
        name="hidden_and_norm",
    )(tokens, *shares, gain[None, :])


def norm_back(d_normed, source, gain):
    inverse = lax.rsqrt(jnp.mean(source * source, axis=1, keepdims=True) + EPSILON)
    scaled = d_normed * gain
    back = inverse * scaled - source * (inverse * inverse * inverse) * jnp.mean(
        scaled * source, axis=1, keepdims=True
    )
    return back, jnp.sum(d_normed * source * inverse, axis=0, keepdims=True)


def accumulate(ref, value):
    @pl.when(pl.program_id(0) == 0)
    def _():
        ref[...] = value

    @pl.when(pl.program_id(0) > 0)
    def _():
        ref[...] += value


def branch_kernel(
    steps, upper_ref, lower_ref, other_upper_ref, other_lower_ref, hidden_ref, d_final_ref, gain_ref, out_ref,
    d_hidden_ref, d_branch_ref, d_mixed_ref, d_gain_ref,
):
    share = shares_of((upper_ref, lower_ref, other_upper_ref, other_lower_ref), steps)
    back, d_gain = norm_back(share, hidden_ref[...], gain_ref[...])
    accumulate(d_gain_ref, d_gain)
    d_hidden = d_final_ref[...].astype(F32) + back
    d_hidden_ref[...] = d_hidden
    d_branch = d_hidden.astype(BF)
    d_branch_ref[...] = d_branch
    d_mixed_ref[...] = dot_nt(d_branch, out_ref[...]).astype(BF)


def branch_back(shares, hidden, d_final, gain, w_out, tile=128):
    rows, width = hidden.shape
    channels = w_out.shape[0]
    flat = pl.BlockSpec((tile, width), lambda i: (i, 0))
    line = pl.BlockSpec((1, width), lambda i: (0, 0))
    return pl.pallas_call(
        functools.partial(branch_kernel, rows // tile),
        grid=(rows // tile,),
        in_specs=half_specs(rows, tile, width)
        + [flat, flat, line, pl.BlockSpec((channels, width), lambda i: (0, 0))],
        out_specs=[
            flat,
            flat,
            pl.BlockSpec((tile, channels), lambda i: (i, 0)),
            line,
        ],
        out_shape=[
            jax.ShapeDtypeStruct((rows, width), F32),
            jax.ShapeDtypeStruct((rows, width), BF),
            jax.ShapeDtypeStruct((rows, channels), BF),
            jax.ShapeDtypeStruct((1, width), F32),
        ],
        compiler_params=pltpu.CompilerParams(vmem_limit_bytes=VMEM),
        cost_estimate=COST,
        name="branch_back",
    )(*shares, hidden, d_final, gain[None, :], w_out)


def input_kernel(
    steps, upper_ref, lower_ref, other_upper_ref, other_lower_ref, tokens_ref, d_hidden_ref, gain_ref, taps_ref, ffn_ref, logit_ref, out_ref, small_ref
):
    tokens = tokens_ref[...].astype(F32)
    gain = gain_ref[...]
    taps, heads = taps_ref.shape[0], logit_ref.shape[0]
    share = shares_of((upper_ref, lower_ref, other_upper_ref, other_lower_ref), steps)
    back, d_gain = norm_back(share, tokens, gain)
    out_ref[...] = (d_hidden_ref[...] + back).astype(BF)
    inverse = lax.rsqrt(jnp.mean(tokens * tokens, axis=1, keepdims=True) + EPSILON)
    d_beta = dot_nn(logit_ref[...].astype(BF), (tokens * inverse * gain).astype(BF))

    @pl.when(pl.program_id(0) == 0)
    def _():
        small_ref[...] = jnp.zeros_like(small_ref)
        small_ref[0:taps, 0 : taps_ref.shape[1]] = taps_ref[...]
        small_ref[taps : taps + 1, :] = ffn_ref[...]

    small_ref[taps + 1 : taps + 2, :] += d_gain
    small_ref[taps + 2 : taps + 2 + heads, :] += d_beta


def input_back(shares, tokens, d_hidden, gain, g_taps, g_ffn_gain, d_logit, tile=128):
    rows, width = tokens.shape
    flat = pl.BlockSpec((tile, width), lambda i: (i, 0))
    line = pl.BlockSpec((1, width), lambda i: (0, 0))
    height = -(-(g_taps.shape[0] + 2 + d_logit.shape[0]) // 8) * 8
    return pl.pallas_call(
        functools.partial(input_kernel, rows // tile),
        grid=(rows // tile,),
        in_specs=half_specs(rows, tile, width)
        + [flat, flat, line]
        + [
            pl.BlockSpec(g_taps.shape, lambda i: (0, 0)),
            line,
            pl.BlockSpec((d_logit.shape[0], tile), lambda i: (0, i)),
        ],
        out_specs=[flat, pl.BlockSpec((height, width), lambda i: (0, 0))],
        out_shape=[
            jax.ShapeDtypeStruct((rows, width), BF),
            jax.ShapeDtypeStruct((height, width), F32),
        ],
        compiler_params=pltpu.CompilerParams(vmem_limit_bytes=VMEM),
        cost_estimate=COST,
        name="input_back",
    )(*shares, tokens, d_hidden, gain[None, :], g_taps, g_ffn_gain, d_logit)


def product_kernel(count, turned, small, *refs):
    lefts, weights = refs[:count], refs[count : 2 * count]
    upper_ref, lower_ref = refs[-2:]
    dot = dot_nt if turned else dot_nn
    out = dot(lefts[0][...], weights[0][...])
    for left, weight in zip(lefts[1:], weights[1:]):
        out = out + dot(left[...], weight[...])
    if small:
        out = out + lax.dot_general(
            refs[2 * count][...].astype(BF), refs[2 * count + 1][...], (((0,), (1,)), ((), ())),
            preferred_element_type=F32,
        )
    half = out.shape[0] // 2
    upper_ref[...] = out[:half].astype(BF)
    lower_ref[...] = out[half:].astype(BF)


def product(lefts, weights, turned, small=(), tile=512):
    width = weights[0].shape[0 if turned else 1]
    whole = lambda x: pl.BlockSpec(x.shape, lambda j: (0, 0))
    left_specs, arrays = [], []
    for left in lefts:
        if isinstance(left, tuple):
            array, index = left
            rows = array.shape[1]
            left_specs.append(
                pl.BlockSpec((None,) + array.shape[1:], lambda j, index=index: (index, 0, 0))
            )
            arrays.append(array)
        else:
            rows = left.shape[0]
            left_specs.append(whole(left))
            arrays.append(left)
    if turned:
        parts = [pl.BlockSpec((tile, w.shape[1]), lambda j: (j, 0)) for w in weights]
    else:
        parts = [pl.BlockSpec((w.shape[0], tile), lambda j: (0, j)) for w in weights]
    more = [whole(small[0]), pl.BlockSpec((tile, small[1].shape[1]), lambda j: (j, 0))] if small else []
    return pl.pallas_call(
        functools.partial(product_kernel, len(lefts), turned, bool(small)),
        grid=(width // tile,),
        in_specs=left_specs + parts + more,
        out_specs=[pl.BlockSpec((rows // 2, tile), lambda j: (0, j))] * 2,
        out_shape=[jax.ShapeDtypeStruct((rows // 2, width), BF)] * 2,
        compiler_params=pltpu.CompilerParams(vmem_limit_bytes=VMEM),
        cost_estimate=COST,
        name="product",
    )(*arrays, *weights, *small)


def fold_kernel(plan, *refs):
    count = 1 + max(out for out, _, _, _ in plan)
    ins, outs = refs[:-count], refs[-count:]
    for out, start, width, terms in plan:
        part = None
        for ref, column in terms:
            term = ins[ref][:, column : column + width].astype(F32)
            part = term if part is None else part + term
        outs[out][:, start : start + width] = part.astype(outs[out].dtype)


def fold(outs, height, dtype):
    step = height
    while step % 2 == 0 and step > 96 and (step // 2) % 8 == 0:
        step //= 2
    arrays, plan, widths = [], [], []
    for out, streams in enumerate(outs):
        start = 0
        for width, terms in streams:
            places = []
            for array, row, column in terms:
                known = [i for i, (a, r) in enumerate(arrays) if a is array and r == row]
                if not known:
                    arrays.append((array, row))
                places.append((known[0] if known else len(arrays) - 1, column))
            plan.append((out, start, width, places))
            start += width
        widths.append(start)
    return pl.pallas_call(
        functools.partial(fold_kernel, plan),
        grid=(height // step,),
        in_specs=[
            pl.BlockSpec((step, array.shape[1]), lambda i, r=row // step: (r + i, 0))
            for array, row in arrays
        ],
        out_specs=[pl.BlockSpec((step, width), lambda i: (i, 0)) for width in widths],
        out_shape=[jax.ShapeDtypeStruct((height, width), dtype) for width in widths],
        compiler_params=pltpu.CompilerParams(vmem_limit_bytes=VMEM),
        cost_estimate=MORE,
        name="fold",
    )(*[array for array, _ in arrays])


def added_kernel(a_ref, b_ref, out_ref):
    out_ref[...] = a_ref[...] + b_ref[...]


def added(a, b):
    return pl.pallas_call(
        added_kernel,
        out_shape=jax.ShapeDtypeStruct(a.shape, a.dtype),
        compiler_params=pltpu.CompilerParams(vmem_limit_bytes=VMEM),
        cost_estimate=COST,
        name="added",
    )(a, b)


def pack(left, order_ref, turned, packed, first=0):
    size, block, _ = turned.shape
    around = left.T
    for i in range(size):
        turned[i] = around[i * block : (i + 1) * block]
    for i in range(packed.shape[0] // block):
        packed[i * block : (i + 1) * block, :] = turned[order_ref[first + i]]


def wgrad_kernel(plan, order_ref, *refs):
    lefts, rights = refs[: len(refs) - 3 - len(plan)], refs[len(refs) - 3 - len(plan) : -3]
    out_ref, turned, packed = refs[-3:]
    step = pl.program_id(0)

    @pl.when(step == 0)
    def _():
        for part, left_ref in enumerate(lefts):
            pack(left_ref[...], order_ref, turned, packed.at[part])

    for (part, first, steps), right_ref in zip(plan, rights):

        @pl.when((step >= first) & (step < first + steps))
        def _(right_ref=right_ref, part=part):
            out_ref[...] = dot_nn(packed[part], right_ref[...]).astype(out_ref.dtype)


def wgrad(order, size, parts, tile=512):
    count = order.shape[0]
    lefts = [left for left, _ in parts]
    rights = [right for _, several in parts for right in several]
    tokens, width = lefts[0].shape
    block = width // size
    tile = next(t for t in (tile, 384, 256, 128) if all(r.shape[1] % t == 0 for r in rights))
    plan, first = [], 0
    for part, (_, several) in enumerate(parts):
        for right in several:
            plan.append((part, first, right.shape[1] // tile))
            first += right.shape[1] // tile
    return pl.pallas_call(
        functools.partial(wgrad_kernel, plan),
        grid_spec=pltpu.PrefetchScalarGridSpec(
            num_scalar_prefetch=1,
            grid=(first,),
            in_specs=[pl.BlockSpec(left.shape, lambda j, order: (0, 0)) for left in lefts]
            + [
                pl.BlockSpec(
                    (tokens, tile), lambda j, order, s=s, n=n: (0, jnp.clip(j - s, 0, n - 1))
                )
                for _, s, n in plan
            ],
            out_specs=pl.BlockSpec((count * block, tile), lambda j, order: (0, j)),
            scratch_shapes=[
                pltpu.VMEM((size, block, tokens), BF),
                pltpu.VMEM((len(lefts), count * block, tokens), BF),
            ],
        ),
        out_shape=jax.ShapeDtypeStruct((count * block, first * tile), BF),
        compiler_params=pltpu.CompilerParams(vmem_limit_bytes=VMEM),
        cost_estimate=COST,
        name="wgrad",
    )(order, *lefts, *rights)


def plane_kernel(order_ref, left_ref, right_ref, out_ref):
    total = dot_nn(left_ref[0], right_ref[0])
    for i in range(1, left_ref.shape[0]):
        total = total + dot_nn(left_ref[i], right_ref[i])
    out_ref[...] = total.astype(out_ref.dtype)


def wgrad_plane(order, left, right, blocks):
    parts, width, tokens = left.shape
    columns = right.shape[2]
    height = width // blocks
    return pl.pallas_call(
        plane_kernel,
        grid_spec=pltpu.PrefetchScalarGridSpec(
            num_scalar_prefetch=1,
            grid=(order.shape[0],),
            in_specs=[
                pl.BlockSpec((parts, height, tokens), lambda j, order: (0, order[j], 0)),
                pl.BlockSpec(right.shape, lambda j, order: (0, 0, 0)),
            ],
            out_specs=pl.BlockSpec((height, columns), lambda j, order: (j, 0)),
        ),
        out_shape=jax.ShapeDtypeStruct((order.shape[0] * height, columns), BF),
        compiler_params=pltpu.CompilerParams(vmem_limit_bytes=VMEM),
        cost_estimate=COST,
        name="wgrad_plane",
    )(order, left, right)


def ffn_kernel(
    order_ref, normed_ref, d_final_ref, gate_ref, up_ref, down_ref,
    inner_ref, d_gate_ref, d_up_ref, g_gate_ref, g_up_ref, turned, packed,
):

    @pl.when(pl.program_id(0) == 0)
    def _():
        pack(normed_ref[...], order_ref, turned, packed)

    gate = dot_nn(normed_ref[...], gate_ref[...])
    lift = dot_nn(normed_ref[...], up_ref[...])
    d_inner = dot_nt(d_final_ref[...], down_ref[...])
    sig = jax.nn.sigmoid(gate)
    silu = gate * sig
    inner_ref[...] = (silu * lift).astype(BF)
    d_gate = (d_inner * lift * sig * (1.0 + gate * (1.0 - sig))).astype(BF)
    d_up = (d_inner * silu).astype(BF)
    d_gate_ref[...] = d_gate
    d_up_ref[...] = d_up
    g_gate_ref[...] = dot_nn(packed[...], d_gate).astype(BF)
    g_up_ref[...] = dot_nn(packed[...], d_up).astype(BF)


def ffn(order, size, normed, d_final, w_gate, w_up, w_down, tile=512):
    rows, width = normed.shape
    units = w_gate.shape[1]
    whole = pl.BlockSpec((rows, width), lambda j, order: (0, 0))
    column = pl.BlockSpec((width, tile), lambda j, order: (0, j))
    out = pl.BlockSpec((rows, tile), lambda j, order: (0, j))
    shape = jax.ShapeDtypeStruct((rows, units), BF)
    grad = jax.ShapeDtypeStruct((width, units), BF)
    return pl.pallas_call(
        ffn_kernel,
        grid_spec=pltpu.PrefetchScalarGridSpec(
            num_scalar_prefetch=1,
            grid=(units // tile,),
            in_specs=[
                whole,
                whole,
                column,
                column,
                pl.BlockSpec((tile, width), lambda j, order: (j, 0)),
            ],
            out_specs=[out, out, out, column, column],
            scratch_shapes=[
                pltpu.VMEM((size, width // size, rows), BF),
                pltpu.VMEM((width, rows), BF),
            ],
        ),
        out_shape=[shape, shape, shape, grad, grad],
        compiler_params=pltpu.CompilerParams(vmem_limit_bytes=VMEM),
        cost_estimate=COST,
        name="ffn",
    )(order, normed, d_final, w_gate, w_up, w_down)


def swap(x, axis, bit):
    size = lax.axis_size(axis)
    return lax.ppermute(x, axis, [(i, i ^ (1 << bit)) for i in range(size)])


def flips_of(count, bits):
    flips = []
    for position in reversed(range(count)):
        flips.append(
            sum(((position >> (len(bits) - 1 - rank)) & 1) << bit for rank, bit in enumerate(bits))
        )
    return jnp.array(flips, jnp.int32)


def halve(terms, bits):
    for bit in bits:
        half = terms[0].shape[0] // 2
        out = sum(t[:half].astype(F32) for t in terms).astype(BF)
        terms = [t[half:] for t in terms] + [swap(out, "dp", bit)]
    return terms


def total(terms):
    return sum(t.astype(F32) for t in terms)


def after(value, *others):
    return lax.optimization_barrier((value,) + others)[0]


class Order:
    def __init__(self):
        self.last = ()

    def gate(self, *values):
        if self.last:
            values = lax.optimization_barrier(tuple(values) + self.last)[: len(values)]
        return values if len(values) > 1 else values[0]

    def mark(self, *values):
        self.last = values
        return values if len(values) > 1 else values[0]


def stream(*arrays):
    return arrays[0].shape[1], [(array, 0, 0) for array in arrays]


def joined(streams, got):
    column, out = 0, []
    for width, terms in streams:
        out.append((width, terms + [(got, 0, column)]))
        column += width
    return out


def on_device(
    tokens,
    cotangent,
    lengths,
    dealing,
    attn_gain,
    w_query,
    w_key,
    w_value,
    w_house,
    w_beta,
    conv_taps,
    w_out,
    ffn_gain,
    w_gate,
    w_up,
    w_down,
):
    rows, width = tokens.shape
    slots, span = cotangent.shape[:2]
    size = lax.axis_size("dp")
    me = lax.axis_index("dp").astype(jnp.int32)
    me1 = me.reshape(1)
    block = width // size
    bits = list(range(size.bit_length() - 1))
    plane, line = bits[:2], bits[2:]
    up = [(i, i + 1) for i in range(size - 1)]
    down = [(i + 1, i) for i in range(size - 1)]
    first = size // 2
    groups = [[i + j for j in range(4)] for i in range(0, size, 4)]
    order_line = (me >> 2) ^ flips_of(size // 4, [b - 2 for b in line])
    order_plane = (jnp.arange(4, dtype=jnp.int32)[:, None] + 4 * order_line[None, :]).reshape(-1)
    order_zxy = me ^ flips_of(size, line + plane)
    order_xyz = me ^ flips_of(size, bits)
    order = Order()

    cot_up, cot_down = order.mark(*slots_to_send(dealing, me1, cotangent))
    cot_low = lax.ppermute(cot_up, "dp", up)
    cot_high = lax.ppermute(cot_down, "dp", down)

    normed1, normed1_t = order.mark(*first_norm(order.gate(tokens), attn_gain))
    plane_normed = lax.all_gather(normed1_t, "dp", axis_index_groups=groups)
    normed = order.gate(normed1)
    logit = lax.dot_general(
        w_beta, normed, (((0,), (1,)), ((), ())), preferred_element_type=F32
    )
    query = dot_nn(normed, w_query).astype(BF)
    key = dot_nn(normed, w_key).astype(BF)
    value = dot_nn(normed, w_value).astype(BF)
    house = dot_nn(normed, w_house)
    order.mark(query, key, value, house, logit)
    mixed, kept = order.mark(
        *mixer_forward(lengths, me1, logit, conv_taps, house, order.gate(query), key, value)
    )

    def shares(parts):
        others = [swap(part, "tensor", 0) for part in parts]
        return lambda: [*parts, *order.gate(*others)]

    attn_shares = shares(order.mark(*product([order.gate(mixed)], [w_out], False)))
    hidden, normed2 = order.mark(*hidden_and_norm(tokens, attn_shares(), ffn_gain))
    d_final = order.mark(
        cotangent_arrived(
            lengths, dealing, me1, cotangent, *order.gate(cot_low, cot_high), rows
        )
    )

    def gated(outs):
        arrays = []
        for streams in outs:
            for _, terms in streams:
                for array, _, _ in terms:
                    if not any(array is known for known in arrays):
                        arrays.append(array)
        after = order.gate(*arrays)
        after = list(after) if isinstance(after, tuple) else [after]
        new = lambda array: next(n for a, n in zip(arrays, after) if a is array)
        return [
            [(w, [(new(array), r, c) for array, r, c in terms]) for w, terms in streams]
            for streams in outs
        ]

    def leave(streams, height, bit):
        (streams,) = gated([streams])
        got = swap(order.mark(fold([streams], height, BF)[0]), "dp", bit)
        return joined([(w, [(a, r + height, c) for a, r, c in terms]) for w, terms in streams], got)

    def finish(outs):
        out = fold(gated(outs), block, F32)
        order.mark(out[0])
        return out

    def wgrad_of(rows_order, left, rights):
        return order.mark(
            wgrad(rows_order, size, [(left, [order.gate(rights[0])] + list(rights[1:]))])
        )

    half, quarter = width // 2, width // 4
    columns = query.shape[1]
    heights = [quarter >> (i + 1) for i in range(len(line))]
    lines = size // 4

    def plane_sum(x):
        return lax.psum_scatter(
            x, "dp", scatter_dimension=0, tiled=True, axis_index_groups=groups
        )

    inner, d_gate, d_up, gate_all, up_all = order.mark(
        *ffn(order_plane, size, order.gate(normed2), d_final, w_gate, w_up, w_down)
    )
    gate_sum, up_sum = plane_sum(gate_all), plane_sum(up_all)
    down_leave = wgrad_of(order_zxy[:first], d_final, [inner])
    down_got = swap(down_leave, "dp", line[0])
    d_norm2_shares = shares(order.mark(*product([order.gate(d_gate), d_up], [w_gate, w_up], True)))
    down_stay = wgrad_of(order_zxy[first:], d_final, [inner])
    downs = [stream(down_stay, down_got)]
    plane_normed = order.mark(order.gate(plane_normed))
    d_hidden, d_branch, d_mixed, g_ffn_gain = order.mark(
        *branch_back(d_norm2_shares(), hidden, d_final, ffn_gain, w_out)
    )
    out_leave = wgrad_of(order_xyz[:first], d_branch, [mixed])
    out_got = swap(out_leave, "dp", 0)

    d_four, d_logit, g_taps = order.mark(
        *mixer_backward(
            lengths, me1, logit, conv_taps, house, query, key, value, order.gate(d_mixed), kept
        )
    )
    plane_four = lax.all_to_all(d_four, "dp", 0, 0, axis_index_groups=groups)
    out_stay = wgrad_of(order_xyz[first:], d_branch, [mixed])
    height = half
    for bit in line[1:]:
        height //= 2
        downs = leave(downs, height, bit)
    d_norm1_shares = shares(
        order.mark(
            *product(
                [(order.gate(d_four), i) for i in range(4)],
                [w_query, w_key, w_value, w_house], True, small=(d_logit, w_beta),
            )
        )
    )
    down_shares = shares(order.mark(*product([order.gate(inner)], [w_down], False)))
    gates = leave([stream(gate_sum)], heights[0], line[0])
    input_grad, small = order.mark(
        *input_back(
            d_norm1_shares(), tokens, d_hidden, attn_gain, g_taps, g_ffn_gain, d_logit
        )
    )
    small_bits, small_got = list(bits), None

    def small_step():
        nonlocal small, small_got
        if small_got is not None:
            small = order.mark(added(small, order.gate(small_got)))
        small_got = swap(small, "dp", small_bits.pop(0)) if small_bits else None

    small_step()
    attn_leave = order.mark(
        wgrad_plane(order_line[: lines // 2], plane_normed, order.gate(plane_four), lines)
    )
    attn_got = swap(attn_leave, "dp", line[0])
    attn_stay = order.mark(
        wgrad_plane(order_line[lines // 2 :], plane_normed, order.gate(plane_four), lines)
    )
    attns = [stream(attn_stay, attn_got)]
    for low, bit in zip(heights[1:], line[1:]):
        gates = leave(gates, low, bit)
    outs = leave([stream(out_stay, out_got)], quarter, 1)
    dealt, deal_up, deal_down = order.mark(
        *rows_dealt(lengths, dealing, me1, hidden, down_shares(), slots, span)
    )
    small_step()
    height //= 2
    downs = leave(downs, height, 0)
    attn_height = half
    for bit in line[1:]:
        attn_height //= 2
        attns = leave(attns, attn_height, bit)
    (g_gate,) = finish([gates])
    small_step()
    ups = leave([stream(up_sum)] + outs, heights[0], line[0])
    out_low = lax.ppermute(deal_up, "dp", up)
    out_high = lax.ppermute(deal_down, "dp", down)
    height //= 2
    downs = leave(downs, height, 1)
    attn_sum = order.mark(fold(gated([attns]), width // lines, BF)[0])
    plane_rows = lax.all_to_all(
        attn_sum.reshape(4, block, columns), "dp", 0, 0, axis_index_groups=groups
    )
    for low, bit in zip(heights[1:], line[1:]):
        ups = leave(ups, low, bit)
    (g_down,) = finish([downs])
    out_low, out_high = order.mark(*order.gate(out_low, out_high))
    while small_got is not None:
        small_step()
    g_up, g_out = finish([[up_one] for up_one in ups])
    g_query, g_key, g_value, g_house = order.gate(plane_rows).astype(F32)

    taps = conv_taps.shape[0]
    per_row = lax.dynamic_slice_in_dim(small[taps:], me * block, block, axis=1)
    taps_total = small[:taps, :columns]
    held_from = lax.dynamic_slice_in_dim(dealing, me * slots, slots) // slots - me
    output = jnp.where(
        (held_from == -1)[:, None, None],
        out_low[None],
        jnp.where(
            (held_from == 1)[:, None, None], out_high[None], dealt.reshape(slots, span, width)
        ),
    )
    return (
        output,
        input_grad,
        per_row[1],
        g_query,
        g_key,
        g_value,
        g_house,
        per_row[2 : 2 + d_logit.shape[0]].T,
        taps_total,
        g_out.T,
        per_row[0],
        g_gate,
        g_up,
        g_down.T,
    )


def solution(mesh):
    in_specs = (
        P("dp", None),
        P("dp", None, None),
        P(),
        P(),
        P(),
        P(None, "tensor"),
        P(None, "tensor"),
        P(None, "tensor"),
        P(None, "tensor"),
        P(None, "tensor"),
        P(None, "tensor"),
        P("tensor", None),
        P(),
        P(None, "tensor"),
        P(None, "tensor"),
        P("tensor", None),
    )
    out_specs = (
        P("dp", None, None),
        P("dp", None),
        P("dp"),
        P("dp", "tensor"),
        P("dp", "tensor"),
        P("dp", "tensor"),
        P("dp", "tensor"),
        P("dp", "tensor"),
        P(None, "tensor"),
        P("tensor", "dp"),
        P("dp"),
        P("dp", "tensor"),
        P("dp", "tensor"),
        P("tensor", "dp"),
    )
    return jax.shard_map(
        on_device, mesh=mesh, in_specs=in_specs, out_specs=out_specs, check_vma=False
    )
```

```python
import functools
import jax
import jax.numpy as jnp
from jax import lax
from jax.experimental import pallas as pl
from jax.experimental.pallas import tpu as pltpu
from jax.sharding import PartitionSpec as P

EPSILON = 1e-06
BF = jnp.bfloat16
F32 = jnp.float32

VMEM = 60 << 20
COST = pl.CostEstimate(flops=0, bytes_accessed=0, transcendentals=0)
MORE = pl.CostEstimate(flops=1_000_000_000, bytes_accessed=1_000_000, transcendentals=0)


def dot_nn(a, b):
    return lax.dot_general(a, b, (((1,), (0,)), ((), ())), preferred_element_type=F32)


def dot_nt(a, b):
    return lax.dot_general(a, b, (((1,), (1,)), ((), ())), preferred_element_type=F32)


def dot_tn(a, b):
    return lax.dot_general(a, b, (((0,), (0,)), ((), ())), preferred_element_type=F32)


def halves(x):
    high = x.astype(BF)
    return high, (x - high.astype(F32)).astype(BF)


def split_product(a, b):
    return dot_nn(a[0], b[0]) + (dot_nn(a[0], b[1]) + dot_nn(a[1], b[0]))


def unit_lower_inverses(stricts, base):
    size, lanes = stricts[0].shape[0], 128
    tiles, per_tile = size // lanes, lanes // base
    lane = lax.broadcasted_iota(jnp.int32, (base, lanes), 1)
    row = lax.broadcasted_iota(jnp.int32, (base, lanes), 0)
    owner, within = lane // base, lane % base
    pieces = [
        strict[t * lanes : (t + 1) * lanes, t * lanes : (t + 1) * lanes]
        for strict in stricts
        for t in range(tiles)
    ]
    compact = []
    for piece in pieces:
        packed = jnp.zeros((base, lanes), F32)
        for block in range(per_tile):
            packed = jnp.where(owner == block, piece[block * base : (block + 1) * base], packed)
        compact.append(packed)
    solved = [jnp.where(row == within, 1.0, 0.0).astype(F32)] * len(pieces)
    for step in range(base - 1):
        index = owner * base + step
        solved = [
            s - jnp.take_along_axis(c, index, axis=1) * s[step : step + 1, :]
            for s, c in zip(solved, compact)
        ]
    inverses = [
        jnp.concatenate([jnp.where(owner == b, s, 0.0) for b in range(per_tile)], axis=0)
        for s in solved
    ]
    grown = base * 2
    row = lax.broadcasted_iota(jnp.int32, (lanes, lanes), 0)
    col = lax.broadcasted_iota(jnp.int32, (lanes, lanes), 1)
    while grown <= lanes:
        joined = (row // grown == col // grown) & (row // (grown // 2) != col // (grown // 2))
        parts = [halves(i) for i in inverses]
        crosses = [halves(jnp.where(joined, p, 0.0)) for p in pieces]
        firsts = [halves(split_product(p, c)) for p, c in zip(parts, crosses)]
        inverses = [i - split_product(f, p) for i, f, p in zip(inverses, firsts, parts)]
        grown *= 2
    whole = []
    parts = [halves(i) for i in inverses]
    corners = [halves(strict[lanes:, :lanes]) for strict in stricts]
    firsts = [halves(split_product(parts[2 * n + 1], c)) for n, c in enumerate(corners)]
    for n, first in enumerate(firsts):
        corner = -split_product(first, parts[2 * n])
        top = jnp.concatenate([inverses[2 * n], jnp.zeros((lanes, lanes), F32)], axis=1)
        whole.append(
            jnp.concatenate([top, jnp.concatenate([corner, inverses[2 * n + 1]], axis=1)], axis=0)
        )
    return whole


def shifted_rows(x, amount, place):
    return jnp.where(place >= amount, pltpu.roll(x, amount, 0), 0.0)


def direction(house, taps, place):
    conv = taps[0:1, :] * house
    for shift in range(1, taps.shape[0]):
        conv = conv + taps[shift : shift + 1, :] * shifted_rows(house, shift, place)
    inverse = lax.rsqrt(jnp.sum(conv * conv, axis=1, keepdims=True) + EPSILON)
    return conv, inverse


PAIRS = ((0, 0), (1, 0), (1, 1))


def masks_of(begin, half, a, b):
    inside = lax.broadcasted_iota(jnp.int32, (half, half), 1) + b * half >= begin[
        a * half : (a + 1) * half
    ]
    if a != b:
        return inside, inside
    col = lax.broadcasted_iota(jnp.int32, (half, half), 1)
    row = lax.broadcasted_iota(jnp.int32, (half, half), 0)
    return inside & (col <= row), inside & (col < row)


def scores_of(query, key, house_dir, begin, half, a, b):
    rows, cols = slice(a * half, (a + 1) * half), slice(b * half, (b + 1) * half)
    left = jnp.concatenate([query[rows], house_dir[rows]], axis=0)
    right = jnp.concatenate([key[cols], house_dir[cols]], axis=0)
    every = dot_nt(left, right)
    col = lax.broadcasted_iota(jnp.int32, (half, half), 1) + b * half
    row = lax.broadcasted_iota(jnp.int32, (half, half), 0) + a * half
    inside = col >= begin[rows]
    upto = inside & (col <= row)
    before = inside & (col < row)
    return (
        every[:half, :half],
        jnp.where(upto, every[:half, half:], 0.0),
        jnp.where(before, every[half:, :half], 0.0),
        jnp.where(before, every[half:, half:], 0.0),
        upto,
        before,
    )


def forward_heads(items, begin, place):
    half = items[0][0].shape[0] // 2
    scaling = items[0][0].shape[1] ** (-0.5)
    both = (slice(0, half), slice(half, 2 * half))
    upto, before = {}, {}
    for a, b in PAIRS:
        upto[a, b], before[a, b] = masks_of(begin, half, a, b)
    heads = []
    for query, key, value, house, logit, taps in items:
        conv, inverse = direction(house, taps, place)
        house_dir = (conv * inverse).astype(BF)
        beta = 2.0 * jax.nn.sigmoid(logit)
        cross, know, gram = {}, {}, {}
        for a, b in PAIRS:
            left = jnp.concatenate([query[both[a]], house_dir[both[a]]], axis=0)
            every = dot_nt(left, house_dir[both[b]])
            beta_cols = beta[:, both[b]]
            cross[a, b] = jnp.where(upto[a, b], every[:half] * -beta_cols, 0.0).astype(BF)
            gram[a, b] = jnp.where(before[a, b], every[half:] * beta_cols, 0.0)
            know[a, b] = jnp.where(
                before[a, b], dot_nt(house_dir[both[a]], key[both[b]]), 0.0
            )
        heads.append((cross, know, gram, query, key.T, value))
    inverses = unit_lower_inverses([h[2][a, a] for h in heads for a in (0, 1)], 16)
    eye = (
        lax.broadcasted_iota(jnp.int32, (half, half), 0)
        == lax.broadcasted_iota(jnp.int32, (half, half), 1)
    )
    tails = [jnp.where(eye, 0.0, i).astype(BF) for i in inverses]
    results = []
    for n, (cross, know, gram, query, key_t, value) in enumerate(heads):
        tail0, tail1 = tails[2 * n : 2 * n + 2]
        z00 = (know[0, 0] + dot_nn(tail0, know[0, 0].astype(BF))).astype(BF)
        z11 = (know[1, 1] + dot_nn(tail1, know[1, 1].astype(BF))).astype(BF)
        rest = know[1, 0] - dot_nn(gram[1, 0].astype(BF), z00)
        z10 = (rest + dot_nn(tail1, rest.astype(BF))).astype(BF)

        def score(pair, lefts, rights):
            out = dot_nn(jnp.concatenate(lefts, axis=1), jnp.concatenate(rights, axis=0))
            return jnp.where(upto[pair], out * scaling, -1e30)

        q0, q1 = query[both[0]], query[both[1]]
        s00 = score((0, 0), [q0, cross[0, 0]], [key_t[:, both[0]], z00])
        s10 = score((1, 0), [q1, cross[1, 0], cross[1, 1]], [key_t[:, both[0]], z00, z10])
        s11 = score((1, 1), [q1, cross[1, 1]], [key_t[:, both[1]], z11])
        top0 = jnp.max(s00, axis=1, keepdims=True)
        top1 = jnp.maximum(
            jnp.max(s10, axis=1, keepdims=True), jnp.max(s11, axis=1, keepdims=True)
        )
        e00, e10, e11 = jnp.exp(s00 - top0), jnp.exp(s10 - top1), jnp.exp(s11 - top1)
        inv0 = 1.0 / jnp.sum(e00, axis=1, keepdims=True)
        inv1 = 1.0 / (jnp.sum(e10, axis=1, keepdims=True) + jnp.sum(e11, axis=1, keepdims=True))
        p00, p10, p11 = (e00 * inv0).astype(BF), (e10 * inv1).astype(BF), (e11 * inv1).astype(BF)
        mixed0 = dot_nn(p00, value[both[0]])
        mixed1 = dot_nn(jnp.concatenate([p10, p11], axis=1), value)
        mixed = jnp.concatenate([mixed0, mixed1], axis=0).astype(BF)
        results.append((mixed, (p00, p10, p11, z00, z10, z11, tail0, tail1)))
    return results


def forward_kernel(heads, slots, lengths_ref, me_ref, logit_ref, taps_ref, house_ref, q_ref, k_ref, v_ref, mixed_ref, kept_ref):
    step = pl.program_id(0)
    rows = q_ref.shape[0]
    row = lax.broadcasted_iota(jnp.int32, (rows, 1), 0)
    begin = begins(starts_of(lengths_ref, me_ref[0], slots), row)
    place = row - begin
    columns = [slice(head * 128, (head + 1) * 128) for head in range(heads)]
    items = [
        (
            q_ref[:, cols], k_ref[:, cols], v_ref[:, cols], house_ref[:, cols],
            logit_ref[pl.ds(step * heads + head, 1), :], taps_ref[:, cols],
        )
        for head, cols in enumerate(columns)
    ]
    for head, (mixed, kept) in enumerate(forward_heads(items, begin, place)):
        mixed_ref[:, columns[head]] = mixed
        for slot, item in enumerate(kept):
            kept_ref[head, slot] = item


def mixer_forward(lengths, me, logit, taps, house, query, key, value, heads=2):
    rows, width = query.shape
    count = width // 128
    half = rows // 2
    wide = pl.BlockSpec((rows, heads * 128), lambda i: (0, i))
    return pl.pallas_call(
        functools.partial(forward_kernel, heads, lengths.shape[1]),
        grid=(count // heads,),
        in_specs=[
            pl.BlockSpec(memory_space=pltpu.SMEM),
            pl.BlockSpec(memory_space=pltpu.SMEM),
            pl.BlockSpec(logit.shape, lambda i: (0, 0)),
            pl.BlockSpec((taps.shape[0], heads * 128), lambda i: (0, i)),
            wide, wide, wide, wide,
        ],
        out_specs=[wide, pl.BlockSpec((heads, 8, half, half), lambda i: (i, 0, 0, 0))],
        out_shape=[
            jax.ShapeDtypeStruct((rows, width), BF),
            jax.ShapeDtypeStruct((count, 8, half, half), BF),
        ],
        compiler_params=pltpu.CompilerParams(vmem_limit_bytes=VMEM),
        cost_estimate=COST,
        name="mixer_forward",
    )(lengths, me, logit, taps, house, query, key, value)


def backward_head(query, key, value, house, logit, taps, begin, place, d_mixed, kept):
    p00, p10, p11, z00, z10, z11, tail0, tail1 = kept
    rows = query.shape[0]
    half = rows // 2
    scaling = query.shape[1] ** (-0.5)
    conv, inverse = direction(house, taps, place)
    direct = conv * inverse
    house_dir = direct.astype(BF)
    beta = 2.0 * jax.nn.sigmoid(logit)
    cross, cross_b, gram, gram_raw, upto, before, beta_cols = {}, {}, {}, {}, {}, {}, {}
    for a, b in PAIRS:
        _, cross[a, b], _, gram_raw[a, b], upto[a, b], before[a, b] = scores_of(
            query, key, house_dir, begin, half, a, b
        )
        beta_cols[b] = beta[:, b * half : (b + 1) * half]
        cross_b[a, b] = (cross[a, b] * beta_cols[b]).astype(BF)
    gram10 = (gram_raw[1, 0] * beta_cols[0]).astype(BF)
    d0, d1 = d_mixed[:half], d_mixed[half:]
    v0, v1 = value[:half], value[half:]
    dp00, dp10, dp11 = dot_nt(d0, v0), dot_nt(d1, v0), dot_nt(d1, v1)
    dv0 = dot_tn(p00, d0) + dot_tn(p10, d1)
    dv1 = dot_tn(p11, d1)
    f00, f10, f11 = p00.astype(F32), p10.astype(F32), p11.astype(F32)
    mean0 = jnp.sum(f00 * dp00, axis=1, keepdims=True)
    mean1 = jnp.sum(f10 * dp10, axis=1, keepdims=True) + jnp.sum(f11 * dp11, axis=1, keepdims=True)
    ds = {
        (0, 0): (f00 * (dp00 - mean0) * scaling).astype(BF),
        (1, 0): (f10 * (dp10 - mean1) * scaling).astype(BF),
        (1, 1): (f11 * (dp11 - mean1) * scaling).astype(BF),
    }
    dx = {
        (0, 0): dot_nt(ds[0, 0], z00),
        (1, 0): dot_nt(ds[1, 0], z00),
        (1, 1): dot_nt(ds[1, 1], z11) + dot_nt(ds[1, 0], z10),
    }
    dz00 = dot_tn(cross_b[0, 0], ds[0, 0]) + dot_tn(cross_b[1, 0], ds[1, 0])
    dz10 = dot_tn(cross_b[1, 1], ds[1, 0])
    dz11 = dot_tn(cross_b[1, 1], ds[1, 1])
    e11 = dz11 + dot_tn(tail1, dz11.astype(BF))
    e10 = dz10 + dot_tn(tail1, dz10.astype(BF))
    rest = dz00 - dot_tn(gram10, e10.astype(BF))
    e00 = rest + dot_tn(tail0, rest.astype(BF))
    e00b, e10b, e11b = e00.astype(BF), e10.astype(BF), e11.astype(BF)
    dn = {
        (0, 0): dot_nt(e00b, z00),
        (1, 0): dot_nt(e10b, z00),
        (1, 1): dot_nt(e10b, z10) + dot_nt(e11b, z11),
    }
    dy = {(0, 0): e00, (1, 0): e10, (1, 1): e11}
    d_beta = [jnp.zeros((1, half), F32), jnp.zeros((1, half), F32)]
    d_q = [0.0, 0.0]
    d_w = [0.0, 0.0]
    d_k = [0.0, 0.0]
    for a, b in PAIRS:
        part_x = jnp.where(upto[a, b], -dx[a, b], 0.0)
        part_n = jnp.where(before[a, b], dn[a, b], 0.0)
        part_y = jnp.where(before[a, b], -dy[a, b], 0.0)
        d_beta[b] = d_beta[b] + jnp.sum(
            part_x * cross[a, b] + part_n * gram_raw[a, b], axis=0, keepdims=True
        )
        upper = jnp.concatenate([ds[a, b], (part_x * beta_cols[b]).astype(BF)], axis=1)
        lower = jnp.concatenate([part_y.astype(BF), (part_n * beta_cols[b]).astype(BF)], axis=1)
        big = jnp.concatenate([upper, lower], axis=0)
        rows_a, cols_b = slice(a * half, (a + 1) * half), slice(b * half, (b + 1) * half)
        right = jnp.concatenate([key[cols_b], house_dir[cols_b]], axis=0)
        left = jnp.concatenate([query[rows_a], house_dir[rows_a]], axis=0)
        by_row = dot_nn(big, right)
        by_col = dot_tn(big, left)
        d_q[a] = d_q[a] + by_row[:half]
        d_w[a] = d_w[a] + by_row[half:]
        d_k[b] = d_k[b] + by_col[:half]
        d_w[b] = d_w[b] + by_col[half:]
    d_dir = jnp.concatenate(d_w, axis=0)
    d_conv = inverse * d_dir - direct * (
        inverse * jnp.sum(direct * d_dir, axis=1, keepdims=True)
    )
    d_house = taps[0:1, :] * d_conv
    d_taps = [jnp.sum(d_conv * house, axis=0, keepdims=True)]
    for shift in range(1, taps.shape[0]):
        live = jnp.where(place >= shift, d_conv, 0.0)
        d_house = d_house + taps[shift : shift + 1, :] * pltpu.roll(live, rows - shift, 0)
        d_taps.append(jnp.sum(live * pltpu.roll(house, shift, 0), axis=0, keepdims=True))
    d_logit = jnp.concatenate(d_beta, axis=1) * beta * (1.0 - 0.5 * beta)
    return (
        jnp.concatenate(d_q, axis=0).astype(BF),
        jnp.concatenate(d_k, axis=0).astype(BF),
        jnp.concatenate([dv0, dv1], axis=0).astype(BF),
        d_house.astype(BF),
        d_logit,
        d_taps,
    )


def backward_kernel(
    heads, slots, lengths_ref, me_ref, logit_ref, taps_ref, house_ref, q_ref, k_ref, v_ref, dm_ref, kept_ref,
    four_ref, dl_ref, dt_ref,
):
    step = pl.program_id(0)
    rows = q_ref.shape[0]
    row = lax.broadcasted_iota(jnp.int32, (rows, 1), 0)
    begin = begins(starts_of(lengths_ref, me_ref[0], slots), row)
    place = row - begin
    for head in range(heads):
        cols = slice(head * 128, (head + 1) * 128)
        logit = logit_ref[pl.ds(step * heads + head, 1), :]
        kept = tuple(kept_ref[head, slot] for slot in range(8))
        d_q, d_k, d_v, d_h, d_l, d_t = backward_head(
            q_ref[:, cols], k_ref[:, cols], v_ref[:, cols], house_ref[:, cols], logit,
            taps_ref[:, cols], begin, place, dm_ref[:, cols], kept,
        )
        for slot, item in enumerate((d_q, d_k, d_v, d_h)):
            four_ref[slot, :, cols] = item
        dl_ref[pl.ds(step * heads + head, 1), :] = d_l
        for tap, item in enumerate(d_t):
            dt_ref[tap : tap + 1, cols] = item


def mixer_backward(lengths, me, logit, taps, house, query, key, value, d_mixed, kept, heads=2):
    rows, width = query.shape
    count = width // 128
    half = rows // 2
    wide = pl.BlockSpec((rows, heads * 128), lambda i: (0, i))
    narrow = pl.BlockSpec((taps.shape[0], heads * 128), lambda i: (0, i))
    whole = pl.BlockSpec(logit.shape, lambda i: (0, 0))
    return pl.pallas_call(
        functools.partial(backward_kernel, heads, lengths.shape[1]),
        grid=(count // heads,),
        in_specs=[
            pl.BlockSpec(memory_space=pltpu.SMEM),
            pl.BlockSpec(memory_space=pltpu.SMEM),
            whole, narrow, wide, wide, wide, wide, wide,
            pl.BlockSpec((heads, 8, half, half), lambda i: (i, 0, 0, 0)),
        ],
        out_specs=[pl.BlockSpec((4, rows, heads * 128), lambda i: (0, 0, i)), whole, narrow],
        out_shape=[
            jax.ShapeDtypeStruct((4, rows, width), BF),
            jax.ShapeDtypeStruct(logit.shape, F32),
            jax.ShapeDtypeStruct(taps.shape, F32),
        ],
        compiler_params=pltpu.CompilerParams(vmem_limit_bytes=VMEM),
        cost_estimate=COST,
        name="mixer_backward",
    )(lengths, me, logit, taps, house, query, key, value, d_mixed, kept)


def starts_of(lengths_ref, me, slots):
    starts, sum_so_far = [], 0
    for j in range(slots):
        starts.append(sum_so_far)
        sum_so_far = sum_so_far + lengths_ref[me, j]
    return starts


def begins(starts, row):
    begin = jnp.zeros_like(row)
    for start in starts[1:]:
        begin = jnp.where(row >= start, start, begin)
    return begin


def group_of(sequence, slots):
    return lax.div(sequence, jnp.int32(slots))


def slot_taken(dealing_ref, me, slots, group):
    found = jnp.int32(0)
    for k in range(slots):
        found = jnp.where(group_of(dealing_ref[me * slots + k], slots) == group, k, found)
    return found


def holder_of(dealing_ref, me, slots, count, sequence):
    far, slot = jnp.int32(0), jnp.int32(0)
    for by in (-1, 0, 1):
        for k in range(slots):
            position = (me + by) * slots + k
            inside = (position >= 0) & (position < count)
            hit = inside & (dealing_ref[jnp.clip(position, 0, count - 1)] == sequence)
            far = jnp.where(hit, by, far)
            slot = jnp.where(hit, k, slot)
    return far, slot


def part_kernel(dealing_ref, me_ref, up_in, down_in, up_out, down_out):
    span = up_in.shape[1]
    for source, out in ((up_in, up_out), (down_in, down_out)):
        out[:span] = source[0]
        out[span:] = jnp.zeros((out.shape[0] - span, out.shape[1]), BF)


def slots_to_send(dealing, me, cotangent):
    slots, span, width = cotangent.shape
    tile = 512
    out = pl.BlockSpec((span + 8, tile), lambda j, dealing, me: (0, j))

    def source(by):
        return pl.BlockSpec(
            (1, span, tile),
            lambda j, dealing, me: (slot_taken(dealing, me[0], slots, me[0] + by), 0, j),
        )

    shape = jax.ShapeDtypeStruct((span + 8, width), BF)
    return pl.pallas_call(
        part_kernel,
        grid_spec=pltpu.PrefetchScalarGridSpec(
            num_scalar_prefetch=2,
            grid=(width // tile,),
            in_specs=[source(1), source(-1)],
            out_specs=[out, out],
        ),
        out_shape=[shape, shape],
        compiler_params=pltpu.CompilerParams(vmem_limit_bytes=VMEM),
        cost_estimate=COST,
        name="slots_to_send",
    )(dealing, me, cotangent, cotangent)


def arrive_kernel(slots, count, span, lengths_ref, dealing_ref, me_ref, own_ref, low_ref, high_ref, out_ref, picks):
    @pl.when(pl.program_id(0) == 0)
    def _():
        me = me_ref[0]
        starts = starts_of(lengths_ref, me, slots)
        row = lax.broadcasted_iota(jnp.int32, (picks.shape[0], 1), 0)
        index = jnp.zeros_like(row)
        for j in range(slots):
            far, slot = holder_of(dealing_ref, me, slots, count, me * slots + j)
            base = jnp.where(far == 0, slot * span, jnp.where(far < 0, slots * span, (slots + 1) * span))
            index = jnp.where(row >= starts[j], base + row - starts[j], index)
        column = lax.broadcasted_iota(jnp.int32, picks.shape, 1)
        picks[...] = jnp.where(column == index, 1.0, 0.0).astype(BF)

    out_ref[...] = (
        dot_nn(picks[:, : slots * span], own_ref[...])
        + dot_nn(picks[:, slots * span : (slots + 1) * span], low_ref[:span])
        + dot_nn(picks[:, (slots + 1) * span :], high_ref[:span])
    ).astype(BF)


def cotangent_arrived(lengths, dealing, me, own, low, high, rows):
    slots, span, width = own.shape
    own = own.reshape(slots * span, width)
    tile = 512
    column = lambda n: pl.BlockSpec((n, tile), lambda j, *s: (0, j))
    return pl.pallas_call(
        functools.partial(arrive_kernel, slots, dealing.shape[0], span),
        grid_spec=pltpu.PrefetchScalarGridSpec(
            num_scalar_prefetch=3,
            grid=(width // tile,),
            in_specs=[column(own.shape[0]), column(low.shape[0]), column(high.shape[0])],
            out_specs=column(rows),
            scratch_shapes=[pltpu.VMEM((rows, (slots + 2) * span), BF)],
        ),
        out_shape=jax.ShapeDtypeStruct((rows, width), BF),
        compiler_params=pltpu.CompilerParams(vmem_limit_bytes=VMEM),
        cost_estimate=COST,
        name="cotangent_arrived",
    )(lengths, dealing, me, own, low, high)


def deal_kernel(
    slots, count, span, lengths_ref, dealing_ref, me_ref, hidden_ref, upper_ref, lower_ref, other_upper_ref, other_lower_ref,
    own_ref, up_ref, down_ref, picks,
):
    @pl.when(pl.program_id(0) == 0)
    def _():
        me = me_ref[0]
        starts = starts_of(lengths_ref, me, slots)

        def zone(chosen):
            start, length = jnp.int32(0), jnp.int32(0)
            for j in range(slots):
                start = jnp.where(chosen[j], starts[j], start)
                length = jnp.where(chosen[j], lengths_ref[me, j], length)
            return start, length

        held = [dealing_ref[me * slots + k] for k in range(slots)]
        far = [holder_of(dealing_ref, me, slots, count, me * slots + j)[0] for j in range(slots)]
        zones = [zone([held[k] == me * slots + j for j in range(slots)]) for k in range(slots)]
        zones.append(zone([far[j] == 1 for j in range(slots)]))
        zones.append(zone([far[j] == -1 for j in range(slots)]))
        row = lax.broadcasted_iota(jnp.int32, (picks.shape[0], 1), 0)
        index = jnp.full_like(row, -1)
        for k, (start, length) in enumerate(zones):
            offset = row - k * span
            index = jnp.where((offset >= 0) & (offset < length), start + offset, index)
        column = lax.broadcasted_iota(jnp.int32, picks.shape, 1)
        picks[...] = jnp.where(column == index, 1.0, 0.0).astype(BF)

    share = jnp.concatenate([upper_ref[...], lower_ref[...]], axis=0).astype(F32)
    other = jnp.concatenate([other_upper_ref[...], other_lower_ref[...]], axis=0).astype(F32)
    final = hidden_ref[...] + (share + other)
    out = dot_nn(picks[...], final.astype(BF)).astype(BF)
    own_ref[...] = out[: slots * span]
    up_ref[...] = out[slots * span : (slots + 1) * span]
    down_ref[...] = out[(slots + 1) * span :]


def rows_dealt(lengths, dealing, me, hidden, shares, slots, span):
    rows, width = hidden.shape
    tile = 512
    column = lambda n: pl.BlockSpec((n, tile), lambda j, *s: (0, j))
    return pl.pallas_call(
        functools.partial(deal_kernel, slots, dealing.shape[0], span),
        grid_spec=pltpu.PrefetchScalarGridSpec(
            num_scalar_prefetch=3,
            grid=(width // tile,),
            in_specs=[column(rows)] + [column(rows // 2)] * 4,
            out_specs=[column(slots * span), column(span), column(span)],
            scratch_shapes=[pltpu.VMEM(((slots + 2) * span, rows), BF)],
        ),
        out_shape=[
            jax.ShapeDtypeStruct((slots * span, width), BF),
            jax.ShapeDtypeStruct((span, width), BF),
            jax.ShapeDtypeStruct((span, width), BF),
        ],
        compiler_params=pltpu.CompilerParams(vmem_limit_bytes=VMEM),
        cost_estimate=COST,
        name="rows_dealt",
    )(lengths, dealing, me, hidden, *shares)


def norm_kernel(tokens_ref, gain_ref, normed_ref, turned_ref):
    data = tokens_ref[...].astype(F32)
    inverse = lax.rsqrt(jnp.mean(data * data, axis=1, keepdims=True) + EPSILON)
    normed = (data * inverse * gain_ref[...]).astype(BF)
    normed_ref[...] = normed
    turned_ref[...] = normed.T


def first_norm(tokens, gain, tile=128):
    rows, width = tokens.shape
    flat = pl.BlockSpec((tile, width), lambda i: (i, 0))
    return pl.pallas_call(
        norm_kernel,
        grid=(rows // tile,),
        in_specs=[flat, pl.BlockSpec((1, width), lambda i: (0, 0))],
        out_specs=[flat, pl.BlockSpec((width, tile), lambda i: (0, i))],
        out_shape=[
            jax.ShapeDtypeStruct((rows, width), BF),
            jax.ShapeDtypeStruct((width, rows), BF),
        ],
        compiler_params=pltpu.CompilerParams(vmem_limit_bytes=VMEM),
        cost_estimate=COST,
        name="first_norm",
    )(tokens, gain[None, :])


def shares_of(halves_of, step_count):
    upper, lower, other_upper, other_lower = halves_of
    above = pl.program_id(0) < step_count // 2
    one = jnp.where(above, upper[...], lower[...]).astype(F32)
    return one + jnp.where(above, other_upper[...], other_lower[...]).astype(F32)


def half_specs(rows, tile, width):
    half = rows // 2 // tile
    above = pl.BlockSpec((tile, width), lambda i: (jnp.minimum(i, half - 1), 0))
    below = pl.BlockSpec((tile, width), lambda i: (jnp.maximum(i - half, 0), 0))
    return [above, below, above, below]


def hidden_kernel(steps, tokens_ref, *refs):
    shares, (gain_ref, hidden_ref, normed_ref) = refs[:4], refs[4:]
    hidden_body(tokens_ref, shares_of(shares, steps), gain_ref, hidden_ref, normed_ref)


def hidden_body(tokens_ref, share, gain_ref, hidden_ref, normed_ref):
    hidden = tokens_ref[...].astype(F32) + share
    inverse = lax.rsqrt(jnp.mean(hidden * hidden, axis=1, keepdims=True) + EPSILON)
    normed = (hidden * inverse * gain_ref[...]).astype(BF)
    hidden_ref[...] = hidden
    normed_ref[...] = normed


def hidden_and_norm(tokens, shares, gain, tile=128):
    rows, width = tokens.shape
    flat = pl.BlockSpec((tile, width), lambda i: (i, 0))
    return pl.pallas_call(
        functools.partial(hidden_kernel, rows // tile),
        grid=(rows // tile,),
        in_specs=[flat] + half_specs(rows, tile, width) + [pl.BlockSpec((1, width), lambda i: (0, 0))],
        out_specs=[flat, flat],
        out_shape=[
            jax.ShapeDtypeStruct((rows, width), F32),
            jax.ShapeDtypeStruct((rows, width), BF),
        ],
        compiler_params=pltpu.CompilerParams(vmem_limit_bytes=VMEM),
        cost_estimate=COST,
        name="hidden_and_norm",
    )(tokens, *shares, gain[None, :])


def norm_back(d_normed, source, gain):
    inverse = lax.rsqrt(jnp.mean(source * source, axis=1, keepdims=True) + EPSILON)
    scaled = d_normed * gain
    back = inverse * scaled - source * (inverse * inverse * inverse) * jnp.mean(
        scaled * source, axis=1, keepdims=True
    )
    return back, jnp.sum(d_normed * source * inverse, axis=0, keepdims=True)


def accumulate(ref, value):
    @pl.when(pl.program_id(0) == 0)
    def _():
        ref[...] = value

    @pl.when(pl.program_id(0) > 0)
    def _():
        ref[...] += value


def branch_kernel(
    steps, upper_ref, lower_ref, other_upper_ref, other_lower_ref, hidden_ref, d_final_ref, gain_ref, out_ref,
    d_hidden_ref, d_branch_ref, d_mixed_ref, d_gain_ref,
):
    share = shares_of((upper_ref, lower_ref, other_upper_ref, other_lower_ref), steps)
    back, d_gain = norm_back(share, hidden_ref[...], gain_ref[...])
    accumulate(d_gain_ref, d_gain)
    d_hidden = d_final_ref[...].astype(F32) + back
    d_hidden_ref[...] = d_hidden
    d_branch = d_hidden.astype(BF)
    d_branch_ref[...] = d_branch
    d_mixed_ref[...] = dot_nt(d_branch, out_ref[...]).astype(BF)


def branch_back(shares, hidden, d_final, gain, w_out, tile=128):
    rows, width = hidden.shape
    channels = w_out.shape[0]
    flat = pl.BlockSpec((tile, width), lambda i: (i, 0))
    line = pl.BlockSpec((1, width), lambda i: (0, 0))
    return pl.pallas_call(
        functools.partial(branch_kernel, rows // tile),
        grid=(rows // tile,),
        in_specs=half_specs(rows, tile, width)
        + [flat, flat, line, pl.BlockSpec((channels, width), lambda i: (0, 0))],
        out_specs=[
            flat,
            flat,
            pl.BlockSpec((tile, channels), lambda i: (i, 0)),
            line,
        ],
        out_shape=[
            jax.ShapeDtypeStruct((rows, width), F32),
            jax.ShapeDtypeStruct((rows, width), BF),
            jax.ShapeDtypeStruct((rows, channels), BF),
            jax.ShapeDtypeStruct((1, width), F32),
        ],
        compiler_params=pltpu.CompilerParams(vmem_limit_bytes=VMEM),
        cost_estimate=COST,
        name="branch_back",
    )(*shares, hidden, d_final, gain[None, :], w_out)


def input_kernel(
    steps, upper_ref, lower_ref, other_upper_ref, other_lower_ref, tokens_ref, d_hidden_ref, gain_ref, taps_ref, ffn_ref, logit_ref, out_ref, small_ref
):
    tokens = tokens_ref[...].astype(F32)
    gain = gain_ref[...]
    taps, heads = taps_ref.shape[0], logit_ref.shape[0]
    share = shares_of((upper_ref, lower_ref, other_upper_ref, other_lower_ref), steps)
    back, d_gain = norm_back(share, tokens, gain)
    out_ref[...] = (d_hidden_ref[...] + back).astype(BF)
    inverse = lax.rsqrt(jnp.mean(tokens * tokens, axis=1, keepdims=True) + EPSILON)
    d_beta = dot_nn(logit_ref[...].astype(BF), (tokens * inverse * gain).astype(BF))

    @pl.when(pl.program_id(0) == 0)
    def _():
        small_ref[...] = jnp.zeros_like(small_ref)
        small_ref[0:taps, 0 : taps_ref.shape[1]] = taps_ref[...]
        small_ref[taps : taps + 1, :] = ffn_ref[...]

    small_ref[taps + 1 : taps + 2, :] += d_gain
    small_ref[taps + 2 : taps + 2 + heads, :] += d_beta


def input_back(shares, tokens, d_hidden, gain, g_taps, g_ffn_gain, d_logit, tile=128):
    rows, width = tokens.shape
    flat = pl.BlockSpec((tile, width), lambda i: (i, 0))
    line = pl.BlockSpec((1, width), lambda i: (0, 0))
    height = -(-(g_taps.shape[0] + 2 + d_logit.shape[0]) // 8) * 8
    return pl.pallas_call(
        functools.partial(input_kernel, rows // tile),
        grid=(rows // tile,),
        in_specs=half_specs(rows, tile, width)
        + [flat, flat, line]
        + [
            pl.BlockSpec(g_taps.shape, lambda i: (0, 0)),
            line,
            pl.BlockSpec((d_logit.shape[0], tile), lambda i: (0, i)),
        ],
        out_specs=[flat, pl.BlockSpec((height, width), lambda i: (0, 0))],
        out_shape=[
            jax.ShapeDtypeStruct((rows, width), BF),
            jax.ShapeDtypeStruct((height, width), F32),
        ],
        compiler_params=pltpu.CompilerParams(vmem_limit_bytes=VMEM),
        cost_estimate=COST,
        name="input_back",
    )(*shares, tokens, d_hidden, gain[None, :], g_taps, g_ffn_gain, d_logit)


def product_kernel(count, turned, small, *refs):
    lefts, weights = refs[:count], refs[count : 2 * count]
    upper_ref, lower_ref = refs[-2:]
    dot = dot_nt if turned else dot_nn
    out = dot(lefts[0][...], weights[0][...])
    for left, weight in zip(lefts[1:], weights[1:]):
        out = out + dot(left[...], weight[...])
    if small:
        out = out + lax.dot_general(
            refs[2 * count][...].astype(BF), refs[2 * count + 1][...], (((0,), (1,)), ((), ())),
            preferred_element_type=F32,
        )
    half = out.shape[0] // 2
    upper_ref[...] = out[:half].astype(BF)
    lower_ref[...] = out[half:].astype(BF)


def product(lefts, weights, turned, small=(), tile=512):
    width = weights[0].shape[0 if turned else 1]
    whole = lambda x: pl.BlockSpec(x.shape, lambda j: (0, 0))
    left_specs, arrays = [], []
    for left in lefts:
        if isinstance(left, tuple):
            array, index = left
            rows = array.shape[1]
            left_specs.append(
                pl.BlockSpec((None,) + array.shape[1:], lambda j, index=index: (index, 0, 0))
            )
            arrays.append(array)
        else:
            rows = left.shape[0]
            left_specs.append(whole(left))
            arrays.append(left)
    if turned:
        parts = [pl.BlockSpec((tile, w.shape[1]), lambda j: (j, 0)) for w in weights]
    else:
        parts = [pl.BlockSpec((w.shape[0], tile), lambda j: (0, j)) for w in weights]
    more = [whole(small[0]), pl.BlockSpec((tile, small[1].shape[1]), lambda j: (j, 0))] if small else []
    return pl.pallas_call(
        functools.partial(product_kernel, len(lefts), turned, bool(small)),
        grid=(width // tile,),
        in_specs=left_specs + parts + more,
        out_specs=[pl.BlockSpec((rows // 2, tile), lambda j: (0, j))] * 2,
        out_shape=[jax.ShapeDtypeStruct((rows // 2, width), BF)] * 2,
        compiler_params=pltpu.CompilerParams(vmem_limit_bytes=VMEM),
        cost_estimate=COST,
        name="product",
    )(*arrays, *weights, *small)


def fold_kernel(plan, *refs):
    count = 1 + max(out for out, _, _, _ in plan)
    ins, outs = refs[:-count], refs[-count:]
    for out, start, width, terms in plan:
        part = None
        for ref, column in terms:
            term = ins[ref][:, column : column + width].astype(F32)
            part = term if part is None else part + term
        outs[out][:, start : start + width] = part.astype(outs[out].dtype)


def fold(outs, height, dtype):
    step = height
    while step % 2 == 0 and step > 96 and (step // 2) % 8 == 0:
        step //= 2
    arrays, plan, widths = [], [], []
    for out, streams in enumerate(outs):
        start = 0
        for width, terms in streams:
            places = []
            for array, row, column in terms:
                known = [i for i, (a, r) in enumerate(arrays) if a is array and r == row]
                if not known:
                    arrays.append((array, row))
                places.append((known[0] if known else len(arrays) - 1, column))
            plan.append((out, start, width, places))
            start += width
        widths.append(start)
    return pl.pallas_call(
        functools.partial(fold_kernel, plan),
        grid=(height // step,),
        in_specs=[
            pl.BlockSpec((step, array.shape[1]), lambda i, r=row // step: (r + i, 0))
            for array, row in arrays
        ],
        out_specs=[pl.BlockSpec((step, width), lambda i: (i, 0)) for width in widths],
        out_shape=[jax.ShapeDtypeStruct((height, width), dtype) for width in widths],
        compiler_params=pltpu.CompilerParams(vmem_limit_bytes=VMEM),
        cost_estimate=MORE,
        name="fold",
    )(*[array for array, _ in arrays])


def added_kernel(a_ref, b_ref, out_ref):
    out_ref[...] = a_ref[...] + b_ref[...]


def added(a, b):
    return pl.pallas_call(
        added_kernel,
        out_shape=jax.ShapeDtypeStruct(a.shape, a.dtype),
        compiler_params=pltpu.CompilerParams(vmem_limit_bytes=VMEM),
        cost_estimate=COST,
        name="added",
    )(a, b)


def pack(left, order_ref, turned, packed, first=0):
    size, block, _ = turned.shape
    around = left.T
    for i in range(size):
        turned[i] = around[i * block : (i + 1) * block]
    for i in range(packed.shape[0] // block):
        packed[i * block : (i + 1) * block, :] = turned[order_ref[first + i]]


def wgrad_kernel(plan, order_ref, *refs):
    lefts, rights = refs[: len(refs) - 3 - len(plan)], refs[len(refs) - 3 - len(plan) : -3]
    out_ref, turned, packed = refs[-3:]
    step = pl.program_id(0)

    @pl.when(step == 0)
    def _():
        for part, left_ref in enumerate(lefts):
            pack(left_ref[...], order_ref, turned, packed.at[part])

    for (part, first, steps), right_ref in zip(plan, rights):

        @pl.when((step >= first) & (step < first + steps))
        def _(right_ref=right_ref, part=part):
            out_ref[...] = dot_nn(packed[part], right_ref[...]).astype(out_ref.dtype)


def wgrad(order, size, parts, tile=512):
    count = order.shape[0]
    lefts = [left for left, _ in parts]
    rights = [right for _, several in parts for right in several]
    tokens, width = lefts[0].shape
    block = width // size
    tile = next(t for t in (tile, 384, 256, 128) if all(r.shape[1] % t == 0 for r in rights))
    plan, first = [], 0
    for part, (_, several) in enumerate(parts):
        for right in several:
            plan.append((part, first, right.shape[1] // tile))
            first += right.shape[1] // tile
    return pl.pallas_call(
        functools.partial(wgrad_kernel, plan),
        grid_spec=pltpu.PrefetchScalarGridSpec(
            num_scalar_prefetch=1,
            grid=(first,),
            in_specs=[pl.BlockSpec(left.shape, lambda j, order: (0, 0)) for left in lefts]
            + [
                pl.BlockSpec(
                    (tokens, tile), lambda j, order, s=s, n=n: (0, jnp.clip(j - s, 0, n - 1))
                )
                for _, s, n in plan
            ],
            out_specs=pl.BlockSpec((count * block, tile), lambda j, order: (0, j)),
            scratch_shapes=[
                pltpu.VMEM((size, block, tokens), BF),
                pltpu.VMEM((len(lefts), count * block, tokens), BF),
            ],
        ),
        out_shape=jax.ShapeDtypeStruct((count * block, first * tile), BF),
        compiler_params=pltpu.CompilerParams(vmem_limit_bytes=VMEM),
        cost_estimate=COST,
        name="wgrad",
    )(order, *lefts, *rights)


def plane_kernel(order_ref, left_ref, right_ref, out_ref):
    total = dot_nn(left_ref[0], right_ref[0])
    for i in range(1, left_ref.shape[0]):
        total = total + dot_nn(left_ref[i], right_ref[i])
    out_ref[...] = total.astype(out_ref.dtype)


def wgrad_plane(order, left, right, blocks):
    parts, width, tokens = left.shape
    columns = right.shape[2]
    height = width // blocks
    return pl.pallas_call(
        plane_kernel,
        grid_spec=pltpu.PrefetchScalarGridSpec(
            num_scalar_prefetch=1,
            grid=(order.shape[0],),
            in_specs=[
                pl.BlockSpec((parts, height, tokens), lambda j, order: (0, order[j], 0)),
                pl.BlockSpec(right.shape, lambda j, order: (0, 0, 0)),
            ],
            out_specs=pl.BlockSpec((height, columns), lambda j, order: (j, 0)),
        ),
        out_shape=jax.ShapeDtypeStruct((order.shape[0] * height, columns), BF),
        compiler_params=pltpu.CompilerParams(vmem_limit_bytes=VMEM),
        cost_estimate=COST,
        name="wgrad_plane",
    )(order, left, right)


def ffn_kernel(
    order_ref, normed_ref, d_final_ref, gate_ref, up_ref, down_ref,
    inner_ref, d_gate_ref, d_up_ref, g_gate_ref, g_up_ref, turned, packed, packed_up,
):

    @pl.when(pl.program_id(0) == 0)
    def _():
        pack(normed_ref[...], order_ref, turned, packed)
        pack(normed_ref[...], order_ref, turned, packed_up, turned.shape[0])

    gate = dot_nn(normed_ref[...], gate_ref[...])
    lift = dot_nn(normed_ref[...], up_ref[...])
    d_inner = dot_nt(d_final_ref[...], down_ref[...])
    sig = jax.nn.sigmoid(gate)
    silu = gate * sig
    inner_ref[...] = (silu * lift).astype(BF)
    d_gate = (d_inner * lift * sig * (1.0 + gate * (1.0 - sig))).astype(BF)
    d_up = (d_inner * silu).astype(BF)
    d_gate_ref[...] = d_gate
    d_up_ref[...] = d_up
    g_gate_ref[...] = dot_nn(packed[...], d_gate).astype(BF)
    g_up_ref[...] = dot_nn(packed_up[...], d_up).astype(BF)


def ffn(order, size, normed, d_final, w_gate, w_up, w_down, tile=512):
    rows, width = normed.shape
    units = w_gate.shape[1]
    whole = pl.BlockSpec((rows, width), lambda j, order: (0, 0))
    column = pl.BlockSpec((width, tile), lambda j, order: (0, j))
    out = pl.BlockSpec((rows, tile), lambda j, order: (0, j))
    shape = jax.ShapeDtypeStruct((rows, units), BF)
    grad = jax.ShapeDtypeStruct((width, units), BF)
    return pl.pallas_call(
        ffn_kernel,
        grid_spec=pltpu.PrefetchScalarGridSpec(
            num_scalar_prefetch=1,
            grid=(units // tile,),
            in_specs=[
                whole,
                whole,
                column,
                column,
                pl.BlockSpec((tile, width), lambda j, order: (j, 0)),
            ],
            out_specs=[out, out, out, column, column],
            scratch_shapes=[
                pltpu.VMEM((size, width // size, rows), BF),
                pltpu.VMEM((width, rows), BF),
                pltpu.VMEM((width, rows), BF),
            ],
        ),
        out_shape=[shape, shape, shape, grad, grad],
        compiler_params=pltpu.CompilerParams(vmem_limit_bytes=VMEM),
        cost_estimate=COST,
        name="ffn",
    )(order, normed, d_final, w_gate, w_up, w_down)


def swap(x, axis, bit):
    size = lax.axis_size(axis)
    return lax.ppermute(x, axis, [(i, i ^ (1 << bit)) for i in range(size)])


def flips_of(count, bits):
    flips = []
    for position in reversed(range(count)):
        flips.append(
            sum(((position >> (len(bits) - 1 - rank)) & 1) << bit for rank, bit in enumerate(bits))
        )
    return jnp.array(flips, jnp.int32)


def halve(terms, bits):
    for bit in bits:
        half = terms[0].shape[0] // 2
        out = sum(t[:half].astype(F32) for t in terms).astype(BF)
        terms = [t[half:] for t in terms] + [swap(out, "dp", bit)]
    return terms


def total(terms):
    return sum(t.astype(F32) for t in terms)


def after(value, *others):
    return lax.optimization_barrier((value,) + others)[0]


class Order:
    def __init__(self):
        self.last = ()

    def gate(self, *values):
        if self.last:
            values = lax.optimization_barrier(tuple(values) + self.last)[: len(values)]
        return values if len(values) > 1 else values[0]

    def mark(self, *values):
        self.last = values
        return values if len(values) > 1 else values[0]


def stream(*arrays):
    return arrays[0].shape[1], [(array, 0, 0) for array in arrays]


def joined(streams, got):
    column, out = 0, []
    for width, terms in streams:
        out.append((width, terms + [(got, 0, column)]))
        column += width
    return out


def on_device(
    tokens,
    cotangent,
    lengths,
    dealing,
    attn_gain,
    w_query,
    w_key,
    w_value,
    w_house,
    w_beta,
    conv_taps,
    w_out,
    ffn_gain,
    w_gate,
    w_up,
    w_down,
):
    rows, width = tokens.shape
    slots, span = cotangent.shape[:2]
    size = lax.axis_size("dp")
    me = lax.axis_index("dp").astype(jnp.int32)
    me1 = me.reshape(1)
    block = width // size
    bits = list(range(size.bit_length() - 1))
    plane, line = bits[:2], bits[2:]
    up = [(i, i + 1) for i in range(size - 1)]
    down = [(i + 1, i) for i in range(size - 1)]
    first = size // 2
    groups = [[i + j for j in range(4)] for i in range(0, size, 4)]
    order_line = (me >> 2) ^ flips_of(size // 4, [b - 2 for b in line])
    order_plane = (jnp.arange(4, dtype=jnp.int32)[:, None] + 4 * order_line[None, :]).reshape(-1)
    order_natural = (
        jnp.arange(4, dtype=jnp.int32)[:, None] + jnp.arange(0, size, 4, dtype=jnp.int32)[None, :]
    ).reshape(-1)
    line_groups = [[i + j for j in range(0, size, 4)] for i in range(4)]
    order_zxy = me ^ flips_of(size, line + plane)
    order_xyz = me ^ flips_of(size, bits)
    order = Order()

    cot_up, cot_down = order.mark(*slots_to_send(dealing, me1, cotangent))
    cot_low = lax.ppermute(cot_up, "dp", up)
    cot_high = lax.ppermute(cot_down, "dp", down)

    normed1, normed1_t = order.mark(*first_norm(order.gate(tokens), attn_gain))
    plane_normed = lax.all_gather(normed1_t, "dp", axis_index_groups=groups)
    normed = order.gate(normed1)
    logit = lax.dot_general(
        w_beta, normed, (((0,), (1,)), ((), ())), preferred_element_type=F32
    )
    query = dot_nn(normed, w_query).astype(BF)
    key = dot_nn(normed, w_key).astype(BF)
    value = dot_nn(normed, w_value).astype(BF)
    house = dot_nn(normed, w_house)
    order.mark(query, key, value, house, logit)
    mixed, kept = order.mark(
        *mixer_forward(lengths, me1, logit, conv_taps, house, order.gate(query), key, value)
    )

    def shares(parts):
        others = [swap(part, "tensor", 0) for part in parts]
        return lambda: [*parts, *order.gate(*others)]

    attn_shares = shares(order.mark(*product([order.gate(mixed)], [w_out], False)))
    hidden, normed2 = order.mark(*hidden_and_norm(tokens, attn_shares(), ffn_gain))
    d_final = order.mark(
        cotangent_arrived(
            lengths, dealing, me1, cotangent, *order.gate(cot_low, cot_high), rows
        )
    )

    def gated(outs):
        arrays = []
        for streams in outs:
            for _, terms in streams:
                for array, _, _ in terms:
                    if not any(array is known for known in arrays):
                        arrays.append(array)
        after = order.gate(*arrays)
        after = list(after) if isinstance(after, tuple) else [after]
        new = lambda array: next(n for a, n in zip(arrays, after) if a is array)
        return [
            [(w, [(new(array), r, c) for array, r, c in terms]) for w, terms in streams]
            for streams in outs
        ]

    def leave(streams, height, bit):
        (streams,) = gated([streams])
        got = swap(order.mark(fold([streams], height, BF)[0]), "dp", bit)
        return joined([(w, [(a, r + height, c) for a, r, c in terms]) for w, terms in streams], got)

    def finish(outs):
        out = fold(gated(outs), block, F32)
        order.mark(out[0])
        return out

    def wgrad_of(rows_order, left, rights):
        return order.mark(
            wgrad(rows_order, size, [(left, [order.gate(rights[0])] + list(rights[1:]))])
        )

    half, quarter = width // 2, width // 4
    columns = query.shape[1]
    heights = [quarter >> (i + 1) for i in range(len(line))]
    lines = size // 4

    def plane_sum(x):
        return lax.psum_scatter(
            x, "dp", scatter_dimension=0, tiled=True, axis_index_groups=groups
        )

    inner, d_gate, d_up, gate_all, up_all = order.mark(
        *ffn(
            jnp.concatenate([order_plane, order_natural]),
            size, order.gate(normed2), d_final, w_gate, w_up, w_down,
        )
    )
    gate_sum, up_sum = plane_sum(gate_all), plane_sum(up_all)
    down_leave = wgrad_of(order_zxy[:first], d_final, [inner])
    down_got = swap(down_leave, "dp", line[0])
    d_norm2_shares = shares(order.mark(*product([order.gate(d_gate), d_up], [w_gate, w_up], True)))
    down_stay = wgrad_of(order_zxy[first:], d_final, [inner])
    downs = [stream(down_stay, down_got)]
    plane_normed = order.mark(order.gate(plane_normed))
    d_hidden, d_branch, d_mixed, g_ffn_gain = order.mark(
        *branch_back(d_norm2_shares(), hidden, d_final, ffn_gain, w_out)
    )
    out_leave = wgrad_of(order_xyz[:first], d_branch, [mixed])
    out_got = swap(out_leave, "dp", 0)

    d_four, d_logit, g_taps = order.mark(
        *mixer_backward(
            lengths, me1, logit, conv_taps, house, query, key, value, order.gate(d_mixed), kept
        )
    )
    plane_four = lax.all_to_all(d_four, "dp", 0, 0, axis_index_groups=groups)
    out_stay = wgrad_of(order_xyz[first:], d_branch, [mixed])
    height = half
    for bit in line[1:]:
        height //= 2
        downs = leave(downs, height, bit)
    d_norm1_shares = shares(
        order.mark(
            *product(
                [(order.gate(d_four), i) for i in range(4)],
                [w_query, w_key, w_value, w_house], True, small=(d_logit, w_beta),
            )
        )
    )
    down_shares = shares(order.mark(*product([order.gate(inner)], [w_down], False)))
    gates = leave([stream(gate_sum)], heights[0], line[0])
    input_grad, small = order.mark(
        *input_back(
            d_norm1_shares(), tokens, d_hidden, attn_gain, g_taps, g_ffn_gain, d_logit
        )
    )
    small_bits, small_got = list(bits), None

    def small_step():
        nonlocal small, small_got
        if small_got is not None:
            small = order.mark(added(small, order.gate(small_got)))
        small_got = swap(small, "dp", small_bits.pop(0)) if small_bits else None

    small_step()
    attn_leave = order.mark(
        wgrad_plane(order_line[: lines // 2], plane_normed, order.gate(plane_four), lines)
    )
    attn_got = swap(attn_leave, "dp", line[0])
    attn_stay = order.mark(
        wgrad_plane(order_line[lines // 2 :], plane_normed, order.gate(plane_four), lines)
    )
    attns = [stream(attn_stay, attn_got)]
    for low, bit in zip(heights[1:], line[1:]):
        gates = leave(gates, low, bit)
    outs = leave([stream(out_stay, out_got)], quarter, 1)
    dealt, deal_up, deal_down = order.mark(
        *rows_dealt(lengths, dealing, me1, hidden, down_shares(), slots, span)
    )
    small_step()
    height //= 2
    downs = leave(downs, height, 0)
    attn_height = half
    for bit in line[1:]:
        attn_height //= 2
        attns = leave(attns, attn_height, bit)
    (g_gate,) = finish([gates])
    small_step()
    outs = leave(outs, heights[0], line[0])
    up_sum = order.mark(order.gate(up_sum))
    up_line = lax.psum_scatter(
        up_sum, "dp", scatter_dimension=0, tiled=True, axis_index_groups=line_groups
    )
    out_low = lax.ppermute(deal_up, "dp", up)
    out_high = lax.ppermute(deal_down, "dp", down)
    height //= 2
    downs = leave(downs, height, 1)
    attn_sum = order.mark(fold(gated([attns]), width // lines, BF)[0])
    plane_rows = lax.all_to_all(
        attn_sum.reshape(4, block, columns), "dp", 0, 0, axis_index_groups=groups
    )
    for low, bit in zip(heights[1:], line[1:]):
        outs = leave(outs, low, bit)
    (g_down,) = finish([downs])
    out_low, out_high = order.mark(*order.gate(out_low, out_high))
    while small_got is not None:
        small_step()
    (g_out,) = finish([outs])
    g_up = order.gate(up_line).astype(F32)
    g_query, g_key, g_value, g_house = order.gate(plane_rows).astype(F32)

    taps = conv_taps.shape[0]
    per_row = lax.dynamic_slice_in_dim(small[taps:], me * block, block, axis=1)
    taps_total = small[:taps, :columns]
    held_from = lax.dynamic_slice_in_dim(dealing, me * slots, slots) // slots - me
    output = jnp.where(
        (held_from == -1)[:, None, None],
        out_low[None],
        jnp.where(
            (held_from == 1)[:, None, None], out_high[None], dealt.reshape(slots, span, width)
        ),
    )
    return (
        output,
        input_grad,
        per_row[1],
        g_query,
        g_key,
        g_value,
        g_house,
        per_row[2 : 2 + d_logit.shape[0]].T,
        taps_total,
        g_out.T,
        per_row[0],
        g_gate,
        g_up,
        g_down.T,
    )


def solution(mesh):
    in_specs = (
        P("dp", None),
        P("dp", None, None),
        P(),
        P(),
        P(),
        P(None, "tensor"),
        P(None, "tensor"),
        P(None, "tensor"),
        P(None, "tensor"),
        P(None, "tensor"),
        P(None, "tensor"),
        P("tensor", None),
        P(),
        P(None, "tensor"),
        P(None, "tensor"),
        P("tensor", None),
    )
    out_specs = (
        P("dp", None, None),
        P("dp", None),
        P("dp"),
        P("dp", "tensor"),
        P("dp", "tensor"),
        P("dp", "tensor"),
        P("dp", "tensor"),
        P("dp", "tensor"),
        P(None, "tensor"),
        P("tensor", "dp"),
        P("dp"),
        P("dp", "tensor"),
        P("dp", "tensor"),
        P("tensor", "dp"),
    )
    return jax.shard_map(
        on_device, mesh=mesh, in_specs=in_specs, out_specs=out_specs, check_vma=False
    )
```

```python
import functools
import jax
import jax.numpy as jnp
from jax import lax
from jax.experimental import pallas as pl
from jax.experimental.pallas import tpu as pltpu
from jax.sharding import PartitionSpec as P

EPSILON = 1e-06
BF = jnp.bfloat16
F32 = jnp.float32

VMEM = 60 << 20
COST = pl.CostEstimate(flops=0, bytes_accessed=0, transcendentals=0)
MORE = pl.CostEstimate(flops=1_000_000_000, bytes_accessed=1_000_000, transcendentals=0)


def dot_nn(a, b):
    return lax.dot_general(a, b, (((1,), (0,)), ((), ())), preferred_element_type=F32)


def dot_nt(a, b):
    return lax.dot_general(a, b, (((1,), (1,)), ((), ())), preferred_element_type=F32)


def dot_tn(a, b):
    return lax.dot_general(a, b, (((0,), (0,)), ((), ())), preferred_element_type=F32)


def halves(x):
    high = x.astype(BF)
    return high, (x - high.astype(F32)).astype(BF)


def split_product(a, b):
    return dot_nn(a[0], b[0]) + (dot_nn(a[0], b[1]) + dot_nn(a[1], b[0]))


def unit_lower_inverses(stricts, base):
    size, lanes = stricts[0].shape[0], 128
    tiles, per_tile = size // lanes, lanes // base
    lane = lax.broadcasted_iota(jnp.int32, (base, lanes), 1)
    row = lax.broadcasted_iota(jnp.int32, (base, lanes), 0)
    owner, within = lane // base, lane % base
    pieces = [
        strict[t * lanes : (t + 1) * lanes, t * lanes : (t + 1) * lanes]
        for strict in stricts
        for t in range(tiles)
    ]
    compact = []
    for piece in pieces:
        packed = jnp.zeros((base, lanes), F32)
        for block in range(per_tile):
            packed = jnp.where(owner == block, piece[block * base : (block + 1) * base], packed)
        compact.append(packed)
    solved = [jnp.where(row == within, 1.0, 0.0).astype(F32)] * len(pieces)
    for step in range(base - 1):
        index = owner * base + step
        solved = [
            s - jnp.take_along_axis(c, index, axis=1) * s[step : step + 1, :]
            for s, c in zip(solved, compact)
        ]
    inverses = [
        jnp.concatenate([jnp.where(owner == b, s, 0.0) for b in range(per_tile)], axis=0)
        for s in solved
    ]
    grown = base * 2
    row = lax.broadcasted_iota(jnp.int32, (lanes, lanes), 0)
    col = lax.broadcasted_iota(jnp.int32, (lanes, lanes), 1)
    while grown <= lanes:
        joined = (row // grown == col // grown) & (row // (grown // 2) != col // (grown // 2))
        parts = [halves(i) for i in inverses]
        crosses = [halves(jnp.where(joined, p, 0.0)) for p in pieces]
        firsts = [halves(split_product(p, c)) for p, c in zip(parts, crosses)]
        inverses = [i - split_product(f, p) for i, f, p in zip(inverses, firsts, parts)]
        grown *= 2
    whole = []
    parts = [halves(i) for i in inverses]
    corners = [halves(strict[lanes:, :lanes]) for strict in stricts]
    firsts = [halves(split_product(parts[2 * n + 1], c)) for n, c in enumerate(corners)]
    for n, first in enumerate(firsts):
        corner = -split_product(first, parts[2 * n])
        top = jnp.concatenate([inverses[2 * n], jnp.zeros((lanes, lanes), F32)], axis=1)
        whole.append(
            jnp.concatenate([top, jnp.concatenate([corner, inverses[2 * n + 1]], axis=1)], axis=0)
        )
    return whole


def shifted_rows(x, amount, place):
    return jnp.where(place >= amount, pltpu.roll(x, amount, 0), 0.0)


def direction(house, taps, place):
    conv = taps[0:1, :] * house
    for shift in range(1, taps.shape[0]):
        conv = conv + taps[shift : shift + 1, :] * shifted_rows(house, shift, place)
    inverse = lax.rsqrt(jnp.sum(conv * conv, axis=1, keepdims=True) + EPSILON)
    return conv, inverse


PAIRS = ((0, 0), (1, 0), (1, 1))


def masks_of(begin, half, a, b):
    inside = lax.broadcasted_iota(jnp.int32, (half, half), 1) + b * half >= begin[
        a * half : (a + 1) * half
    ]
    if a != b:
        return inside, inside
    col = lax.broadcasted_iota(jnp.int32, (half, half), 1)
    row = lax.broadcasted_iota(jnp.int32, (half, half), 0)
    return inside & (col <= row), inside & (col < row)


def scores_of(query, key, house_dir, begin, half, a, b):
    rows, cols = slice(a * half, (a + 1) * half), slice(b * half, (b + 1) * half)
    left = jnp.concatenate([query[rows], house_dir[rows]], axis=0)
    right = jnp.concatenate([key[cols], house_dir[cols]], axis=0)
    every = dot_nt(left, right)
    col = lax.broadcasted_iota(jnp.int32, (half, half), 1) + b * half
    row = lax.broadcasted_iota(jnp.int32, (half, half), 0) + a * half
    inside = col >= begin[rows]
    upto = inside & (col <= row)
    before = inside & (col < row)
    return (
        every[:half, :half],
        jnp.where(upto, every[:half, half:], 0.0),
        jnp.where(before, every[half:, :half], 0.0),
        jnp.where(before, every[half:, half:], 0.0),
        upto,
        before,
    )


def forward_heads(items, begin, place):
    half = items[0][0].shape[0] // 2
    scaling = items[0][0].shape[1] ** (-0.5)
    both = (slice(0, half), slice(half, 2 * half))
    upto, before = {}, {}
    for a, b in PAIRS:
        upto[a, b], before[a, b] = masks_of(begin, half, a, b)
    heads = []
    for query, key, value, house, logit, taps in items:
        conv, inverse = direction(house, taps, place)
        house_dir = (conv * inverse).astype(BF)
        beta = 2.0 * jax.nn.sigmoid(logit)
        cross, know, gram = {}, {}, {}
        for a, b in PAIRS:
            left = jnp.concatenate([query[both[a]], house_dir[both[a]]], axis=0)
            every = dot_nt(left, house_dir[both[b]])
            beta_cols = beta[:, both[b]]
            cross[a, b] = jnp.where(upto[a, b], every[:half] * -beta_cols, 0.0).astype(BF)
            gram[a, b] = jnp.where(before[a, b], every[half:] * beta_cols, 0.0)
            know[a, b] = jnp.where(
                before[a, b], dot_nt(house_dir[both[a]], key[both[b]]), 0.0
            )
        heads.append((cross, know, gram, query, key.T, value))
    inverses = unit_lower_inverses([h[2][a, a] for h in heads for a in (0, 1)], 16)
    eye = (
        lax.broadcasted_iota(jnp.int32, (half, half), 0)
        == lax.broadcasted_iota(jnp.int32, (half, half), 1)
    )
    tails = [jnp.where(eye, 0.0, i).astype(BF) for i in inverses]
    results = []
    for n, (cross, know, gram, query, key_t, value) in enumerate(heads):
        tail0, tail1 = tails[2 * n : 2 * n + 2]
        z00 = (know[0, 0] + dot_nn(tail0, know[0, 0].astype(BF))).astype(BF)
        z11 = (know[1, 1] + dot_nn(tail1, know[1, 1].astype(BF))).astype(BF)
        rest = know[1, 0] - dot_nn(gram[1, 0].astype(BF), z00)
        z10 = (rest + dot_nn(tail1, rest.astype(BF))).astype(BF)

        def score(pair, lefts, rights):
            out = dot_nn(jnp.concatenate(lefts, axis=1), jnp.concatenate(rights, axis=0))
            return jnp.where(upto[pair], out * scaling, -1e30)

        q0, q1 = query[both[0]], query[both[1]]
        s00 = score((0, 0), [q0, cross[0, 0]], [key_t[:, both[0]], z00])
        s10 = score((1, 0), [q1, cross[1, 0], cross[1, 1]], [key_t[:, both[0]], z00, z10])
        s11 = score((1, 1), [q1, cross[1, 1]], [key_t[:, both[1]], z11])
        top0 = jnp.max(s00, axis=1, keepdims=True)
        top1 = jnp.maximum(
            jnp.max(s10, axis=1, keepdims=True), jnp.max(s11, axis=1, keepdims=True)
        )
        e00, e10, e11 = jnp.exp(s00 - top0), jnp.exp(s10 - top1), jnp.exp(s11 - top1)
        inv0 = 1.0 / jnp.sum(e00, axis=1, keepdims=True)
        inv1 = 1.0 / (jnp.sum(e10, axis=1, keepdims=True) + jnp.sum(e11, axis=1, keepdims=True))
        p00, p10, p11 = (e00 * inv0).astype(BF), (e10 * inv1).astype(BF), (e11 * inv1).astype(BF)
        mixed0 = dot_nn(p00, value[both[0]])
        mixed1 = dot_nn(jnp.concatenate([p10, p11], axis=1), value)
        mixed = jnp.concatenate([mixed0, mixed1], axis=0).astype(BF)
        results.append((mixed, (p00, p10, p11, z00, z10, z11, tail0, tail1)))
    return results


def forward_kernel(heads, slots, lengths_ref, me_ref, logit_ref, taps_ref, house_ref, q_ref, k_ref, v_ref, mixed_ref, kept_ref):
    step = pl.program_id(0)
    rows = q_ref.shape[0]
    row = lax.broadcasted_iota(jnp.int32, (rows, 1), 0)
    begin = begins(starts_of(lengths_ref, me_ref[0], slots), row)
    place = row - begin
    columns = [slice(head * 128, (head + 1) * 128) for head in range(heads)]
    items = [
        (
            q_ref[:, cols], k_ref[:, cols], v_ref[:, cols], house_ref[:, cols],
            logit_ref[pl.ds(step * heads + head, 1), :], taps_ref[:, cols],
        )
        for head, cols in enumerate(columns)
    ]
    for head, (mixed, kept) in enumerate(forward_heads(items, begin, place)):
        mixed_ref[:, columns[head]] = mixed
        for slot, item in enumerate(kept):
            kept_ref[head, slot] = item


def mixer_forward(lengths, me, logit, taps, house, query, key, value, heads=2):
    rows, width = query.shape
    count = width // 128
    half = rows // 2
    wide = pl.BlockSpec((rows, heads * 128), lambda i: (0, i))
    return pl.pallas_call(
        functools.partial(forward_kernel, heads, lengths.shape[1]),
        grid=(count // heads,),
        in_specs=[
            pl.BlockSpec(memory_space=pltpu.SMEM),
            pl.BlockSpec(memory_space=pltpu.SMEM),
            pl.BlockSpec(logit.shape, lambda i: (0, 0)),
            pl.BlockSpec((taps.shape[0], heads * 128), lambda i: (0, i)),
            wide, wide, wide, wide,
        ],
        out_specs=[wide, pl.BlockSpec((heads, 8, half, half), lambda i: (i, 0, 0, 0))],
        out_shape=[
            jax.ShapeDtypeStruct((rows, width), BF),
            jax.ShapeDtypeStruct((count, 8, half, half), BF),
        ],
        compiler_params=pltpu.CompilerParams(vmem_limit_bytes=VMEM),
        cost_estimate=COST,
        name="mixer_forward",
    )(lengths, me, logit, taps, house, query, key, value)


def backward_head(query, key, value, house, logit, taps, begin, place, d_mixed, kept):
    p00, p10, p11, z00, z10, z11, tail0, tail1 = kept
    rows = query.shape[0]
    half = rows // 2
    scaling = query.shape[1] ** (-0.5)
    conv, inverse = direction(house, taps, place)
    direct = conv * inverse
    house_dir = direct.astype(BF)
    beta = 2.0 * jax.nn.sigmoid(logit)
    cross, cross_b, gram, gram_raw, upto, before, beta_cols = {}, {}, {}, {}, {}, {}, {}
    for a, b in PAIRS:
        _, cross[a, b], _, gram_raw[a, b], upto[a, b], before[a, b] = scores_of(
            query, key, house_dir, begin, half, a, b
        )
        beta_cols[b] = beta[:, b * half : (b + 1) * half]
        cross_b[a, b] = (cross[a, b] * beta_cols[b]).astype(BF)
    gram10 = (gram_raw[1, 0] * beta_cols[0]).astype(BF)
    d0, d1 = d_mixed[:half], d_mixed[half:]
    v0, v1 = value[:half], value[half:]
    dp00, dp10, dp11 = dot_nt(d0, v0), dot_nt(d1, v0), dot_nt(d1, v1)
    dv0 = dot_tn(p00, d0) + dot_tn(p10, d1)
    dv1 = dot_tn(p11, d1)
    f00, f10, f11 = p00.astype(F32), p10.astype(F32), p11.astype(F32)
    mean0 = jnp.sum(f00 * dp00, axis=1, keepdims=True)
    mean1 = jnp.sum(f10 * dp10, axis=1, keepdims=True) + jnp.sum(f11 * dp11, axis=1, keepdims=True)
    ds = {
        (0, 0): (f00 * (dp00 - mean0) * scaling).astype(BF),
        (1, 0): (f10 * (dp10 - mean1) * scaling).astype(BF),
        (1, 1): (f11 * (dp11 - mean1) * scaling).astype(BF),
    }
    dx = {
        (0, 0): dot_nt(ds[0, 0], z00),
        (1, 0): dot_nt(ds[1, 0], z00),
        (1, 1): dot_nt(ds[1, 1], z11) + dot_nt(ds[1, 0], z10),
    }
    dz00 = dot_tn(cross_b[0, 0], ds[0, 0]) + dot_tn(cross_b[1, 0], ds[1, 0])
    dz10 = dot_tn(cross_b[1, 1], ds[1, 0])
    dz11 = dot_tn(cross_b[1, 1], ds[1, 1])
    e11 = dz11 + dot_tn(tail1, dz11.astype(BF))
    e10 = dz10 + dot_tn(tail1, dz10.astype(BF))
    rest = dz00 - dot_tn(gram10, e10.astype(BF))
    e00 = rest + dot_tn(tail0, rest.astype(BF))
    e00b, e10b, e11b = e00.astype(BF), e10.astype(BF), e11.astype(BF)
    dn = {
        (0, 0): dot_nt(e00b, z00),
        (1, 0): dot_nt(e10b, z00),
        (1, 1): dot_nt(e10b, z10) + dot_nt(e11b, z11),
    }
    dy = {(0, 0): e00, (1, 0): e10, (1, 1): e11}
    d_beta = [jnp.zeros((1, half), F32), jnp.zeros((1, half), F32)]
    d_q = [0.0, 0.0]
    d_w = [0.0, 0.0]
    d_k = [0.0, 0.0]
    for a, b in PAIRS:
        part_x = jnp.where(upto[a, b], -dx[a, b], 0.0)
        part_n = jnp.where(before[a, b], dn[a, b], 0.0)
        part_y = jnp.where(before[a, b], -dy[a, b], 0.0)
        d_beta[b] = d_beta[b] + jnp.sum(
            part_x * cross[a, b] + part_n * gram_raw[a, b], axis=0, keepdims=True
        )
        upper = jnp.concatenate([ds[a, b], (part_x * beta_cols[b]).astype(BF)], axis=1)
        lower = jnp.concatenate([part_y.astype(BF), (part_n * beta_cols[b]).astype(BF)], axis=1)
        big = jnp.concatenate([upper, lower], axis=0)
        rows_a, cols_b = slice(a * half, (a + 1) * half), slice(b * half, (b + 1) * half)
        right = jnp.concatenate([key[cols_b], house_dir[cols_b]], axis=0)
        left = jnp.concatenate([query[rows_a], house_dir[rows_a]], axis=0)
        by_row = dot_nn(big, right)
        by_col = dot_tn(big, left)
        d_q[a] = d_q[a] + by_row[:half]
        d_w[a] = d_w[a] + by_row[half:]
        d_k[b] = d_k[b] + by_col[:half]
        d_w[b] = d_w[b] + by_col[half:]
    d_dir = jnp.concatenate(d_w, axis=0)
    d_conv = inverse * d_dir - direct * (
        inverse * jnp.sum(direct * d_dir, axis=1, keepdims=True)
    )
    d_house = taps[0:1, :] * d_conv
    d_taps = [jnp.sum(d_conv * house, axis=0, keepdims=True)]
    for shift in range(1, taps.shape[0]):
        live = jnp.where(place >= shift, d_conv, 0.0)
        d_house = d_house + taps[shift : shift + 1, :] * pltpu.roll(live, rows - shift, 0)
        d_taps.append(jnp.sum(live * pltpu.roll(house, shift, 0), axis=0, keepdims=True))
    d_logit = jnp.concatenate(d_beta, axis=1) * beta * (1.0 - 0.5 * beta)
    return (
        jnp.concatenate(d_q, axis=0).astype(BF),
        jnp.concatenate(d_k, axis=0).astype(BF),
        jnp.concatenate([dv0, dv1], axis=0).astype(BF),
        d_house.astype(BF),
        d_logit,
        d_taps,
    )


def backward_kernel(
    heads, slots, lengths_ref, me_ref, logit_ref, taps_ref, house_ref, q_ref, k_ref, v_ref, dm_ref, kept_ref,
    four_ref, dl_ref, dt_ref,
):
    step = pl.program_id(0)
    rows = q_ref.shape[0]
    row = lax.broadcasted_iota(jnp.int32, (rows, 1), 0)
    begin = begins(starts_of(lengths_ref, me_ref[0], slots), row)
    place = row - begin
    for head in range(heads):
        cols = slice(head * 128, (head + 1) * 128)
        logit = logit_ref[pl.ds(step * heads + head, 1), :]
        kept = tuple(kept_ref[head, slot] for slot in range(8))
        d_q, d_k, d_v, d_h, d_l, d_t = backward_head(
            q_ref[:, cols], k_ref[:, cols], v_ref[:, cols], house_ref[:, cols], logit,
            taps_ref[:, cols], begin, place, dm_ref[:, cols], kept,
        )
        for slot, item in enumerate((d_q, d_k, d_v, d_h)):
            four_ref[slot, :, cols] = item
        dl_ref[pl.ds(step * heads + head, 1), :] = d_l
        for tap, item in enumerate(d_t):
            dt_ref[tap : tap + 1, cols] = item


def mixer_backward(lengths, me, logit, taps, house, query, key, value, d_mixed, kept, heads=2):
    rows, width = query.shape
    count = width // 128
    half = rows // 2
    wide = pl.BlockSpec((rows, heads * 128), lambda i: (0, i))
    narrow = pl.BlockSpec((taps.shape[0], heads * 128), lambda i: (0, i))
    whole = pl.BlockSpec(logit.shape, lambda i: (0, 0))
    return pl.pallas_call(
        functools.partial(backward_kernel, heads, lengths.shape[1]),
        grid=(count // heads,),
        in_specs=[
            pl.BlockSpec(memory_space=pltpu.SMEM),
            pl.BlockSpec(memory_space=pltpu.SMEM),
            whole, narrow, wide, wide, wide, wide, wide,
            pl.BlockSpec((heads, 8, half, half), lambda i: (i, 0, 0, 0)),
        ],
        out_specs=[pl.BlockSpec((4, rows, heads * 128), lambda i: (0, 0, i)), whole, narrow],
        out_shape=[
            jax.ShapeDtypeStruct((4, rows, width), BF),
            jax.ShapeDtypeStruct(logit.shape, F32),
            jax.ShapeDtypeStruct(taps.shape, F32),
        ],
        compiler_params=pltpu.CompilerParams(vmem_limit_bytes=VMEM),
        cost_estimate=COST,
        name="mixer_backward",
    )(lengths, me, logit, taps, house, query, key, value, d_mixed, kept)


def starts_of(lengths_ref, me, slots):
    starts, sum_so_far = [], 0
    for j in range(slots):
        starts.append(sum_so_far)
        sum_so_far = sum_so_far + lengths_ref[me, j]
    return starts


def begins(starts, row):
    begin = jnp.zeros_like(row)
    for start in starts[1:]:
        begin = jnp.where(row >= start, start, begin)
    return begin


def group_of(sequence, slots):
    return lax.div(sequence, jnp.int32(slots))


def slot_taken(dealing_ref, me, slots, group):
    found = jnp.int32(0)
    for k in range(slots):
        found = jnp.where(group_of(dealing_ref[me * slots + k], slots) == group, k, found)
    return found


def holder_of(dealing_ref, me, slots, count, sequence):
    far, slot = jnp.int32(0), jnp.int32(0)
    for by in (-1, 0, 1):
        for k in range(slots):
            position = (me + by) * slots + k
            inside = (position >= 0) & (position < count)
            hit = inside & (dealing_ref[jnp.clip(position, 0, count - 1)] == sequence)
            far = jnp.where(hit, by, far)
            slot = jnp.where(hit, k, slot)
    return far, slot


def part_kernel(dealing_ref, me_ref, up_in, down_in, up_out, down_out):
    span = up_in.shape[1]
    for source, out in ((up_in, up_out), (down_in, down_out)):
        out[:span] = source[0]
        out[span:] = jnp.zeros((out.shape[0] - span, out.shape[1]), BF)


def slots_to_send(dealing, me, cotangent):
    slots, span, width = cotangent.shape
    tile = 512
    out = pl.BlockSpec((span + 8, tile), lambda j, dealing, me: (0, j))

    def source(by):
        return pl.BlockSpec(
            (1, span, tile),
            lambda j, dealing, me: (slot_taken(dealing, me[0], slots, me[0] + by), 0, j),
        )

    shape = jax.ShapeDtypeStruct((span + 8, width), BF)
    return pl.pallas_call(
        part_kernel,
        grid_spec=pltpu.PrefetchScalarGridSpec(
            num_scalar_prefetch=2,
            grid=(width // tile,),
            in_specs=[source(1), source(-1)],
            out_specs=[out, out],
        ),
        out_shape=[shape, shape],
        compiler_params=pltpu.CompilerParams(vmem_limit_bytes=VMEM),
        cost_estimate=COST,
        name="slots_to_send",
    )(dealing, me, cotangent, cotangent)


def arrive_kernel(slots, count, span, lengths_ref, dealing_ref, me_ref, own_ref, low_ref, high_ref, out_ref, picks):
    @pl.when(pl.program_id(0) == 0)
    def _():
        me = me_ref[0]
        starts = starts_of(lengths_ref, me, slots)
        row = lax.broadcasted_iota(jnp.int32, (picks.shape[0], 1), 0)
        index = jnp.zeros_like(row)
        for j in range(slots):
            far, slot = holder_of(dealing_ref, me, slots, count, me * slots + j)
            base = jnp.where(far == 0, slot * span, jnp.where(far < 0, slots * span, (slots + 1) * span))
            index = jnp.where(row >= starts[j], base + row - starts[j], index)
        column = lax.broadcasted_iota(jnp.int32, picks.shape, 1)
        picks[...] = jnp.where(column == index, 1.0, 0.0).astype(BF)

    out_ref[...] = (
        dot_nn(picks[:, : slots * span], own_ref[...])
        + dot_nn(picks[:, slots * span : (slots + 1) * span], low_ref[:span])
        + dot_nn(picks[:, (slots + 1) * span :], high_ref[:span])
    ).astype(BF)


def cotangent_arrived(lengths, dealing, me, own, low, high, rows):
    slots, span, width = own.shape
    own = own.reshape(slots * span, width)
    tile = 512
    column = lambda n: pl.BlockSpec((n, tile), lambda j, *s: (0, j))
    return pl.pallas_call(
        functools.partial(arrive_kernel, slots, dealing.shape[0], span),
        grid_spec=pltpu.PrefetchScalarGridSpec(
            num_scalar_prefetch=3,
            grid=(width // tile,),
            in_specs=[column(own.shape[0]), column(low.shape[0]), column(high.shape[0])],
            out_specs=column(rows),
            scratch_shapes=[pltpu.VMEM((rows, (slots + 2) * span), BF)],
        ),
        out_shape=jax.ShapeDtypeStruct((rows, width), BF),
        compiler_params=pltpu.CompilerParams(vmem_limit_bytes=VMEM),
        cost_estimate=COST,
        name="cotangent_arrived",
    )(lengths, dealing, me, own, low, high)


def deal_kernel(
    slots, count, span, lengths_ref, dealing_ref, me_ref, hidden_ref, upper_ref, lower_ref, other_upper_ref, other_lower_ref,
    own_ref, up_ref, down_ref, picks,
):
    @pl.when(pl.program_id(0) == 0)
    def _():
        me = me_ref[0]
        starts = starts_of(lengths_ref, me, slots)

        def zone(chosen):
            start, length = jnp.int32(0), jnp.int32(0)
            for j in range(slots):
                start = jnp.where(chosen[j], starts[j], start)
                length = jnp.where(chosen[j], lengths_ref[me, j], length)
            return start, length

        held = [dealing_ref[me * slots + k] for k in range(slots)]
        far = [holder_of(dealing_ref, me, slots, count, me * slots + j)[0] for j in range(slots)]
        zones = [zone([held[k] == me * slots + j for j in range(slots)]) for k in range(slots)]
        zones.append(zone([far[j] == 1 for j in range(slots)]))
        zones.append(zone([far[j] == -1 for j in range(slots)]))
        row = lax.broadcasted_iota(jnp.int32, (picks.shape[0], 1), 0)
        index = jnp.full_like(row, -1)
        for k, (start, length) in enumerate(zones):
            offset = row - k * span
            index = jnp.where((offset >= 0) & (offset < length), start + offset, index)
        column = lax.broadcasted_iota(jnp.int32, picks.shape, 1)
        picks[...] = jnp.where(column == index, 1.0, 0.0).astype(BF)

    share = jnp.concatenate([upper_ref[...], lower_ref[...]], axis=0).astype(F32)
    other = jnp.concatenate([other_upper_ref[...], other_lower_ref[...]], axis=0).astype(F32)
    final = hidden_ref[...] + (share + other)
    out = dot_nn(picks[...], final.astype(BF)).astype(BF)
    own_ref[...] = out[: slots * span]
    up_ref[...] = out[slots * span : (slots + 1) * span]
    down_ref[...] = out[(slots + 1) * span :]


def rows_dealt(lengths, dealing, me, hidden, shares, slots, span):
    rows, width = hidden.shape
    tile = 512
    column = lambda n: pl.BlockSpec((n, tile), lambda j, *s: (0, j))
    return pl.pallas_call(
        functools.partial(deal_kernel, slots, dealing.shape[0], span),
        grid_spec=pltpu.PrefetchScalarGridSpec(
            num_scalar_prefetch=3,
            grid=(width // tile,),
            in_specs=[column(rows)] + [column(rows // 2)] * 4,
            out_specs=[column(slots * span), column(span), column(span)],
            scratch_shapes=[pltpu.VMEM(((slots + 2) * span, rows), BF)],
        ),
        out_shape=[
            jax.ShapeDtypeStruct((slots * span, width), BF),
            jax.ShapeDtypeStruct((span, width), BF),
            jax.ShapeDtypeStruct((span, width), BF),
        ],
        compiler_params=pltpu.CompilerParams(vmem_limit_bytes=VMEM),
        cost_estimate=COST,
        name="rows_dealt",
    )(lengths, dealing, me, hidden, *shares)


def norm_kernel(tokens_ref, gain_ref, normed_ref, turned_ref):
    data = tokens_ref[...].astype(F32)
    inverse = lax.rsqrt(jnp.mean(data * data, axis=1, keepdims=True) + EPSILON)
    normed = (data * inverse * gain_ref[...]).astype(BF)
    normed_ref[...] = normed
    turned_ref[...] = normed.T


def first_norm(tokens, gain, tile=128):
    rows, width = tokens.shape
    flat = pl.BlockSpec((tile, width), lambda i: (i, 0))
    return pl.pallas_call(
        norm_kernel,
        grid=(rows // tile,),
        in_specs=[flat, pl.BlockSpec((1, width), lambda i: (0, 0))],
        out_specs=[flat, pl.BlockSpec((width, tile), lambda i: (0, i))],
        out_shape=[
            jax.ShapeDtypeStruct((rows, width), BF),
            jax.ShapeDtypeStruct((width, rows), BF),
        ],
        compiler_params=pltpu.CompilerParams(vmem_limit_bytes=VMEM),
        cost_estimate=COST,
        name="first_norm",
    )(tokens, gain[None, :])


def shares_of(halves_of, step_count):
    upper, lower, other_upper, other_lower = halves_of
    above = pl.program_id(0) < step_count // 2
    one = jnp.where(above, upper[...], lower[...]).astype(F32)
    return one + jnp.where(above, other_upper[...], other_lower[...]).astype(F32)


def half_specs(rows, tile, width):
    half = rows // 2 // tile
    above = pl.BlockSpec((tile, width), lambda i: (jnp.minimum(i, half - 1), 0))
    below = pl.BlockSpec((tile, width), lambda i: (jnp.maximum(i - half, 0), 0))
    return [above, below, above, below]


def hidden_kernel(steps, tokens_ref, *refs):
    shares, (gain_ref, hidden_ref, normed_ref) = refs[:4], refs[4:]
    hidden_body(tokens_ref, shares_of(shares, steps), gain_ref, hidden_ref, normed_ref)


def hidden_body(tokens_ref, share, gain_ref, hidden_ref, normed_ref):
    hidden = tokens_ref[...].astype(F32) + share
    inverse = lax.rsqrt(jnp.mean(hidden * hidden, axis=1, keepdims=True) + EPSILON)
    normed = (hidden * inverse * gain_ref[...]).astype(BF)
    hidden_ref[...] = hidden
    normed_ref[...] = normed


def hidden_and_norm(tokens, shares, gain, tile=128):
    rows, width = tokens.shape
    flat = pl.BlockSpec((tile, width), lambda i: (i, 0))
    return pl.pallas_call(
        functools.partial(hidden_kernel, rows // tile),
        grid=(rows // tile,),
        in_specs=[flat] + half_specs(rows, tile, width) + [pl.BlockSpec((1, width), lambda i: (0, 0))],
        out_specs=[flat, flat],
        out_shape=[
            jax.ShapeDtypeStruct((rows, width), F32),
            jax.ShapeDtypeStruct((rows, width), BF),
        ],
        compiler_params=pltpu.CompilerParams(vmem_limit_bytes=VMEM),
        cost_estimate=COST,
        name="hidden_and_norm",
    )(tokens, *shares, gain[None, :])


def norm_back(d_normed, source, gain):
    inverse = lax.rsqrt(jnp.mean(source * source, axis=1, keepdims=True) + EPSILON)
    scaled = d_normed * gain
    back = inverse * scaled - source * (inverse * inverse * inverse) * jnp.mean(
        scaled * source, axis=1, keepdims=True
    )
    return back, jnp.sum(d_normed * source * inverse, axis=0, keepdims=True)


def accumulate(ref, value):
    @pl.when(pl.program_id(0) == 0)
    def _():
        ref[...] = value

    @pl.when(pl.program_id(0) > 0)
    def _():
        ref[...] += value


def branch_kernel(
    steps, upper_ref, lower_ref, other_upper_ref, other_lower_ref, hidden_ref, d_final_ref, gain_ref, out_ref,
    d_hidden_ref, d_branch_ref, d_mixed_ref, d_gain_ref,
):
    share = shares_of((upper_ref, lower_ref, other_upper_ref, other_lower_ref), steps)
    back, d_gain = norm_back(share, hidden_ref[...], gain_ref[...])
    accumulate(d_gain_ref, d_gain)
    d_hidden = d_final_ref[...].astype(F32) + back
    d_hidden_ref[...] = d_hidden
    d_branch = d_hidden.astype(BF)
    d_branch_ref[...] = d_branch
    d_mixed_ref[...] = dot_nt(d_branch, out_ref[...]).astype(BF)


def branch_back(shares, hidden, d_final, gain, w_out, tile=128):
    rows, width = hidden.shape
    channels = w_out.shape[0]
    flat = pl.BlockSpec((tile, width), lambda i: (i, 0))
    line = pl.BlockSpec((1, width), lambda i: (0, 0))
    return pl.pallas_call(
        functools.partial(branch_kernel, rows // tile),
        grid=(rows // tile,),
        in_specs=half_specs(rows, tile, width)
        + [flat, flat, line, pl.BlockSpec((channels, width), lambda i: (0, 0))],
        out_specs=[
            flat,
            flat,
            pl.BlockSpec((tile, channels), lambda i: (i, 0)),
            line,
        ],
        out_shape=[
            jax.ShapeDtypeStruct((rows, width), F32),
            jax.ShapeDtypeStruct((rows, width), BF),
            jax.ShapeDtypeStruct((rows, channels), BF),
            jax.ShapeDtypeStruct((1, width), F32),
        ],
        compiler_params=pltpu.CompilerParams(vmem_limit_bytes=VMEM),
        cost_estimate=COST,
        name="branch_back",
    )(*shares, hidden, d_final, gain[None, :], w_out)


def input_kernel(
    steps, upper_ref, lower_ref, other_upper_ref, other_lower_ref, tokens_ref, d_hidden_ref, gain_ref, taps_ref, ffn_ref, logit_ref, out_ref, small_ref
):
    tokens = tokens_ref[...].astype(F32)
    gain = gain_ref[...]
    taps, heads = taps_ref.shape[0], logit_ref.shape[0]
    share = shares_of((upper_ref, lower_ref, other_upper_ref, other_lower_ref), steps)
    back, d_gain = norm_back(share, tokens, gain)
    out_ref[...] = (d_hidden_ref[...] + back).astype(BF)
    inverse = lax.rsqrt(jnp.mean(tokens * tokens, axis=1, keepdims=True) + EPSILON)
    d_beta = dot_nn(logit_ref[...].astype(BF), (tokens * inverse * gain).astype(BF))

    @pl.when(pl.program_id(0) == 0)
    def _():
        small_ref[...] = jnp.zeros_like(small_ref)
        small_ref[0:taps, 0 : taps_ref.shape[1]] = taps_ref[...]
        small_ref[taps : taps + 1, :] = ffn_ref[...]

    small_ref[taps + 1 : taps + 2, :] += d_gain
    small_ref[taps + 2 : taps + 2 + heads, :] += d_beta


def input_back(shares, tokens, d_hidden, gain, g_taps, g_ffn_gain, d_logit, tile=128):
    rows, width = tokens.shape
    flat = pl.BlockSpec((tile, width), lambda i: (i, 0))
    line = pl.BlockSpec((1, width), lambda i: (0, 0))
    height = -(-(g_taps.shape[0] + 2 + d_logit.shape[0]) // 8) * 8
    return pl.pallas_call(
        functools.partial(input_kernel, rows // tile),
        grid=(rows // tile,),
        in_specs=half_specs(rows, tile, width)
        + [flat, flat, line]
        + [
            pl.BlockSpec(g_taps.shape, lambda i: (0, 0)),
            line,
            pl.BlockSpec((d_logit.shape[0], tile), lambda i: (0, i)),
        ],
        out_specs=[flat, pl.BlockSpec((height, width), lambda i: (0, 0))],
        out_shape=[
            jax.ShapeDtypeStruct((rows, width), BF),
            jax.ShapeDtypeStruct((height, width), F32),
        ],
        compiler_params=pltpu.CompilerParams(vmem_limit_bytes=VMEM),
        cost_estimate=COST,
        name="input_back",
    )(*shares, tokens, d_hidden, gain[None, :], g_taps, g_ffn_gain, d_logit)


def product_kernel(count, turned, small, *refs):
    lefts, weights = refs[:count], refs[count : 2 * count]
    upper_ref, lower_ref = refs[-2:]
    dot = dot_nt if turned else dot_nn
    out = dot(lefts[0][...], weights[0][...])
    for left, weight in zip(lefts[1:], weights[1:]):
        out = out + dot(left[...], weight[...])
    if small:
        out = out + lax.dot_general(
            refs[2 * count][...].astype(BF), refs[2 * count + 1][...], (((0,), (1,)), ((), ())),
            preferred_element_type=F32,
        )
    half = out.shape[0] // 2
    upper_ref[...] = out[:half].astype(BF)
    lower_ref[...] = out[half:].astype(BF)


def product(lefts, weights, turned, small=(), tile=512):
    width = weights[0].shape[0 if turned else 1]
    whole = lambda x: pl.BlockSpec(x.shape, lambda j: (0, 0))
    left_specs, arrays = [], []
    for left in lefts:
        if isinstance(left, tuple):
            array, index = left
            rows = array.shape[1]
            left_specs.append(
                pl.BlockSpec((None,) + array.shape[1:], lambda j, index=index: (index, 0, 0))
            )
            arrays.append(array)
        else:
            rows = left.shape[0]
            left_specs.append(whole(left))
            arrays.append(left)
    if turned:
        parts = [pl.BlockSpec((tile, w.shape[1]), lambda j: (j, 0)) for w in weights]
    else:
        parts = [pl.BlockSpec((w.shape[0], tile), lambda j: (0, j)) for w in weights]
    more = [whole(small[0]), pl.BlockSpec((tile, small[1].shape[1]), lambda j: (j, 0))] if small else []
    return pl.pallas_call(
        functools.partial(product_kernel, len(lefts), turned, bool(small)),
        grid=(width // tile,),
        in_specs=left_specs + parts + more,
        out_specs=[pl.BlockSpec((rows // 2, tile), lambda j: (0, j))] * 2,
        out_shape=[jax.ShapeDtypeStruct((rows // 2, width), BF)] * 2,
        compiler_params=pltpu.CompilerParams(vmem_limit_bytes=VMEM),
        cost_estimate=COST,
        name="product",
    )(*arrays, *weights, *small)


def fold_kernel(plan, *refs):
    count = 1 + max(out for out, _, _, _ in plan)
    ins, outs = refs[:-count], refs[-count:]
    for out, start, width, terms in plan:
        part = None
        for ref, column in terms:
            term = ins[ref][:, column : column + width].astype(F32)
            part = term if part is None else part + term
        outs[out][:, start : start + width] = part.astype(outs[out].dtype)


def fold(outs, height, dtype):
    step = height
    while step % 2 == 0 and step > 96 and (step // 2) % 8 == 0:
        step //= 2
    arrays, plan, widths = [], [], []
    for out, streams in enumerate(outs):
        start = 0
        for width, terms in streams:
            places = []
            for array, row, column in terms:
                known = [i for i, (a, r) in enumerate(arrays) if a is array and r == row]
                if not known:
                    arrays.append((array, row))
                places.append((known[0] if known else len(arrays) - 1, column))
            plan.append((out, start, width, places))
            start += width
        widths.append(start)
    return pl.pallas_call(
        functools.partial(fold_kernel, plan),
        grid=(height // step,),
        in_specs=[
            pl.BlockSpec((step, array.shape[1]), lambda i, r=row // step: (r + i, 0))
            for array, row in arrays
        ],
        out_specs=[pl.BlockSpec((step, width), lambda i: (i, 0)) for width in widths],
        out_shape=[jax.ShapeDtypeStruct((height, width), dtype) for width in widths],
        compiler_params=pltpu.CompilerParams(vmem_limit_bytes=VMEM),
        cost_estimate=MORE,
        name="fold",
    )(*[array for array, _ in arrays])


def added_kernel(a_ref, b_ref, out_ref):
    out_ref[...] = a_ref[...] + b_ref[...]


def added(a, b):
    return pl.pallas_call(
        added_kernel,
        out_shape=jax.ShapeDtypeStruct(a.shape, a.dtype),
        compiler_params=pltpu.CompilerParams(vmem_limit_bytes=VMEM),
        cost_estimate=COST,
        name="added",
    )(a, b)


def pack(left, order_ref, turned, packed, first=0):
    size, block, _ = turned.shape
    around = left.T
    for i in range(size):
        turned[i] = around[i * block : (i + 1) * block]
    for i in range(packed.shape[0] // block):
        packed[i * block : (i + 1) * block, :] = turned[order_ref[first + i]]


def wgrad_kernel(plan, order_ref, *refs):
    lefts, rights = refs[: len(refs) - 3 - len(plan)], refs[len(refs) - 3 - len(plan) : -3]
    out_ref, turned, packed = refs[-3:]
    step = pl.program_id(0)

    @pl.when(step == 0)
    def _():
        for part, left_ref in enumerate(lefts):
            pack(left_ref[...], order_ref, turned, packed.at[part])

    for (part, first, steps), right_ref in zip(plan, rights):

        @pl.when((step >= first) & (step < first + steps))
        def _(right_ref=right_ref, part=part):
            out_ref[...] = dot_nn(packed[part], right_ref[...]).astype(out_ref.dtype)


def wgrad(order, size, parts, tile=512):
    count = order.shape[0]
    lefts = [left for left, _ in parts]
    rights = [right for _, several in parts for right in several]
    tokens, width = lefts[0].shape
    block = width // size
    tile = next(t for t in (tile, 384, 256, 128) if all(r.shape[1] % t == 0 for r in rights))
    plan, first = [], 0
    for part, (_, several) in enumerate(parts):
        for right in several:
            plan.append((part, first, right.shape[1] // tile))
            first += right.shape[1] // tile
    return pl.pallas_call(
        functools.partial(wgrad_kernel, plan),
        grid_spec=pltpu.PrefetchScalarGridSpec(
            num_scalar_prefetch=1,
            grid=(first,),
            in_specs=[pl.BlockSpec(left.shape, lambda j, order: (0, 0)) for left in lefts]
            + [
                pl.BlockSpec(
                    (tokens, tile), lambda j, order, s=s, n=n: (0, jnp.clip(j - s, 0, n - 1))
                )
                for _, s, n in plan
            ],
            out_specs=pl.BlockSpec((count * block, tile), lambda j, order: (0, j)),
            scratch_shapes=[
                pltpu.VMEM((size, block, tokens), BF),
                pltpu.VMEM((len(lefts), count * block, tokens), BF),
            ],
        ),
        out_shape=jax.ShapeDtypeStruct((count * block, first * tile), BF),
        compiler_params=pltpu.CompilerParams(vmem_limit_bytes=VMEM),
        cost_estimate=COST,
        name="wgrad",
    )(order, *lefts, *rights)


def plane_kernel(order_ref, left_ref, right_ref, out_ref):
    total = dot_nn(left_ref[0], right_ref[0])
    for i in range(1, left_ref.shape[0]):
        total = total + dot_nn(left_ref[i], right_ref[i])
    out_ref[...] = total.astype(out_ref.dtype)


def wgrad_plane(order, left, right, blocks):
    parts, width, tokens = left.shape
    columns = right.shape[2]
    height = width // blocks
    return pl.pallas_call(
        plane_kernel,
        grid_spec=pltpu.PrefetchScalarGridSpec(
            num_scalar_prefetch=1,
            grid=(order.shape[0],),
            in_specs=[
                pl.BlockSpec((parts, height, tokens), lambda j, order: (0, order[j], 0)),
                pl.BlockSpec(right.shape, lambda j, order: (0, 0, 0)),
            ],
            out_specs=pl.BlockSpec((height, columns), lambda j, order: (j, 0)),
        ),
        out_shape=jax.ShapeDtypeStruct((order.shape[0] * height, columns), BF),
        compiler_params=pltpu.CompilerParams(vmem_limit_bytes=VMEM),
        cost_estimate=COST,
        name="wgrad_plane",
    )(order, left, right)


def ffn_kernel(
    order_ref, normed_ref, d_final_ref, gate_ref, up_ref, down_ref,
    inner_ref, d_gate_ref, d_up_ref, g_gate_ref, g_up_ref, turned, packed, packed_up,
):

    @pl.when(pl.program_id(0) == 0)
    def _():
        pack(normed_ref[...], order_ref, turned, packed)
        pack(normed_ref[...], order_ref, turned, packed_up, turned.shape[0])

    gate = dot_nn(normed_ref[...], gate_ref[...])
    lift = dot_nn(normed_ref[...], up_ref[...])
    d_inner = dot_nt(d_final_ref[...], down_ref[...])
    sig = jax.nn.sigmoid(gate)
    silu = gate * sig
    inner_ref[...] = (silu * lift).astype(BF)
    d_gate = (d_inner * lift * sig * (1.0 + gate * (1.0 - sig))).astype(BF)
    d_up = (d_inner * silu).astype(BF)
    d_gate_ref[...] = d_gate
    d_up_ref[...] = d_up
    g_gate_ref[...] = dot_nn(packed[...], d_gate).astype(BF)
    g_up_ref[...] = dot_nn(packed_up[...], d_up).astype(BF)


def ffn(order, size, normed, d_final, w_gate, w_up, w_down, tile=512):
    rows, width = normed.shape
    units = w_gate.shape[1]
    whole = pl.BlockSpec((rows, width), lambda j, order: (0, 0))
    column = pl.BlockSpec((width, tile), lambda j, order: (0, j))
    out = pl.BlockSpec((rows, tile), lambda j, order: (0, j))
    shape = jax.ShapeDtypeStruct((rows, units), BF)
    grad = jax.ShapeDtypeStruct((width, units), BF)
    return pl.pallas_call(
        ffn_kernel,
        grid_spec=pltpu.PrefetchScalarGridSpec(
            num_scalar_prefetch=1,
            grid=(units // tile,),
            in_specs=[
                whole,
                whole,
                column,
                column,
                pl.BlockSpec((tile, width), lambda j, order: (j, 0)),
            ],
            out_specs=[out, out, out, column, column],
            scratch_shapes=[
                pltpu.VMEM((size, width // size, rows), BF),
                pltpu.VMEM((width, rows), BF),
                pltpu.VMEM((width, rows), BF),
            ],
        ),
        out_shape=[shape, shape, shape, grad, grad],
        compiler_params=pltpu.CompilerParams(vmem_limit_bytes=VMEM),
        cost_estimate=COST,
        name="ffn",
    )(order, normed, d_final, w_gate, w_up, w_down)


def swap(x, axis, bit):
    size = lax.axis_size(axis)
    return lax.ppermute(x, axis, [(i, i ^ (1 << bit)) for i in range(size)])


def flips_of(count, bits):
    flips = []
    for position in reversed(range(count)):
        flips.append(
            sum(((position >> (len(bits) - 1 - rank)) & 1) << bit for rank, bit in enumerate(bits))
        )
    return jnp.array(flips, jnp.int32)


def halve(terms, bits):
    for bit in bits:
        half = terms[0].shape[0] // 2
        out = sum(t[:half].astype(F32) for t in terms).astype(BF)
        terms = [t[half:] for t in terms] + [swap(out, "dp", bit)]
    return terms


def total(terms):
    return sum(t.astype(F32) for t in terms)


def after(value, *others):
    return lax.optimization_barrier((value,) + others)[0]


class Order:
    def __init__(self):
        self.last = ()

    def gate(self, *values):
        if self.last:
            values = lax.optimization_barrier(tuple(values) + self.last)[: len(values)]
        return values if len(values) > 1 else values[0]

    def mark(self, *values):
        self.last = values
        return values if len(values) > 1 else values[0]


def stream(*arrays):
    return arrays[0].shape[1], [(array, 0, 0) for array in arrays]


def joined(streams, got):
    column, out = 0, []
    for width, terms in streams:
        out.append((width, terms + [(got, 0, column)]))
        column += width
    return out


def on_device(
    tokens,
    cotangent,
    lengths,
    dealing,
    attn_gain,
    w_query,
    w_key,
    w_value,
    w_house,
    w_beta,
    conv_taps,
    w_out,
    ffn_gain,
    w_gate,
    w_up,
    w_down,
):
    rows, width = tokens.shape
    slots, span = cotangent.shape[:2]
    size = lax.axis_size("dp")
    me = lax.axis_index("dp").astype(jnp.int32)
    me1 = me.reshape(1)
    block = width // size
    bits = list(range(size.bit_length() - 1))
    plane, line = bits[:2], bits[2:]
    up = [(i, i + 1) for i in range(size - 1)]
    down = [(i + 1, i) for i in range(size - 1)]
    first = size // 2
    groups = [[i + j for j in range(4)] for i in range(0, size, 4)]
    order_line = (me >> 2) ^ flips_of(size // 4, [b - 2 for b in line])
    order_plane = (jnp.arange(4, dtype=jnp.int32)[:, None] + 4 * order_line[None, :]).reshape(-1)
    order_natural = (
        jnp.arange(4, dtype=jnp.int32)[:, None] + jnp.arange(0, size, 4, dtype=jnp.int32)[None, :]
    ).reshape(-1)
    line_groups = [[i + j for j in range(0, size, 4)] for i in range(4)]
    order_zxy = me ^ flips_of(size, line + plane)
    order_xyz = me ^ flips_of(size, bits)
    order = Order()

    cot_up, cot_down = order.mark(*slots_to_send(dealing, me1, cotangent))
    cot_low = lax.ppermute(cot_up, "dp", up)
    cot_high = lax.ppermute(cot_down, "dp", down)

    normed1, normed1_t = order.mark(*first_norm(order.gate(tokens), attn_gain))
    plane_normed = lax.all_gather(normed1_t, "dp", axis_index_groups=groups)
    normed = order.gate(normed1)
    logit = lax.dot_general(
        w_beta, normed, (((0,), (1,)), ((), ())), preferred_element_type=F32
    )
    query = dot_nn(normed, w_query).astype(BF)
    key = dot_nn(normed, w_key).astype(BF)
    value = dot_nn(normed, w_value).astype(BF)
    house = dot_nn(normed, w_house)
    order.mark(query, key, value, house, logit)
    mixed, kept = order.mark(
        *mixer_forward(lengths, me1, logit, conv_taps, house, order.gate(query), key, value)
    )

    def shares(parts):
        others = [swap(part, "tensor", 0) for part in parts]
        return lambda: [*parts, *order.gate(*others)]

    attn_shares = shares(order.mark(*product([order.gate(mixed)], [w_out], False)))
    hidden, normed2 = order.mark(*hidden_and_norm(tokens, attn_shares(), ffn_gain))
    d_final = order.mark(
        cotangent_arrived(
            lengths, dealing, me1, cotangent, *order.gate(cot_low, cot_high), rows
        )
    )

    def gated(outs):
        arrays = []
        for streams in outs:
            for _, terms in streams:
                for array, _, _ in terms:
                    if not any(array is known for known in arrays):
                        arrays.append(array)
        after = order.gate(*arrays)
        after = list(after) if isinstance(after, tuple) else [after]
        new = lambda array: next(n for a, n in zip(arrays, after) if a is array)
        return [
            [(w, [(new(array), r, c) for array, r, c in terms]) for w, terms in streams]
            for streams in outs
        ]

    def leave(streams, height, bit):
        (streams,) = gated([streams])
        got = swap(order.mark(fold([streams], height, BF)[0]), "dp", bit)
        return joined([(w, [(a, r + height, c) for a, r, c in terms]) for w, terms in streams], got)

    def finish(outs):
        out = fold(gated(outs), block, F32)
        order.mark(out[0])
        return out

    def wgrad_of(rows_order, left, rights):
        return order.mark(
            wgrad(rows_order, size, [(left, [order.gate(rights[0])] + list(rights[1:]))])
        )

    half, quarter = width // 2, width // 4
    columns = query.shape[1]
    heights = [quarter >> (i + 1) for i in range(len(line))]
    lines = size // 4

    def plane_sum(x):
        return lax.psum_scatter(
            x, "dp", scatter_dimension=0, tiled=True, axis_index_groups=groups
        )

    inner, d_gate, d_up, gate_all, up_all = order.mark(
        *ffn(
            jnp.concatenate([order_plane, order_natural]),
            size, order.gate(normed2), d_final, w_gate, w_up, w_down,
        )
    )
    gate_sum, up_sum = plane_sum(gate_all), plane_sum(up_all)
    down_leave = wgrad_of(order_zxy[:first], d_final, [inner])
    down_got = swap(down_leave, "dp", line[0])
    d_norm2_shares = shares(order.mark(*product([order.gate(d_gate), d_up], [w_gate, w_up], True)))
    down_stay = wgrad_of(order_zxy[first:], d_final, [inner])
    downs = [stream(down_stay, down_got)]
    plane_normed = order.mark(order.gate(plane_normed))
    d_hidden, d_branch, d_mixed, g_ffn_gain = order.mark(
        *branch_back(d_norm2_shares(), hidden, d_final, ffn_gain, w_out)
    )
    out_leave = wgrad_of(order_xyz[:first], d_branch, [mixed])
    out_got = swap(out_leave, "dp", 0)

    d_four, d_logit, g_taps = order.mark(
        *mixer_backward(
            lengths, me1, logit, conv_taps, house, query, key, value, order.gate(d_mixed), kept
        )
    )
    plane_four = lax.all_to_all(d_four, "dp", 0, 0, axis_index_groups=groups)
    out_stay = wgrad_of(order_xyz[first:], d_branch, [mixed])
    height = half
    for bit in line[1:]:
        height //= 2
        downs = leave(downs, height, bit)
    d_norm1_shares = shares(
        order.mark(
            *product(
                [(order.gate(d_four), i) for i in range(4)],
                [w_query, w_key, w_value, w_house], True, small=(d_logit, w_beta),
            )
        )
    )
    down_shares = shares(order.mark(*product([order.gate(inner)], [w_down], False)))
    gates = leave([stream(gate_sum)], heights[0], line[0])
    input_grad, small = order.mark(
        *input_back(
            d_norm1_shares(), tokens, d_hidden, attn_gain, g_taps, g_ffn_gain, d_logit
        )
    )
    small_bits, small_got = list(bits), None

    def small_step():
        nonlocal small, small_got
        if small_got is not None:
            small = order.mark(added(small, order.gate(small_got)))
        small_got = swap(small, "dp", small_bits.pop(0)) if small_bits else None

    small_step()
    attn_leave = order.mark(
        wgrad_plane(order_line[: lines // 2], plane_normed, order.gate(plane_four), lines)
    )
    attn_got = swap(attn_leave, "dp", line[0])
    attn_stay = order.mark(
        wgrad_plane(order_line[lines // 2 :], plane_normed, order.gate(plane_four), lines)
    )
    attns = [stream(attn_stay, attn_got)]
    for low, bit in zip(heights[1:], line[1:]):
        gates = leave(gates, low, bit)
    outs = leave([stream(out_stay, out_got)], quarter, 1)
    dealt, deal_up, deal_down = order.mark(
        *rows_dealt(lengths, dealing, me1, hidden, down_shares(), slots, span)
    )
    small_step()
    height //= 2
    downs = leave(downs, height, 0)
    attn_height = half
    for bit in line[1:]:
        attn_height //= 2
        attns = leave(attns, attn_height, bit)
    (g_gate,) = finish([gates])
    small_step()
    outs = leave(outs, heights[0], line[0])
    up_sum = order.mark(order.gate(up_sum))
    up_line = lax.psum_scatter(
        up_sum, "dp", scatter_dimension=0, tiled=True, axis_index_groups=line_groups
    )
    out_low = lax.ppermute(deal_up, "dp", up)
    out_high = lax.ppermute(deal_down, "dp", down)
    height //= 2
    downs = leave(downs, height, 1)
    attn_sum = order.mark(fold(gated([attns]), width // lines, BF)[0])
    plane_rows = lax.all_to_all(
        attn_sum.reshape(4, block, columns), "dp", 0, 0, axis_index_groups=groups
    )
    for low, bit in zip(heights[1:], line[1:]):
        outs = leave(outs, low, bit)
    g_up = order.mark(order.gate(up_line).astype(F32))
    (g_down,) = finish([downs])
    out_low, out_high = order.mark(*order.gate(out_low, out_high))
    while small_got is not None:
        small_step()
    (g_out,) = finish([outs])
    g_query, g_key, g_value, g_house = order.gate(plane_rows).astype(F32)

    taps = conv_taps.shape[0]
    per_row = lax.dynamic_slice_in_dim(small[taps:], me * block, block, axis=1)
    taps_total = small[:taps, :columns]
    held_from = lax.dynamic_slice_in_dim(dealing, me * slots, slots) // slots - me
    output = jnp.where(
        (held_from == -1)[:, None, None],
        out_low[None],
        jnp.where(
            (held_from == 1)[:, None, None], out_high[None], dealt.reshape(slots, span, width)
        ),
    )
    return (
        output,
        input_grad,
        per_row[1],
        g_query,
        g_key,
        g_value,
        g_house,
        per_row[2 : 2 + d_logit.shape[0]].T,
        taps_total,
        g_out.T,
        per_row[0],
        g_gate,
        g_up,
        g_down.T,
    )


def solution(mesh):
    in_specs = (
        P("dp", None),
        P("dp", None, None),
        P(),
        P(),
        P(),
        P(None, "tensor"),
        P(None, "tensor"),
        P(None, "tensor"),
        P(None, "tensor"),
        P(None, "tensor"),
        P(None, "tensor"),
        P("tensor", None),
        P(),
        P(None, "tensor"),
        P(None, "tensor"),
        P("tensor", None),
    )
    out_specs = (
        P("dp", None, None),
        P("dp", None),
        P("dp"),
        P("dp", "tensor"),
        P("dp", "tensor"),
        P("dp", "tensor"),
        P("dp", "tensor"),
        P("dp", "tensor"),
        P(None, "tensor"),
        P("tensor", "dp"),
        P("dp"),
        P("dp", "tensor"),
        P("dp", "tensor"),
        P("tensor", "dp"),
    )
    return jax.shard_map(
        on_device, mesh=mesh, in_specs=in_specs, out_specs=out_specs, check_vma=False
    )
```
